256 devices in a mesh: section: 2 (over core), expert: 64 (over y, z, x_lo), dp: 2 (over x_hi).
Axes of the slice: x: 4 (x_hi: 2, x_lo: 2; x = x_hi * 2 + x_lo), y: 4, z: 8, core: 2. Of those that a mesh axis runs over, the one named last changes fastest.
Arguments:
- activations: bfloat16 [2, 2048, 1024], P(None, ('expert', 'dp')), may hold values from -60 to 60
- cotangent: bfloat16 [2, 2048, 1024], P(None, ('expert', 'dp')), may hold values from -6 to 6
- norm_gain: float32 [2, 1024], P('section'), may hold values from 0.1 to 1.9
- w_gate: bfloat16 [2, 64, 1024, 768], P('section', 'expert', 'dp'), may hold values from -0.1875 to 0.1875
- w_up: bfloat16 [2, 64, 1024, 768], P('section', 'expert', 'dp'), may hold values from -0.1875 to 0.1875
- w_down: bfloat16 [2, 64, 768, 1024], P('section', 'expert', None, 'dp'), may hold values from -0.21875 to 0.21875
- routes: int32 [2, 2, 2048, 6], P('section', None, ('expert', 'dp')), may hold values from 0 to 63, all different within a row; in each aligned block of 16 rows (0 to 15, 16 to 31, ..., all dimensions but the last counted through in order) at most 2 rows name the same one
- gate_weights: float32 [2, 2, 2048, 6], P('section', None, ('expert', 'dp')), may hold values from 0.05 to 0.6
Outputs:
- hidden_out: bfloat16 [2, 2, 2048, 1024], P('section', None, ('expert', 'dp'))
- input_grads: bfloat16 [2, 2, 2048, 1024], P('section', None, ('expert', 'dp'))
- grad_gain: float32 [2, 1024], P('section')
- grad_gate: float32 [2, 64, 1024, 768], P('section', 'expert', 'dp')
- grad_up: float32 [2, 64, 1024, 768], P('section', 'expert', 'dp')
- grad_down: float32 [2, 64, 768, 1024], P('section', 'expert', None, 'dp')
The draws below stay inside these ranges and needn't reach their ends.
Inputs may be any that keep to these rules, and one draw needn't show every extreme that they name: `routes`: each token names 6 different experts. Among the rows of one device (16 tokens of one layer and micro-batch) no expert is named more than 2 times, and in some blocks one is named exactly 2 times.
All inputs are finite; a program needn't handle non-finite values.
Results may differ from the reference program's by a relative error of at most 0.012.
Values may be sent and summed in bfloat16 or wider, within the bound.
No kernel may reach another device: no remote copies, remote signals or barrier semaphores. Data moves between devices by JAX's collectives and lax.ppermute only.
A program may use at most 128 MiB of HBM per device.

```python
import math
import jax
import jax.numpy as jnp
import numpy as np
from jax import lax

D = 1024
HID = 768
TOP = 6
MICRO = 2
TOK_DEV = 16
EXPERTS = 64
CAP = 2
TOKENS = 2048
N_SECTION = 2


def draw_activations(key, part):
    key_rows, key_cols, key_sample = jax.random.split(key, 3)
    row_scale = jnp.exp(jax.random.uniform(key_rows, (MICRO, TOKENS, 1), jnp.float32, math.log(0.3), math.log(3.0)))
    col_scale = jnp.exp(jax.random.uniform(key_cols, (1, 1, D), jnp.float32, math.log(0.3), math.log(3.0)))
    sample = jax.random.normal(key_sample, (MICRO, TOKENS, D), jnp.float32)
    return jnp.clip(sample * row_scale * col_scale, -60.0, 60.0).astype(jnp.bfloat16)


def shard_levels(key, extent, cuts, low, largest):
    level = 1.0
    for position, blocks in cuts:
        steps = jax.random.uniform(jax.random.fold_in(jax.random.fold_in(key, 6), position), (blocks,), jnp.float32, low / len(cuts), largest / len(cuts))
        level = level * jnp.repeat(jnp.exp(steps), extent[position] // blocks).reshape((-1,) + (1,) * (len(extent) - 1 - position))
    return level


def routed_block(own_key, own, number, rows, number_of, top, limit, lean):
    ranking = jax.random.permutation(own_key, number_of)
    packed, common = portions_of(number_of, rows * top, limit, lean, True), portions_of(number_of, rows * top, limit, lean, False)
    places = jnp.arange(number_of)

    def named(sizes, turn):
        used = int((sizes > 0).sum())
        fixed = max(1, used // 4)
        shifted = fixed + (places - fixed + turn * (used - fixed)) % max(1, number_of - fixed)
        return jnp.zeros((number_of,), jnp.int32).at[ranking[jnp.where(places < fixed, places, shifted)]].set(jnp.asarray(sizes, jnp.int32))

    sizes = jnp.where(number % 4 == 0, named(packed, number // 4), named(common, number - number // 4 - 1))
    mixed = jax.random.permutation(jax.random.fold_in(own, 3), number_of)
    giver, taker = mixed[0:number_of // 2 * 2:2], mixed[1:number_of // 2 * 2:2]
    slack = jnp.minimum(sizes[giver] - 1, limit - sizes[taker]) // 2
    slack = jnp.where((giver == ranking[0]) | (taker == ranking[0]) | (sizes[taker] == 0), 0, jnp.maximum(slack, 0))
    shifted = jax.random.randint(jax.random.fold_in(own, 4), (number_of // 2,), 0, 1 << 20) % (slack + 1)
    sizes = sizes.at[giver].add(-shifted).at[taker].add(shifted)
    labels = jnp.searchsorted(jnp.cumsum(sizes), jnp.arange(rows * top), side="right").astype(jnp.int32)
    grid = labels.reshape(top, rows).T
    grid = grid[jax.random.permutation(jax.random.fold_in(own, 1), rows)]
    turn = jax.random.randint(jax.random.fold_in(own, 2), (rows, 1), 0, top)
    return jnp.take_along_axis(grid, (jnp.arange(top)[None, :] + turn) % top, axis=1)


def portions_of(number_of, total, reach, lean, full):
    weights = [(1 << 20) // math.isqrt(standing ** lean) + 1 for standing in range(1, number_of + 1)]
    largest = reach if full else min(reach, max(-(-total // number_of), total * weights[0] // sum(weights)))
    least = 1 if total - largest >= number_of - 1 else 0
    counts, surplus = [largest] + [least] * (number_of - 1), total - largest - least * (number_of - 1)
    while surplus > 0:
        candidates = [i for i in range(1, number_of) if counts[i] < largest] or [i for i in range(1, number_of) if counts[i] < reach]
        pool, remaining = sum([weights[i] for i in candidates]), surplus
        for i in candidates:
            addition = min(reach - counts[i], max(1, remaining * weights[i] // pool), surplus)
            counts[i] = counts[i] + addition
            surplus = surplus - addition
    return np.array(counts)


def gaussian(own_key, shape, width, reach, cuts=(), kind=jnp.bfloat16):
    drawn = width * jax.random.normal(own_key, shape, jnp.float32)
    if cuts:
        drawn = drawn * shard_levels(own_key, shape, cuts, -0.22, 0.18)
    return jnp.clip(drawn, -reach, reach).astype(kind)


def setup_inputs(seed: int = 0) -> dict:
    keys = jax.random.split(jax.random.key(seed), 9)
    activations = draw_activations(jax.random.fold_in(keys[8], 71), 0)
    cotangent = gaussian(keys[1], (MICRO, TOKENS, D), 0.5, 6.0, ((1, 128),))
    norm_gain = jnp.clip(1.0 + 0.18 * jax.random.normal(keys[2], (N_SECTION, D), jnp.float32), 0.1, 1.9)
    w_gate = gaussian(keys[3], (N_SECTION, EXPERTS, D, HID), D ** -0.5, 0.1875, ((0, 2), (1, 64), (2, 2)))
    w_up = gaussian(keys[4], (N_SECTION, EXPERTS, D, HID), D ** -0.5, 0.1875, ((0, 2), (1, 64), (2, 2)))
    w_down = gaussian(keys[5], (N_SECTION, EXPERTS, HID, D), HID ** -0.5, 0.21875, ((0, 2), (1, 64), (3, 2)))
    routes_keys = jax.random.split(jax.random.fold_in(keys[6], 1), N_SECTION * MICRO * TOKENS // TOK_DEV)
    routes_turns = jax.random.permutation(jax.random.fold_in(keys[6], 3), N_SECTION * MICRO * TOKENS // TOK_DEV)
    routes = jax.vmap(lambda own, number: routed_block(jax.random.fold_in(keys[6], 2), own, number, TOK_DEV, EXPERTS, TOP, CAP, 2))(routes_keys, routes_turns).reshape((N_SECTION, MICRO, TOKENS, TOP))
    gate_weights = jnp.clip(0.05 + 0.55 * jax.random.uniform(keys[7], (N_SECTION, MICRO, TOKENS, TOP), jnp.float32) ** shard_levels(keys[7], (N_SECTION, MICRO, TOKENS, TOP), ((0, 2), (2, 128)), -0.2, 0.2), 0.05, 0.6)
    return {"activations": activations, "cotangent": cotangent, "norm_gain": norm_gain, "w_gate": w_gate, "w_up": w_up, "w_down": w_down, "routes": routes, "gate_weights": gate_weights}


epsilon = 1e-06

def normalize(layer_in, gain):
    values = layer_in.astype(jnp.float32)
    scaling = lax.rsqrt(lax.optimization_barrier(jnp.mean(values * values, axis=-1, keepdims=True)) + epsilon)
    return (values, scaling, (values * scaling * gain).astype(jnp.bfloat16))

def slot_place(flat_ids):
    onehot = (flat_ids[:, None] == jnp.arange(EXPERTS, dtype=jnp.int32)[None, :]).astype(jnp.int32)
    before = jnp.cumsum(onehot, axis=0) - onehot
    return flat_ids * CAP + lax.optimization_barrier(jnp.sum(before * onehot, axis=1))

def slot_tables(route_ids, gate_rows):
    blocks = TOKENS // TOK_DEV
    flat_ids = route_ids.reshape(blocks, TOK_DEV * TOP).astype(jnp.int32)
    places = jax.vmap(slot_place)(flat_ids)
    within = jnp.arange(TOK_DEV * TOP, dtype=jnp.int32) // TOP
    token_ids = within[None, :] + (jnp.arange(blocks, dtype=jnp.int32) * TOK_DEV)[:, None]
    block_ids = jnp.broadcast_to(jnp.arange(blocks, dtype=jnp.int32)[:, None], places.shape)
    slot_token = jnp.full((blocks, EXPERTS * CAP), TOKENS, jnp.int32).at[block_ids, places].set(token_ids)
    slot_gate = jnp.zeros((blocks, EXPERTS * CAP), jnp.float32).at[block_ids, places].set(gate_rows.reshape(blocks, TOK_DEV * TOP))
    slot_token = slot_token.reshape(blocks, EXPERTS, CAP).transpose(1, 0, 2).reshape(EXPERTS, blocks * CAP)
    slot_gate = slot_gate.reshape(blocks, EXPERTS, CAP).transpose(1, 0, 2).reshape(EXPERTS, blocks * CAP)
    return (slot_token, slot_gate)

def expert_rows(normed_rows, w_first, w_second):
    pre_gate = jnp.dot(normed_rows, w_first, preferred_element_type=jnp.float32)
    pre_up = jnp.dot(normed_rows, w_second, preferred_element_type=jnp.float32)
    acts = (jax.nn.silu(pre_gate) * pre_up).astype(jnp.bfloat16)
    return (pre_gate, pre_up, acts)

def layer_forward(layer_in, gain, gate_all, up_all, down_all, route_ids, gate_rows):
    values, scaling, normed = normalize(layer_in, gain)
    slot_token, slot_gate = slot_tables(route_ids, gate_rows)
    padded = jnp.concatenate([normed, jnp.zeros((1, D), jnp.bfloat16)], axis=0)

    def per_expert(totals, members):
        slot_ids, slot_weight, w_first, w_second, w_third = members
        pre_gate, pre_up, acts = expert_rows(padded[slot_ids], w_first, w_second)
        result = jnp.dot(acts, w_third, preferred_element_type=jnp.float32).astype(jnp.bfloat16)
        return (totals.at[slot_ids].add(slot_weight[:, None] * result.astype(jnp.float32)), None)
    totals, unused = lax.scan(per_expert, jnp.zeros((TOKENS + 1, D), jnp.float32), (slot_token, slot_gate, gate_all, up_all, down_all))
    return (values + totals[:TOKENS]).astype(jnp.bfloat16)

def layer_backward(layer_in, gain, gate_all, up_all, down_all, route_ids, gate_rows, upstream):
    values, scaling, normed = normalize(layer_in, gain)
    slot_token, slot_gate = slot_tables(route_ids, gate_rows)
    padded = jnp.concatenate([normed, jnp.zeros((1, D), jnp.bfloat16)], axis=0)
    padded_grad = jnp.concatenate([upstream, jnp.zeros((1, D), jnp.bfloat16)], axis=0)

    def per_expert(totals, members):
        slot_ids, slot_weight, w_first, w_second, w_third = members
        normed_rows = padded[slot_ids]
        pre_gate, pre_up, acts = expert_rows(normed_rows, w_first, w_second)
        out_grad = (slot_weight[:, None] * padded_grad[slot_ids].astype(jnp.float32)).astype(jnp.bfloat16)
        act_grad = jnp.dot(out_grad, w_third.T, preferred_element_type=jnp.float32)
        sigma = jax.nn.sigmoid(pre_gate)
        gate_grad = (act_grad * pre_up * sigma * (1.0 + pre_gate * (1.0 - sigma))).astype(jnp.bfloat16)
        up_grad = (act_grad * pre_gate * sigma).astype(jnp.bfloat16)
        pick_grad = (jnp.dot(gate_grad, w_first.T, preferred_element_type=jnp.float32) + jnp.dot(up_grad, w_second.T, preferred_element_type=jnp.float32)).astype(jnp.bfloat16)
        totals = totals.at[slot_ids].add(pick_grad.astype(jnp.float32))
        terms = (jnp.dot(normed_rows.T, gate_grad, preferred_element_type=jnp.float32), jnp.dot(normed_rows.T, up_grad, preferred_element_type=jnp.float32), jnp.dot(acts.T, out_grad, preferred_element_type=jnp.float32))
        return (totals, terms)
    totals, terms = lax.scan(per_expert, jnp.zeros((TOKENS + 1, D), jnp.float32), (slot_token, slot_gate, gate_all, up_all, down_all))
    normed_grad = totals[:TOKENS]
    gain_term = lax.optimization_barrier(jnp.sum(normed_grad * values * scaling, axis=0))
    weighted = normed_grad * gain
    layer_grad = upstream.astype(jnp.float32) + scaling * (weighted - values * scaling * scaling * lax.optimization_barrier(jnp.mean(weighted * values, axis=-1, keepdims=True)))
    return (layer_grad.astype(jnp.bfloat16), gain_term, terms)

def reference(activations, cotangent, norm_gain, w_gate, w_up, w_down, routes, gate_weights):
    layer_inputs = []
    layer_outputs = []
    for section in range(N_SECTION):
        inputs_now = []
        outputs_now = []
        for micro in range(MICRO):
            layer_in = activations[micro] if section == 0 else layer_outputs[section - 1][micro]
            inputs_now.append(layer_in)
            outputs_now.append(layer_forward(layer_in, norm_gain[section], w_gate[section], w_up[section], w_down[section], routes[section, micro], gate_weights[section, micro]))
        layer_inputs.append(inputs_now)
        layer_outputs.append(outputs_now)
    input_grads = [None] * N_SECTION
    gain_grads = [None] * N_SECTION
    gate_grads = [None] * N_SECTION
    up_grads = [None] * N_SECTION
    down_grads = [None] * N_SECTION
    upstream_all = [cotangent[micro] for micro in range(MICRO)]
    for section in reversed(range(N_SECTION)):
        grads_now = []
        gain_sum = jnp.zeros((D,), jnp.float32)
        sums = None
        for micro in range(MICRO):
            layer_grad, gain_term, terms = layer_backward(layer_inputs[section][micro], norm_gain[section], w_gate[section], w_up[section], w_down[section], routes[section, micro], gate_weights[section, micro], upstream_all[micro])
            grads_now.append(layer_grad)
            gain_sum = gain_sum + gain_term
            sums = terms if sums is None else jax.tree.map(jnp.add, sums, terms)
        input_grads[section] = jnp.stack(grads_now)
        gain_grads[section] = gain_sum
        gate_grads[section], up_grads[section], down_grads[section] = sums
        upstream_all = grads_now
    hidden_out = jnp.stack([jnp.stack(outputs_now) for outputs_now in layer_outputs])
    return (hidden_out, jnp.stack(input_grads), jnp.stack(gain_grads), jnp.stack(gate_grads), jnp.stack(up_grads), jnp.stack(down_grads))
```

```python
import functools
import jax
import jax.numpy as jnp
from jax import lax
from jax.experimental import pallas as pl
from jax.experimental.pallas import tpu as pltpu
from jax.sharding import PartitionSpec as P

epsilon = 1e-06
f32 = jnp.float32
bf16 = jnp.bfloat16
every = ("section", "expert", "dp")
vmem = pl.BlockSpec(memory_space=pltpu.VMEM)
smem = pl.BlockSpec(memory_space=pltpu.SMEM)
anywhere = pl.BlockSpec(memory_space=pl.ANY)


def dot(left, right):
    return jnp.dot(left, right, preferred_element_type=f32)


def dot_nt(left, right):
    return lax.dot_general(left, right, (((1,), (1,)), ((), ())), preferred_element_type=f32)


def dot_tn(left, right):
    return lax.dot_general(left, right, (((0,), (0,)), ((), ())), preferred_element_type=f32)


def call(body, name, in_specs, outs, scratch=(), flops=0, moved=0):
    return pl.pallas_call(
        body,
        name=name,
        in_specs=in_specs,
        out_shape=[jax.ShapeDtypeStruct(shape, dtype) for shape, dtype in outs],
        out_specs=[vmem] * len(outs),
        scratch_shapes=list(scratch),
        cost_estimate=pl.CostEstimate(flops=flops, bytes_accessed=moved, transcendentals=0),
    )


def tables_body(key_ref, key_t_ref, gate_ref, gate_t_ref, pick, high, low, pick_t, high_t, low_t):
    layers, picks, width = key_ref.shape
    rows = pick.shape[1]
    for layer in range(layers):
        for start in range(0, rows, 128):
            index = lax.broadcasted_iota(jnp.int32, (128, width), 0) + start
            chosen = jnp.zeros((128, width), f32)
            weight = jnp.zeros((128, width), f32)
            for k in range(picks):
                match = index == key_ref[layer, k : k + 1, :]
                chosen = jnp.where(match, 1.0, chosen)
                weight = jnp.where(match, gate_ref[layer, k : k + 1, :], weight)
            upper = weight.astype(bf16)
            pick[layer, start : start + 128, :] = chosen.astype(bf16)
            high[layer, start : start + 128, :] = upper
            low[layer, start : start + 128, :] = (weight - upper.astype(f32)).astype(bf16)
            index = lax.broadcasted_iota(jnp.int32, (width, 128), 1) + start
            chosen = jnp.zeros((width, 128), f32)
            weight = jnp.zeros((width, 128), f32)
            for k in range(picks):
                match = index == key_t_ref[layer, :, k : k + 1]
                chosen = jnp.where(match, 1.0, chosen)
                weight = jnp.where(match, gate_t_ref[layer, :, k : k + 1], weight)
            upper = weight.astype(bf16)
            pick_t[layer, :, start : start + 128] = chosen.astype(bf16)
            high_t[layer, :, start : start + 128] = upper
            low_t[layer, :, start : start + 128] = (weight - upper.astype(f32)).astype(bf16)


def tables(keys, gates):
    layers, width, picks = keys.shape
    rows = 8 * width
    down = ((layers, rows, width), bf16)
    across = ((layers, width, rows), bf16)
    return call(
        tables_body, "tables", [vmem] * 4, [down] * 3 + [across] * 3, flops=10**6, moved=3 * 10**6
    )(keys.transpose(0, 2, 1), keys, gates.transpose(0, 2, 1), gates)


def token_stats(block):
    values = block.astype(f32).reshape(-1, 8, 128)
    mean = jnp.sum(jnp.sum(values * values, axis=2, keepdims=True), axis=1, keepdims=True) / 1024.0
    return (values, lax.rsqrt(mean + epsilon))


def normalized(block, gain):
    values, scaling = token_stats(block)
    return (values * scaling * gain[None]).astype(bf16).reshape(block.shape)


def chunked(rows):
    return rows.astype(bf16).reshape(64, -1, 128)


def send_first_body(x_ref, grad_ref, gain_ref, pick, high, low, out):
    out[:, :16, :] = chunked(dot(pick[...], normalized(x_ref[...], gain_ref[...])))
    grad = grad_ref[...]
    out[:, 16:, :] = chunked(dot(high[...], grad) + dot(low[...], grad))


def to_matrix(rows, wide, target):
    wide[...] = rows
    slots = rows.shape[0] // 8
    for j in range(8):
        target[:, 128 * j : 128 * (j + 1)] = wide[pl.ds(j, slots, stride=8), :].astype(bf16)


def to_rows(matrix, wide):
    slots = matrix.shape[0]
    for j in range(8):
        wide[pl.ds(j, slots, stride=8), :] = matrix[:, 128 * j : 128 * (j + 1)]
    return wide[...].astype(bf16)


def fetch(place_ref, layer, sources, targets, sems):
    own, swapped, other, passed = sources
    here = place_ref[0] == layer
    mine = pl.multiple_of(place_ref[1] * 512, 512)
    rest = pl.multiple_of((1 - place_ref[1]) * 512, 512)

    def copies(first, second):
        found = []
        for n in range(3):
            for h, (source, start) in enumerate(((first[n], mine), (second[n], rest))):
                if n < 2:
                    target = targets[n].at[pl.ds(start, 512), :]
                else:
                    target = targets[n].at[:, pl.ds(start, 512)]
                found.append(pltpu.make_async_copy(source, target, sems.at[n, h]))
        return found

    @pl.when(here)
    def _():
        for copy in copies(own, other):
            copy.start()

    @pl.when(jnp.logical_not(here))
    def _():
        for copy in copies(swapped, passed):
            copy.start()

    waits = copies(own, other)
    return [waits[0:2], waits[2:4], waits[4:6]]


def finish(pair):
    for copy in pair:
        copy.wait()


def gated(pre_gate, pre_up):
    return pre_gate / (1.0 + jnp.exp(-pre_gate)) * pre_up


def halves(place_ref, source, target):
    mine = pl.multiple_of(place_ref[1] * 512, 512)
    rest = pl.multiple_of((1 - place_ref[1]) * 512, 512)
    target[0][:, target[2] : target[2] + 512] = source[:, pl.ds(mine, 512)]
    target[1][:, target[2] : target[2] + 512] = source[:, pl.ds(rest, 512)]


def first_forward_body(*refs):
    place_ref, arrived = refs[0:2]
    sources = (refs[2:5], refs[5:8], refs[8:11], refs[11:14])
    result, early, early_far, gate_out, up_out = refs[14:19]
    w_gate, w_up, w_down, wide, rows, sems = refs[19:]
    waits = fetch(place_ref, 0, sources, (w_gate, w_up, w_down), sems)
    to_matrix(arrived[:, :16, :].reshape(1024, 128).astype(f32), wide, rows)
    halves(place_ref, rows, (early, early_far, 0))
    finish(waits[0])
    pre_gate = dot(rows[...], w_gate[...])
    gate_out[...] = pre_gate
    finish(waits[1])
    pre_up = dot(rows[...], w_up[...])
    up_out[...] = pre_up
    acts = gated(pre_gate, pre_up).astype(bf16)
    early[:, 512:] = acts
    early_far[:, 512:] = acts
    finish(waits[2])
    result[...] = to_rows(dot(acts, w_down[...]), wide).reshape(64, 16, 128)


def expert_grads(act_grad, pre_gate, pre_up):
    sigma = 1.0 / (1.0 + jnp.exp(-pre_gate))
    gate_grad = (act_grad * pre_up * sigma * (1.0 + pre_gate * (1.0 - sigma))).astype(bf16)
    up_grad = (act_grad * pre_gate * sigma).astype(bf16)
    return (gate_grad, up_grad)


def gain_part(pick_rows, normed_rows):
    product = pick_rows.astype(f32) * normed_rows.astype(f32)
    return jnp.sum(product.reshape(-1, 8, 128), axis=0)


def second_body(*refs):
    place_ref, arrived, cot = refs[0:3]
    sources = (refs[3:6], refs[6:9], refs[9:12], refs[12:15])
    picked, result, early, early_far, late, late_far, gain_out = refs[15:22]
    w_gate, w_up, w_down, wide, rows, grads, sems = refs[22:]
    waits = fetch(place_ref, 1, sources, (w_gate, w_up, w_down), sems)
    normed_rows = arrived[...].reshape(1024, 128)
    to_matrix(normed_rows.astype(f32), wide, rows)
    halves(place_ref, rows, (early, early_far, 0))
    to_matrix(cot[:, 16:, :].reshape(1024, 128).astype(f32), wide, grads)
    halves(place_ref, grads, (late, late_far, 0))
    finish(waits[0])
    pre_gate = dot(rows[...], w_gate[...])
    finish(waits[1])
    pre_up = dot(rows[...], w_up[...])
    acts = gated(pre_gate, pre_up).astype(bf16)
    early[:, 512:] = acts
    early_far[:, 512:] = acts
    finish(waits[2])
    act_grad = dot_nt(grads[...], w_down[...])
    gate_grad, up_grad = expert_grads(act_grad, pre_gate, pre_up)
    for target in (late, late_far):
        target[:, 512:1280] = gate_grad
        target[:, 1280:] = up_grad
    pick_rows = to_rows(dot_nt(gate_grad, w_gate[...]) + dot_nt(up_grad, w_up[...]), wide)
    picked[...] = pick_rows.reshape(64, 16, 128)
    gain_out[...] = gain_part(pick_rows, normed_rows)
    result[...] = to_rows(dot(acts, w_down[...]), wide).reshape(64, 16, 128)


def first_backward_body(*refs):
    place_ref, arrived, normed, pre_gate, pre_up, gain_second = refs[0:6]
    sources = (refs[6:9], refs[9:12], refs[12:15], refs[15:18])
    picked, late, late_far = refs[18:21]
    w_gate, w_up, w_down, wide, grads, sems = refs[21:]
    waits = fetch(place_ref, 0, sources, (w_gate, w_up, w_down), sems)
    to_matrix(arrived[:, :16, :].reshape(1024, 128).astype(f32), wide, grads)
    halves(place_ref, grads, (late, late_far, 0))
    finish(waits[2])
    act_grad = dot_nt(grads[...], w_down[...])
    gate_grad, up_grad = expert_grads(act_grad, pre_gate[...], pre_up[...])
    for target in (late, late_far):
        target[:, 512:1280] = gate_grad
        target[:, 1280:] = up_grad
    finish(waits[0])
    finish(waits[1])
    pick_rows = to_rows(dot_nt(gate_grad, w_gate[...]) + dot_nt(up_grad, w_up[...]), wide)
    picked[:, :16, :] = pick_rows.reshape(64, 16, 128)
    gain_first = gain_part(pick_rows, normed[:, :16, :].reshape(1024, 128))
    both = jnp.concatenate([gain_first, gain_second[...]], axis=0).astype(bf16)
    picked[:, 16:, :] = jnp.broadcast_to(both[None], (64, 16, 128))


def combined(high_t, low_t, rows):
    return dot(high_t[...], rows) + dot(low_t[...], rows)


def between_body(returned, x_ref, gain_ref, high_t, low_t, pick, hidden, out):
    rows = returned[...].reshape(1024, 128)
    result = (x_ref[...].astype(f32) + combined(high_t, low_t, rows)).astype(bf16)
    hidden[...] = result
    out[...] = chunked(dot(pick[...], normalized(result, gain_ref[...])))


def input_gradient(rows, upstream, x_block, gain, pick_t):
    normed_grad = dot(pick_t, rows).reshape(-1, 8, 128)
    values, scaling = token_stats(x_block)
    weighted = normed_grad * gain[None]
    mean = (
        jnp.sum(jnp.sum(weighted * values, axis=2, keepdims=True), axis=1, keepdims=True) / 1024.0
    )
    change = scaling * (weighted - values * scaling * scaling * mean)
    return (upstream.astype(f32) + change.reshape(upstream.shape)).astype(bf16)


def turn_body(returned, result, x_ref, grad_ref, gain_ref, pick_t, high, low, grad_out, out):
    rows = returned[...].reshape(1024, 128)
    grad = input_gradient(rows, grad_ref[...], x_ref[...], gain_ref[...], pick_t[...])
    grad_out[...] = grad
    out[:, :16, :] = chunked(dot(high[...], grad) + dot(low[...], grad))
    out[:, 16:, :] = result[...]


def second_output_body(arrived, x_ref, high_t, low_t, hidden):
    rows = arrived[:, 16:, :].reshape(1024, 128)
    hidden[...] = (x_ref[...].astype(f32) + combined(high_t, low_t, rows)).astype(bf16)


def last_body(returned, x_ref, grad_ref, gain_ref, pick_t, grad_out, gain_out):
    rows = returned[:, :16, :].reshape(1024, 128)
    grad_out[...] = input_gradient(
        rows, grad_ref[...], x_ref[...], gain_ref[...], pick_t[...]
    )
    gain_out[...] = jnp.sum(returned[:, 16:, :].astype(f32), axis=0)


def weight_body(*refs):
    place_ref = refs[0]
    first, second = refs[1:9], refs[9:17]
    gate_out, up_out, down_out, early, late, sems = refs[17:]

    def copies(group):
        found = []
        for n in range(4):
            found.append(
                pltpu.make_async_copy(group[n], early.at[pl.ds(128 * n, 128), :], sems.at[0, n])
            )
            found.append(
                pltpu.make_async_copy(group[4 + n], late.at[pl.ds(128 * n, 128), :], sems.at[1, n])
            )
        return found

    @pl.when(place_ref[0] == 0)
    def _():
        for copy in copies(first):
            copy.start()

    @pl.when(place_ref[0] != 0)
    def _():
        for copy in copies(second):
            copy.start()

    for copy in copies(first):
        copy.wait()
    normed = early[:, :512]
    gate_out[...] = dot_tn(normed, late[:, 512:1280])
    up_out[...] = dot_tn(normed, late[:, 1280:])
    down_out[...] = dot_tn(early[:, 512:], late[:, :512])


def slot_keys(routes, gates):
    tokens, picks = routes.shape
    flat = routes.reshape(-1)
    count = tokens * picks
    earlier = jnp.arange(count)[:, None] > jnp.arange(count)[None, :]
    same = (flat[:, None] == flat[None, :]) & earlier
    places = (flat * 2 + jnp.sum(same.astype(jnp.int32), axis=1)).reshape(tokens, 1, picks)
    keys = places * 8 + jnp.arange(8, dtype=jnp.int32)[None, :, None]
    spread = jnp.broadcast_to(gates[:, None, :], (tokens, 8, picks))
    return (keys.reshape(-1, picks), spread.reshape(-1, picks))


def after(block, other):
    return lax.optimization_barrier((block, other))[0]


def per_device(activations, cotangent, norm_gain, w_gate, w_up, w_down, routes, gate_weights):
    section = lax.axis_index("section")
    part = lax.axis_index("dp")
    experts = lax.axis_size("expert")
    upper = section == 1
    place = jnp.stack([section, part]).astype(jnp.int32)
    micro_count, tokens, width = activations.shape
    swap = [(0, 1), (1, 0)]

    def across(layer, cross):
        source = 1 - layer if cross else layer
        return [
            (source * experts * 2 + e * 2 + d, layer * experts * 2 + e * 2 + 1 - d)
            for e in range(experts)
            for d in range(2)
        ]

    def exchange(block):
        return lax.all_to_all(block, "expert", split_axis=0, concat_axis=0, tiled=True)

    own = (w_gate[0, 0], w_up[0, 0], w_down[0, 0])

    own_gain = norm_gain.reshape(8, 128)
    sent = jnp.where(upper, 0, 1)
    sent_routes = lax.dynamic_index_in_dim(routes[0], sent, 0, keepdims=False).astype(f32)
    sent_gates = lax.dynamic_index_in_dim(gate_weights[0], sent, 0, keepdims=False)
    packed = jnp.concatenate(
        [jnp.pad(jnp.concatenate([sent_routes, sent_gates], axis=1), ((0, 0), (0, 116))), own_gain]
    )
    got = lax.ppermute(packed, "section", swap)
    got_routes = got[:tokens, 0:6].astype(jnp.int32)
    got_gates = got[:tokens, 6:12]
    got_gain = got[tokens:]
    kept_routes = lax.dynamic_index_in_dim(routes[0], section, 0, keepdims=False)
    kept_gates = lax.dynamic_index_in_dim(gate_weights[0], section, 0, keepdims=False)
    first_keys = slot_keys(
        jnp.where(upper, got_routes, kept_routes), jnp.where(upper, got_gates, kept_gates)
    )
    second_keys = slot_keys(
        jnp.where(upper, kept_routes, got_routes), jnp.where(upper, kept_gates, got_gates)
    )
    first_gain = jnp.where(upper, got_gain, own_gain)
    second_gain = jnp.where(upper, own_gain, got_gain)
    pick, high, low, pick_t, high_t, low_t = tables(
        jnp.stack([first_keys[0], second_keys[0]]), jnp.stack([first_keys[1], second_keys[1]])
    )

    other = [lax.ppermute(w, every, across(0, False)) for w in own]
    swapped = [lax.ppermute(w, "section", swap) for w in own]
    passed = [lax.ppermute(w, "section", [(0, 1)]) for w in other]

    x_first = lax.dynamic_index_in_dim(activations, section, 0, keepdims=False).reshape(-1, 128)
    grad_last = lax.dynamic_index_in_dim(cotangent, section, 0, keepdims=False).reshape(-1, 128)

    big = ((64, 32, 128), bf16)
    small = ((64, 16, 128), bf16)
    block = ((128, 128), bf16)
    early_shape = ((128, 1280), bf16)
    late_shape = ((128, 2048), bf16)
    weight_scratch = [
        pltpu.VMEM((1024, 768), bf16),
        pltpu.VMEM((1024, 768), bf16),
        pltpu.VMEM((768, 1024), bf16),
    ]
    wide = pltpu.VMEM((1024, 128), f32)
    matrix = pltpu.VMEM((128, 1024), bf16)
    sems = pltpu.SemaphoreType.DMA((3, 2))

    out_first = call(
        send_first_body, "send_first", [vmem] * 6, [big], flops=10**8, moved=2 * 10**6
    )(x_first, grad_last, first_gain, pick[0], high[1], low[1])[0]
    arrived_first = exchange(out_first)

    result, early0, early0_far, pre_gate, pre_up = call(
        first_forward_body,
        "first_forward",
        [smem, vmem] + [anywhere] * 12,
        [small, early_shape, early_shape, ((128, 768), f32), ((128, 768), f32)],
        weight_scratch + [wide, matrix, sems],
        flops=6 * 10**8,
        moved=6 * 10**6,
    )(place, arrived_first, *own, *swapped, *other, *passed)
    returned = exchange(result)

    late_own = [after(w, o) for w, o in zip(own, other)]
    other1 = [lax.ppermute(w, every, across(1, False)) for w in late_own]
    passed1 = [lax.ppermute(w, "section", [(1, 0)]) for w in other1]

    hidden_first, out_second = call(
        between_body, "between", [vmem] * 6, [block, small], flops=10**8, moved=2 * 10**6
    )(returned, x_first, second_gain, high_t[0], low_t[0], pick[1])
    arrived_second = exchange(out_second)

    picked, result_second, early1, early1_far, late1, late1_far, gain_second = call(
        second_body,
        "second",
        [smem, vmem, vmem] + [anywhere] * 12,
        [small, small, early_shape, early_shape, late_shape, late_shape, ((8, 128), f32)],
        weight_scratch + [wide, matrix, matrix, sems],
        flops=12 * 10**8,
        moved=8 * 10**6,
    )(place, arrived_second, arrived_first, *own, *swapped, *other1, *passed1)
    returned = exchange(picked)

    grad_middle, out_third = call(
        turn_body, "turn", [vmem] * 8, [block, big], flops=10**8, moved=2 * 10**6
    )(
        returned,
        result_second,
        hidden_first,
        grad_last,
        second_gain,
        pick_t[1],
        high[0],
        low[0],
    )
    arrived_third = exchange(out_third)

    picked, late0, late0_far = call(
        first_backward_body,
        "first_backward",
        [smem] + [vmem] * 5 + [anywhere] * 12,
        [big, late_shape, late_shape],
        weight_scratch + [wide, matrix, sems],
        flops=6 * 10**8,
        moved=8 * 10**6,
    )(
        place,
        arrived_third,
        arrived_first,
        pre_gate,
        pre_up,
        gain_second,
        *own,
        *swapped,
        *other,
        *passed,
    )
    returned = exchange(picked)

    def gathered(layer, near, far):
        return (
            near,
            lax.ppermute(near, "section", [(1 - layer, layer)]),
            lax.ppermute(far, every, across(layer, False)),
            lax.ppermute(far, every, across(layer, True)),
        )

    weight_grads = call(
        weight_body,
        "weight_grads",
        [smem] + [anywhere] * 16,
        [((512, 768), f32), ((512, 768), f32), ((768, 512), f32)],
        [
            pltpu.VMEM((512, 1280), bf16),
            pltpu.VMEM((512, 2048), bf16),
            pltpu.SemaphoreType.DMA((2, 4)),
        ],
        flops=12 * 10**8,
        moved=8 * 10**6,
    )(
        place,
        *gathered(0, early0, early0_far),
        *gathered(0, late0, late0_far),
        *gathered(1, early1, early1_far),
        *gathered(1, late1, late1_far),
    )

    hidden_second = call(
        second_output_body, "second_output", [vmem] * 4, [block], flops=10**8, moved=10**6
    )(arrived_third, hidden_first, high_t[1], low_t[1])[0]
    grad_first, gain_rows = call(
        last_body, "last", [vmem] * 5, [block, ((16, 128), f32)], flops=10**8, moved=10**6
    )(returned, x_first, grad_middle, first_gain, pick_t[0])

    def owned(first, second):
        mine = jnp.where(upper, second, first)
        theirs = lax.ppermute(jnp.where(upper, first, second), "section", swap)
        both = jnp.where(upper, jnp.stack([theirs, mine]), jnp.stack([mine, theirs]))
        return both.reshape(1, micro_count, tokens, width)

    beside = [(e * 2 + d, e * 2 + 1 - d) for e in range(experts) for d in range(2)]
    gain_rows = gain_rows + lax.ppermute(gain_rows, "section", swap)
    gain_rows = gain_rows + lax.ppermute(gain_rows, ("expert", "dp"), beside)
    gain_grad = jnp.where(upper, gain_rows[8:], gain_rows[:8]) / own_gain
    return (
        owned(hidden_first, hidden_second),
        owned(grad_first, grad_middle),
        gain_grad.reshape(1, width),
        weight_grads[0][None, None],
        weight_grads[1][None, None],
        weight_grads[2][None, None],
    )


def solution(mesh):
    placed = (
        P(None, ("expert", "dp"), None),
        P(None, ("expert", "dp"), None),
        P("section", None),
        P("section", "expert", "dp", None),
        P("section", "expert", "dp", None),
        P("section", "expert", None, "dp"),
        P("section", None, ("expert", "dp"), None),
        P("section", None, ("expert", "dp"), None),
    )
    return jax.shard_map(
        per_device,
        mesh=mesh,
        in_specs=placed,
        out_specs=(
            P("section", None, ("expert", "dp"), None),
            P("section", None, ("expert", "dp"), None),
            P("section", None),
            P("section", "expert", "dp", None),
            P("section", "expert", "dp", None),
            P("section", "expert", None, "dp"),
        ),
        check_vma=False,
    )
```

```python
import jax
import jax.numpy as jnp
from jax import lax
from jax.experimental import pallas as pl
from jax.experimental.pallas import tpu as pltpu
from jax.sharding import PartitionSpec as P

epsilon = 1e-06
f32 = jnp.float32
bf16 = jnp.bfloat16
every = ("section", "expert", "dp")
vmem = pl.BlockSpec(memory_space=pltpu.VMEM)
smem = pl.BlockSpec(memory_space=pltpu.SMEM)
anywhere = pl.BlockSpec(memory_space=pl.ANY)


def dot(left, right):
    return jnp.dot(left, right, preferred_element_type=f32)


def dot_nt(left, right):
    return lax.dot_general(left, right, (((1,), (1,)), ((), ())), preferred_element_type=f32)


def dot_tn(left, right):
    return lax.dot_general(left, right, (((0,), (0,)), ((), ())), preferred_element_type=f32)


def call(body, in_specs, outs, scratch=(), flops=0, moved=0, grant=16, out_spec=vmem):
    return pl.pallas_call(
        body,
        in_specs=in_specs,
        out_shape=[jax.ShapeDtypeStruct(shape, dtype) for shape, dtype in outs],
        out_specs=[out_spec] * len(outs),
        scratch_shapes=list(scratch),
        cost_estimate=pl.CostEstimate(flops=flops, bytes_accessed=moved, transcendentals=0),
        compiler_params=pltpu.CompilerParams(vmem_limit_bytes=grant * 2**20),
    )


def token_rows(block, wide):
    values = block.astype(f32)
    for j in range(8):
        wide[pl.ds(j, 16, stride=8), :] = values[:, 128 * j : 128 * (j + 1)]
    return wide[...].astype(bf16)


def token_matrix(rows, wide):
    wide[...] = rows.astype(f32)
    return [wide[pl.ds(j, 16, stride=8), :].astype(bf16) for j in range(8)]


def token_stats(block):
    values = block.astype(f32).reshape(-1, 8, 128)
    mean = jnp.sum(jnp.sum(values * values, axis=2, keepdims=True), axis=1, keepdims=True) / 1024.0
    return (values, lax.rsqrt(mean + epsilon))


def normalized(block, gain):
    values, scaling = token_stats(block)
    return (values * scaling * gain[None]).astype(bf16).reshape(block.shape)


def chunked(rows):
    return rows.astype(bf16).reshape(64, -1, 128)


def fill_tables(ids, gates, pick, high, low):
    token = lax.broadcasted_iota(jnp.int32, (16, 128), 0)
    lane = lax.broadcasted_iota(jnp.int32, (16, 128), 1)
    spread = jnp.where(lax.shift_right_logical(lane, 3) == token, 1.0, 0.0).astype(bf16)
    names = dot(ids.astype(f32).astype(bf16), spread)
    gates_high = gates.astype(bf16)
    gates_low = (gates - gates_high.astype(f32)).astype(bf16)
    upper = dot(gates_high, spread)
    lower = dot(gates_low, spread)
    expert = lax.broadcasted_iota(jnp.int32, (64, 128), 0).astype(f32)
    named = jnp.zeros((64, 128), f32)
    first = jnp.zeros((64, 128), f32)
    second = jnp.zeros((64, 128), f32)
    for k in range(ids.shape[0]):
        match = expert == names[k : k + 1, :]
        named = jnp.where(match, 1.0, named)
        first = jnp.where(match, upper[k : k + 1, :], first)
        second = jnp.where(match, lower[k : k + 1, :], second)
    row = lax.broadcasted_iota(jnp.int32, (128, 128), 0)
    column = lax.broadcasted_iota(jnp.int32, (128, 128), 1)
    earlier = ((row & 7) == 0) & (
        lax.shift_right_logical(row, 3) < lax.shift_right_logical(column, 3)
    )
    before = dot(named.astype(bf16), jnp.where(earlier, 1.0, 0.0).astype(bf16))
    code = jnp.where(named > 0.0, before + 1.0, 0.0)
    slot_row = lax.broadcasted_iota(jnp.int32, (1, 16, 128), 1)
    slot_lane = lax.broadcasted_iota(jnp.int32, (1, 16, 128), 2)
    wanted = lax.shift_right_logical(slot_row, 3).astype(f32) + 1.0
    wanted = jnp.where((slot_row & 7) == (slot_lane & 7), wanted, 9.0)
    shape = (64, 16, 128)
    match = jnp.broadcast_to(code[:, None, :], shape) == jnp.broadcast_to(wanted, shape)
    zero = jnp.zeros(shape, f32)
    pick[...] = jnp.where(match, 1.0, zero).astype(bf16).reshape(1024, 128)
    first = jnp.broadcast_to(first[:, None, :], shape)
    high[...] = jnp.where(match, first, zero).astype(bf16).reshape(1024, 128)
    second = jnp.broadcast_to(second[:, None, :], shape)
    low[...] = jnp.where(match, second, zero).astype(bf16).reshape(1024, 128)


def start_body(*refs):
    place_ref, own_routes, got_routes, own_gates, got_gates = refs[0:5]
    x_ref, grad_ref, own_gain, got_gain = refs[5:9]
    out, x_rows, grad_rows = refs[9:12]
    pick0, high0, low0, pick1, high1, low1 = refs[12:18]
    wide = refs[18]
    section = place_ref[0]
    ids = (own_routes[:, section, :], got_routes[:, section, :])
    gates = (own_gates[:, section, :], got_gates[:, section, :])
    lower = section == 0
    fill_tables(
        jnp.where(lower, ids[0], ids[1]),
        jnp.where(lower, gates[0], gates[1]),
        pick0,
        high0,
        low0,
    )
    fill_tables(
        jnp.where(lower, ids[1], ids[0]),
        jnp.where(lower, gates[1], gates[0]),
        pick1,
        high1,
        low1,
    )
    x_block = token_rows(x_ref[section], wide)
    x_rows[...] = x_block
    gain = jnp.where(lower, own_gain[...], got_gain[...])
    out[:, :16, :] = chunked(dot(pick0[...], normalized(x_block, gain)))
    grad = token_rows(grad_ref[section], wide)
    grad_rows[...] = grad
    out[:, 16:, :] = chunked(dot(high1[...], grad) + dot(low1[...], grad))


def flip_body(*refs):
    for source, target in zip(refs[:6], refs[6:]):
        target[...] = source[...].astype(f32).T.astype(bf16)


def pack_body(*refs):
    place_ref = refs[0]
    own, swapped = refs[1:4], refs[4:7]
    outs = refs[7:11]
    sems = refs[11]
    section = place_ref[0]
    start = pl.multiple_of(section * 256, 256)
    start_down = pl.multiple_of(section * 384, 128)

    def copies(sources):
        found = []
        for layer, (gate, up, down) in enumerate(sources):
            both, last = outs[2 * layer], outs[2 * layer + 1]
            found.append(
                pltpu.make_async_copy(
                    gate.at[pl.ds(start, 256), :], both.at[0:256, :], sems.at[layer, 0]
                )
            )
            found.append(
                pltpu.make_async_copy(
                    up.at[pl.ds(start, 256), :], both.at[256:512, :], sems.at[layer, 1]
                )
            )
            found.append(
                pltpu.make_async_copy(
                    down.at[pl.ds(start_down, 384), :], last, sems.at[layer, 2]
                )
            )
        return found

    @pl.when(section == 0)
    def _():
        for copy in copies((own, swapped)):
            copy.start()

    @pl.when(section != 0)
    def _():
        for copy in copies((swapped, own)):
            copy.start()

    for copy in copies((own, swapped)):
        copy.wait()


def to_matrix(rows, wide, target):
    wide[...] = rows
    slots = rows.shape[0] // 8
    for j in range(8):
        target[:, 128 * j : 128 * (j + 1)] = wide[pl.ds(j, slots, stride=8), :].astype(bf16)


def to_rows(matrix, wide):
    slots = matrix.shape[0]
    for j in range(8):
        wide[pl.ds(j, slots, stride=8), :] = matrix[:, 128 * j : 128 * (j + 1)]
    return wide[...].astype(bf16)


def fetch(place_ref, layer, sources, targets, sems):
    own, swapped = sources[0:3], sources[3:6]
    portions = (sources[6:8], sources[8:10])
    section, part = place_ref[0], place_ref[1]
    mine = pl.multiple_of(part * 512, 512)
    rest = pl.multiple_of((1 - part) * 512, 512)

    def near(group):
        found = []
        for n in range(3):
            if n < 2:
                target = targets[n].at[pl.ds(mine, 512), :]
            else:
                target = targets[n].at[:, pl.ds(mine, 512)]
            found.append(pltpu.make_async_copy(group[n], target, sems.at[n, 0]))
        return found

    def far():
        found = []
        for n in range(3):
            for p, (both, down) in enumerate(portions):
                index = section if p == 0 else 1 - section
                if n < 2:
                    start = pl.multiple_of(rest + index * 256, 256)
                    source = both.at[256 * n : 256 * (n + 1), :]
                    target = targets[n].at[pl.ds(start, 256), :]
                else:
                    start = pl.multiple_of(index * 384, 128)
                    source = down
                    target = targets[n].at[pl.ds(start, 384), pl.ds(rest, 512)]
                found.append(pltpu.make_async_copy(source, target, sems.at[n, 1 + p]))
        return found

    @pl.when(section == layer)
    def _():
        for copy in near(own):
            copy.start()

    @pl.when(section != layer)
    def _():
        for copy in near(swapped):
            copy.start()

    others = far()
    for copy in others:
        copy.start()
    waits = near(own)
    return [[waits[n], others[2 * n], others[2 * n + 1]] for n in range(3)]


def finish(group):
    for copy in group:
        copy.wait()


def gated(pre_gate, pre_up):
    return pre_gate / (1.0 + jnp.exp(-pre_gate)) * pre_up


def halves(place_ref, source, near, far):
    mine = pl.multiple_of(place_ref[1] * 512, 512)
    rest = pl.multiple_of((1 - place_ref[1]) * 512, 512)
    near[:, :512] = source[:, pl.ds(mine, 512)]
    far[:, :512] = source[:, pl.ds(rest, 512)]


def first_forward_body(*refs):
    place_ref, arrived = refs[0:2]
    sources = refs[2:12]
    result, early, early_far, gate_out, up_out = refs[12:17]
    w_gate, w_up, w_down, wide, rows, sems = refs[17:]
    waits = fetch(place_ref, 0, sources, (w_gate, w_up, w_down), sems)
    to_matrix(arrived[:, :16, :].reshape(1024, 128).astype(f32), wide, rows)
    halves(place_ref, rows, early, early_far)
    finish(waits[0])
    pre_gate = dot(rows[...], w_gate[...])
    gate_out[...] = pre_gate
    finish(waits[1])
    pre_up = dot(rows[...], w_up[...])
    up_out[...] = pre_up
    acts = gated(pre_gate, pre_up).astype(bf16)
    early[:, 512:] = acts
    early_far[:, 512:] = acts
    finish(waits[2])
    result[...] = to_rows(dot(acts, w_down[...]), wide).reshape(64, 16, 128)


def expert_grads(act_grad, pre_gate, pre_up):
    sigma = 1.0 / (1.0 + jnp.exp(-pre_gate))
    gate_grad = (act_grad * pre_up * sigma * (1.0 + pre_gate * (1.0 - sigma))).astype(bf16)
    up_grad = (act_grad * pre_gate * sigma).astype(bf16)
    return (gate_grad, up_grad)


def gain_part(pick_rows, normed_rows):
    product = pick_rows.astype(f32) * normed_rows.astype(f32)
    return jnp.sum(product.reshape(-1, 8, 128), axis=0)


def second_body(*refs):
    place_ref, arrived, cot, early0, early0_far = refs[0:5]
    sources = refs[5:15]
    picked, result, kept, beside, straight, cross, late, late_far, gain_out = refs[15:24]
    w_gate, w_up, w_down, wide, rows, grads, early, early_far, sems = refs[24:]
    waits = fetch(place_ref, 1, sources, (w_gate, w_up, w_down), sems)
    normed_rows = arrived[...].reshape(1024, 128)
    to_matrix(normed_rows.astype(f32), wide, rows)
    halves(place_ref, rows, early, early_far)
    to_matrix(cot[:, 16:, :].reshape(1024, 128).astype(f32), wide, grads)
    halves(place_ref, grads, late, late_far)
    finish(waits[0])
    pre_gate = dot(rows[...], w_gate[...])
    finish(waits[1])
    pre_up = dot(rows[...], w_up[...])
    acts = gated(pre_gate, pre_up).astype(bf16)
    early[:, 512:] = acts
    early_far[:, 512:] = acts
    finish(waits[2])
    act_grad = dot_nt(grads[...], w_down[...])
    gate_grad, up_grad = expert_grads(act_grad, pre_gate, pre_up)
    for target in (late, late_far):
        target[:, 512:1280] = gate_grad
        target[:, 1280:] = up_grad
    pick_rows = to_rows(dot_nt(gate_grad, w_gate[...]) + dot_nt(up_grad, w_up[...]), wide)
    picked[...] = pick_rows.reshape(64, 16, 128)
    gain_out[...] = gain_part(pick_rows, normed_rows)
    result[...] = to_rows(dot(acts, w_down[...]), wide).reshape(64, 16, 128)

    @pl.when(place_ref[0] == 0)
    def _():
        kept[...] = early0[...]
        beside[...] = early[...]
        straight[...] = early0_far[...]
        cross[...] = early_far[...]

    @pl.when(place_ref[0] != 0)
    def _():
        kept[...] = early[...]
        beside[...] = early0[...]
        straight[...] = early_far[...]
        cross[...] = early0_far[...]


def first_backward_body(*refs):
    place_ref, arrived, normed, pre_gate, pre_up, gain_second = refs[0:6]
    sources = refs[6:16]
    picked, late, late_far = refs[16:19]
    w_gate, w_up, w_down, wide, grads, sems = refs[19:]
    waits = fetch(place_ref, 0, sources, (w_gate, w_up, w_down), sems)
    to_matrix(arrived[:, :16, :].reshape(1024, 128).astype(f32), wide, grads)
    halves(place_ref, grads, late, late_far)
    finish(waits[2])
    act_grad = dot_nt(grads[...], w_down[...])
    gate_grad, up_grad = expert_grads(act_grad, pre_gate[...], pre_up[...])
    for target in (late, late_far):
        target[:, 512:1280] = gate_grad
        target[:, 1280:] = up_grad
    finish(waits[0])
    finish(waits[1])
    pick_rows = to_rows(dot_nt(gate_grad, w_gate[...]) + dot_nt(up_grad, w_up[...]), wide)
    picked[:, :16, :] = pick_rows.reshape(64, 16, 128)
    gain_first = gain_part(pick_rows, normed[:, :16, :].reshape(1024, 128))
    both = jnp.concatenate([gain_first, gain_second[...]], axis=0).astype(bf16)
    picked[:, 16:, :] = jnp.broadcast_to(both[None], (64, 16, 128))


def combined(high_t, low_t, rows):
    return dot(high_t[...], rows) + dot(low_t[...], rows)


def between_body(returned, x_ref, gain_ref, high_t, low_t, pick, hidden, out):
    rows = returned[...].reshape(1024, 128)
    result = (x_ref[...].astype(f32) + combined(high_t, low_t, rows)).astype(bf16)
    hidden[...] = result
    out[...] = chunked(dot(pick[...], normalized(result, gain_ref[...])))


def input_gradient(rows, upstream, x_block, gain, pick_t):
    normed_grad = dot(pick_t, rows).reshape(-1, 8, 128)
    values, scaling = token_stats(x_block)
    weighted = normed_grad * gain[None]
    mean = (
        jnp.sum(jnp.sum(weighted * values, axis=2, keepdims=True), axis=1, keepdims=True) / 1024.0
    )
    change = scaling * (weighted - values * scaling * scaling * mean)
    return (upstream.astype(f32) + change.reshape(upstream.shape)).astype(bf16)


def turn_body(returned, result, x_ref, grad_ref, gain_ref, pick_t, high, low, grad_out, out):
    rows = returned[...].reshape(1024, 128)
    grad = input_gradient(rows, grad_ref[...], x_ref[...], gain_ref[...], pick_t[...])
    grad_out[...] = grad
    out[:, :16, :] = chunked(dot(high[...], grad) + dot(low[...], grad))
    out[:, 16:, :] = result[...]


def second_output_body(place_ref, arrived, x_ref, high_t, low_t, hidden, sent):
    rows = arrived[:, 16:, :].reshape(1024, 128)
    before = x_ref[...].astype(f32)
    result = before + combined(high_t, low_t, rows)
    hidden[...] = result.astype(bf16)
    sent[...] = jnp.where(place_ref[0] == 0, result, before).astype(bf16)


def arrange(section, first, second, got, wide, out):
    mine = jnp.where(section == 0, first.astype(f32), second.astype(f32))
    for index, rows in ((section, mine), (1 - section, got)):
        for j, piece in enumerate(token_matrix(rows, wide)):
            out[index, :, 128 * j : 128 * (j + 1)] = piece


def hidden_body(place_ref, first, second, got, out, wide):
    arrange(place_ref[0], first[...], second[...], got[...], wide, out)


def last_body(place_ref, returned, x_ref, grad_ref, gain_ref, pick_t, grad_out, sent, gain_out):
    rows = returned[:, :16, :].reshape(1024, 128)
    grad = input_gradient(rows, grad_ref[...], x_ref[...], gain_ref[...], pick_t[...])
    grad_out[...] = grad
    sent[...] = jnp.where(
        place_ref[0] == 0, grad_ref[...].astype(f32), grad.astype(f32)
    ).astype(bf16)
    gain_out[...] = jnp.sum(returned[:, 16:, :].astype(f32), axis=0)


def final_body(*refs):
    place_ref, first, second, got = refs[0:4]
    gain_rows, gain_beside, gain_straight, gain_cross, own_gain = refs[4:9]
    out, gain_out, wide = refs[9:]
    arrange(place_ref[0], first[...], second[...], got[...], wide, out)
    total = (gain_rows[...] + gain_beside[...]) + (gain_straight[...] + gain_cross[...])
    gain_out[...] = jnp.where(place_ref[0] == 0, total[:8], total[8:]) / own_gain[...]


def weight_body(*refs):
    place_ref = refs[0]
    early_parts, first, second = refs[1:5], refs[5:9], refs[9:13]
    outs = refs[13:16]
    early, late, gate, up, down, sems, out_sems = refs[16:]

    def copies(target, group, row):
        return [
            pltpu.make_async_copy(group[n], target.at[pl.ds(128 * n, 128), :], sems.at[row, n])
            for n in range(4)
        ]

    @pl.when(place_ref[0] == 0)
    def _():
        for copy in copies(late, first, 1):
            copy.start()

    @pl.when(place_ref[0] != 0)
    def _():
        for copy in copies(late, second, 1):
            copy.start()

    for copy in copies(early, early_parts, 0):
        copy.start()
    for copy in copies(early, early_parts, 0) + copies(late, first, 1):
        copy.wait()
    normed = early[:, :512]
    done = []
    for n, target in enumerate((gate, up, down)):
        if n < 2:
            target[...] = dot_tn(normed, late[:, 512 + 768 * n : 1280 + 768 * n])
        else:
            target[...] = dot_tn(early[:, 512:], late[:, :512])
        copy = pltpu.make_async_copy(target, outs[n], out_sems.at[n])
        copy.start()
        done.append(copy)
    for copy in done:
        copy.wait()


def after(block, other):
    return lax.optimization_barrier((block, other))[0]


def window(activations, cotangent, norm_gain, w_gate, w_up, w_down, routes, gate_weights):
    section = lax.axis_index("section")
    part = lax.axis_index("dp")
    experts = lax.axis_size("expert")
    place = jnp.stack([section, part]).astype(jnp.int32)
    micro_count, tokens, width = activations.shape
    swap = [(0, 1), (1, 0)]

    def flat(s, e, d):
        return (s * experts + e) * 2 + d

    def pairs(layer, cross):
        found = []
        for s in range(2):
            target = 1 - s if cross else s
            if layer is None or target == layer:
                found += [
                    (flat(s, e, d), flat(target, e, 1 - d))
                    for e in range(experts)
                    for d in range(2)
                ]
        return found

    def beside(block, route=swap):
        return lax.ppermute(block, "section", route)

    def away(block, layer=None, cross=False):
        return lax.ppermute(block, every, pairs(layer, cross))

    def exchange(block):
        return lax.all_to_all(block, "expert", split_axis=0, concat_axis=0, tiled=True)

    own = (w_gate[0, 0], w_up[0, 0], w_down[0, 0])
    own_gain = norm_gain.reshape(8, 128)
    own_routes = routes[0].transpose(2, 0, 1)
    own_gates = gate_weights[0].transpose(2, 0, 1)
    got_routes = beside(own_routes)
    got_gates = beside(own_gates)
    got_gain = beside(own_gain)
    swapped = tuple(beside(w) for w in own)

    big = ((64, 32, 128), bf16)
    small = ((64, 16, 128), bf16)
    block = ((128, 128), bf16)
    early_shape = ((128, 1280), bf16)
    late_shape = ((128, 2048), bf16)
    down = ((1024, 128), bf16)
    across = ((128, 1024), bf16)
    weight_scratch = [
        pltpu.VMEM((1024, 768), bf16),
        pltpu.VMEM((1024, 768), bf16),
        pltpu.VMEM((768, 1024), bf16),
    ]
    wide = pltpu.VMEM((1024, 128), f32)
    narrow = pltpu.VMEM((128, 128), f32)
    matrix = pltpu.VMEM((128, 1024), bf16)
    sems = pltpu.SemaphoreType.DMA((3, 3))

    out_first, x_first, grad_last, *maps = call(
        start_body,
        [smem] + [vmem] * 8,
        [big, block, block] + [down] * 6,
        [narrow],
        flops=10**8,
        moved=2 * 10**6,
    )(
        place,
        own_routes,
        got_routes,
        own_gates,
        got_gates,
        activations,
        cotangent,
        own_gain,
        got_gain,
    )
    _, high0, low0, pick1, _, _ = maps
    first_gain = jnp.where(section == 0, own_gain, got_gain)
    second_gain = jnp.where(section == 0, got_gain, own_gain)

    packed = call(
        pack_body,
        [smem] + [anywhere] * 6,
        [((512, 768), bf16), ((384, 512), bf16)] * 2,
        [pltpu.SemaphoreType.DMA((2, 3))],
        flops=1,
        moved=5 * 10**6,
    )(place, *own, *swapped)
    portions0 = [away(w) for w in packed[:2]]
    portions0 += [beside(w) for w in portions0]
    arrived_first = exchange(out_first)

    flipped = call(flip_body, [vmem] * 6, [across] * 6, flops=10**6, moved=3 * 10**6)(*maps)
    pick0_t, high0_t, low0_t, pick1_t, high1_t, low1_t = flipped

    result, early0, early0_far, pre_gate, pre_up = call(
        first_forward_body,
        [smem, vmem] + [anywhere] * 10,
        [small, early_shape, early_shape, ((128, 768), f32), ((128, 768), f32)],
        weight_scratch + [wide, matrix, sems],
        flops=6 * 10**8,
        moved=6 * 10**6,
    )(place, arrived_first, *own, *swapped, *portions0)
    returned = exchange(result)

    portions1 = [away(after(w, other)) for w, other in zip(packed[2:], portions0)]
    portions1 += [beside(w) for w in portions1]

    hidden_first, out_second = call(
        between_body, [vmem] * 6, [block, small], flops=10**8, moved=2 * 10**6
    )(returned, x_first, second_gain, high0_t, low0_t, pick1)
    arrived_second = exchange(out_second)

    picked, result_second, kept, sent, straight, cross, late1, late1_far, gain_second = call(
        second_body,
        [smem] + [vmem] * 4 + [anywhere] * 10,
        [small, small] + [early_shape] * 4 + [late_shape] * 2 + [((8, 128), f32)],
        weight_scratch
        + [wide, matrix, matrix, pltpu.VMEM((128, 1280), bf16), pltpu.VMEM((128, 1280), bf16), sems],
        flops=12 * 10**8,
        moved=8 * 10**6,
        grant=20,
    )(place, arrived_second, arrived_first, early0, early0_far, *own, *swapped, *portions1)
    returned = exchange(picked)

    early_parts = (kept, beside(sent), away(straight), away(cross, cross=True))
    late1_parts = (late1, beside(late1, [(0, 1)]), away(late1_far, 1), away(late1_far, 1, True))

    grad_middle, out_third = call(
        turn_body, [vmem] * 8, [block, big], flops=10**8, moved=2 * 10**6
    )(
        returned,
        result_second,
        hidden_first,
        grad_last,
        second_gain,
        pick1_t,
        high0,
        low0,
    )
    arrived_third = exchange(out_third)

    picked, late0, late0_far = call(
        first_backward_body,
        [smem] + [vmem] * 5 + [anywhere] * 10,
        [big, late_shape, late_shape],
        weight_scratch + [wide, matrix, sems],
        flops=6 * 10**8,
        moved=8 * 10**6,
    )(
        place,
        arrived_third,
        arrived_first,
        pre_gate,
        pre_up,
        gain_second,
        *own,
        *swapped,
        *portions0,
    )
    late0_parts = (late0, beside(late0, [(1, 0)]), away(late0_far, 0), away(late0_far, 0, True))
    returned = exchange(picked)

    hidden_second, hidden_sent = call(
        second_output_body, [smem] + [vmem] * 4, [block, block], flops=10**8, moved=10**6
    )(place, arrived_third, hidden_first, high1_t, low1_t)
    both = ((micro_count, tokens, width), bf16)
    hidden = call(
        hidden_body, [smem] + [vmem] * 3, [both], [narrow], flops=10**5, moved=10**5
    )(place, hidden_first, hidden_second, beside(hidden_sent))[0]

    weight_grads = call(
        weight_body,
        [smem] + [anywhere] * 12,
        [((512, 768), f32), ((512, 768), f32), ((768, 512), f32)],
        [
            pltpu.VMEM((512, 1280), bf16),
            pltpu.VMEM((512, 2048), bf16),
            pltpu.VMEM((512, 768), f32),
            pltpu.VMEM((512, 768), f32),
            pltpu.VMEM((768, 512), f32),
            pltpu.SemaphoreType.DMA((2, 4)),
            pltpu.SemaphoreType.DMA((3,)),
        ],
        flops=12 * 10**8,
        moved=8 * 10**6,
        grant=24,
        out_spec=anywhere,
    )(place, *early_parts, *late0_parts, *late1_parts)

    grad_first, grad_sent, gain_rows = call(
        last_body, [smem] + [vmem] * 5, [block, block, ((16, 128), f32)], flops=10**8, moved=10**6
    )(place, returned, x_first, grad_middle, first_gain, pick0_t)
    grads, gain_grad = call(
        final_body, [smem] + [vmem] * 8, [both, ((8, 128), f32)], [narrow], flops=10**5, moved=10**5
    )(
        place,
        grad_first,
        grad_middle,
        beside(grad_sent),
        gain_rows,
        beside(gain_rows),
        away(gain_rows),
        away(gain_rows, cross=True),
        own_gain,
    )
    return (
        hidden[None],
        grads[None],
        gain_grad.reshape(1, width),
        weight_grads[0][None, None],
        weight_grads[1][None, None],
        weight_grads[2][None, None],
    )


def solution(mesh):
    placed = (
        P(None, ("expert", "dp"), None),
        P(None, ("expert", "dp"), None),
        P("section", None),
        P("section", "expert", "dp", None),
        P("section", "expert", "dp", None),
        P("section", "expert", None, "dp"),
        P("section", None, ("expert", "dp"), None),
        P("section", None, ("expert", "dp"), None),
    )
    return jax.shard_map(
        window,
        mesh=mesh,
        in_specs=placed,
        out_specs=(
            P("section", None, ("expert", "dp"), None),
            P("section", None, ("expert", "dp"), None),
            P("section", None),
            P("section", "expert", "dp", None),
            P("section", "expert", "dp", None),
            P("section", "expert", None, "dp"),
        ),
        check_vma=False,
    )
```

```python
import functools
import jax
import jax.numpy as jnp
from jax import lax
from jax.experimental import pallas as pl
from jax.experimental.pallas import tpu as pltpu
from jax.sharding import PartitionSpec as P

epsilon = 1e-06
f32 = jnp.float32
bf16 = jnp.bfloat16
every = ("section", "expert", "dp")
vmem = pl.BlockSpec(memory_space=pltpu.VMEM)
smem = pl.BlockSpec(memory_space=pltpu.SMEM)
anywhere = pl.BlockSpec(memory_space=pl.ANY)


def dot(left, right):
    return jnp.dot(left, right, preferred_element_type=f32)


def dot_nt(left, right):
    return lax.dot_general(left, right, (((1,), (1,)), ((), ())), preferred_element_type=f32)


def dot_tn(left, right):
    return lax.dot_general(left, right, (((0,), (0,)), ((), ())), preferred_element_type=f32)


def call(body, in_specs, outs, scratch=(), flops=0, moved=0, grant=None, out_spec=vmem):
    return pl.pallas_call(
        body,
        in_specs=in_specs,
        out_shape=[jax.ShapeDtypeStruct(shape, dtype) for shape, dtype in outs],
        out_specs=[out_spec] * len(outs),
        scratch_shapes=list(scratch),
        cost_estimate=pl.CostEstimate(flops=flops, bytes_accessed=moved, transcendentals=0),
        compiler_params=pltpu.CompilerParams(vmem_limit_bytes=grant and grant * 2**20),
    )


def token_rows(block, wide):
    values = block.astype(f32)
    for j in range(8):
        wide[pl.ds(j, 16, stride=8), :] = values[:, 128 * j : 128 * (j + 1)]
    return wide[...].astype(bf16)


def token_matrix(rows, wide):
    wide[...] = rows.astype(f32)
    return [wide[pl.ds(j, 16, stride=8), :].astype(bf16) for j in range(8)]


def token_stats(block):
    values = block.astype(f32).reshape(-1, 8, 128)
    mean = jnp.sum(jnp.sum(values * values, axis=2, keepdims=True), axis=1, keepdims=True) / 1024.0
    return (values, lax.rsqrt(mean + epsilon))


def normalized(block, gain):
    values, scaling = token_stats(block)
    return (values * scaling * gain[None]).astype(bf16).reshape(block.shape)


def chunked(rows):
    return rows.astype(bf16).reshape(64, -1, 128)


def fill_tables(ids, gates, pick, high, low):
    token = lax.broadcasted_iota(jnp.int32, (16, 128), 0)
    lane = lax.broadcasted_iota(jnp.int32, (16, 128), 1)
    spread = jnp.where(lax.shift_right_logical(lane, 3) == token, 1.0, 0.0).astype(bf16)
    names = dot(ids.astype(f32).astype(bf16), spread)
    gates_high = gates.astype(bf16)
    gates_low = (gates - gates_high.astype(f32)).astype(bf16)
    upper = dot(gates_high, spread)
    lower = dot(gates_low, spread)
    expert = lax.broadcasted_iota(jnp.int32, (64, 128), 0).astype(f32)
    named = jnp.zeros((64, 128), f32)
    first = jnp.zeros((64, 128), f32)
    second = jnp.zeros((64, 128), f32)
    for k in range(ids.shape[0]):
        match = expert == names[k : k + 1, :]
        named = jnp.where(match, 1.0, named)
        first = jnp.where(match, upper[k : k + 1, :], first)
        second = jnp.where(match, lower[k : k + 1, :], second)
    row = lax.broadcasted_iota(jnp.int32, (128, 128), 0)
    column = lax.broadcasted_iota(jnp.int32, (128, 128), 1)
    earlier = ((row & 7) == 0) & (
        lax.shift_right_logical(row, 3) < lax.shift_right_logical(column, 3)
    )
    before = dot(named.astype(bf16), jnp.where(earlier, 1.0, 0.0).astype(bf16))
    code = jnp.where(named > 0.0, before + 1.0, 0.0)
    slot_row = lax.broadcasted_iota(jnp.int32, (1, 16, 128), 1)
    slot_lane = lax.broadcasted_iota(jnp.int32, (1, 16, 128), 2)
    wanted = lax.shift_right_logical(slot_row, 3).astype(f32) + 1.0
    wanted = jnp.where((slot_row & 7) == (slot_lane & 7), wanted, 9.0)
    shape = (64, 16, 128)
    match = jnp.broadcast_to(code[:, None, :], shape) == jnp.broadcast_to(wanted, shape)
    zero = jnp.zeros(shape, f32)
    pick[...] = jnp.where(match, 1.0, zero).astype(bf16).reshape(1024, 128)
    first = jnp.broadcast_to(first[:, None, :], shape)
    high[...] = jnp.where(match, first, zero).astype(bf16).reshape(1024, 128)
    second = jnp.broadcast_to(second[:, None, :], shape)
    low[...] = jnp.where(match, second, zero).astype(bf16).reshape(1024, 128)


def start_body(*refs):
    place_ref, own_routes, got_routes, own_gates, got_gates = refs[0:5]
    x_ref, grad_ref, own_gain, got_gain = refs[5:9]
    out, x_rows, grad_rows = refs[9:12]
    pick0, high0, low0, pick1, high1, low1 = refs[12:18]
    wide = refs[18]
    section = place_ref[0]
    ids = (own_routes[:, section, :], got_routes[:, section, :])
    gates = (own_gates[:, section, :], got_gates[:, section, :])
    lower = section == 0
    fill_tables(
        jnp.where(lower, ids[0], ids[1]),
        jnp.where(lower, gates[0], gates[1]),
        pick0,
        high0,
        low0,
    )
    fill_tables(
        jnp.where(lower, ids[1], ids[0]),
        jnp.where(lower, gates[1], gates[0]),
        pick1,
        high1,
        low1,
    )
    x_block = token_rows(x_ref[section], wide)
    x_rows[...] = x_block
    gain = jnp.where(lower, own_gain[...], got_gain[...])
    out[:, :16, :] = chunked(dot(pick0[...], normalized(x_block, gain)))
    grad = token_rows(grad_ref[section], wide)
    grad_rows[...] = grad
    out[:, 16:, :] = chunked(dot(high1[...], grad) + dot(low1[...], grad))


def flip_body(*refs):
    for source, target in zip(refs[:6], refs[6:]):
        target[...] = source[...].astype(f32).T.astype(bf16)


def pack_body(layer, *refs):
    place_ref = refs[0]
    own, swapped = refs[1:4], refs[4:7]
    both, last, sems = refs[7:10]
    section = place_ref[0]
    start = pl.multiple_of(section * 256, 256)
    start_down = pl.multiple_of(section * 384, 128)

    def copies(group):
        gate, up, down = group
        return [
            pltpu.make_async_copy(gate.at[pl.ds(start, 256), :], both.at[0:256, :], sems.at[0]),
            pltpu.make_async_copy(up.at[pl.ds(start, 256), :], both.at[256:512, :], sems.at[1]),
            pltpu.make_async_copy(down.at[pl.ds(start_down, 384), :], last, sems.at[2]),
        ]

    @pl.when(section == layer)
    def _():
        for copy in copies(own):
            copy.start()

    @pl.when(section != layer)
    def _():
        for copy in copies(swapped):
            copy.start()

    for copy in copies(own):
        copy.wait()


def to_matrix(rows, wide, target):
    wide[...] = rows
    slots = rows.shape[0] // 8
    for j in range(8):
        target[:, 128 * j : 128 * (j + 1)] = wide[pl.ds(j, slots, stride=8), :].astype(bf16)


def to_rows(matrix, wide):
    slots = matrix.shape[0]
    for j in range(8):
        wide[pl.ds(j, slots, stride=8), :] = matrix[:, 128 * j : 128 * (j + 1)]
    return wide[...].astype(bf16)


def fetch(place_ref, layer, sources, targets, sems):
    own, swapped = sources[0:3], sources[3:6]
    portions = (sources[6:8], sources[8:10])
    section, part = place_ref[0], place_ref[1]
    mine = pl.multiple_of(part * 512, 512)
    rest = pl.multiple_of((1 - part) * 512, 512)

    def near(group):
        found = []
        for n in range(3):
            if n < 2:
                target = targets[n].at[pl.ds(mine, 512), :]
            else:
                target = targets[n].at[:, pl.ds(mine, 512)]
            found.append(pltpu.make_async_copy(group[n], target, sems.at[n, 0]))
        return found

    def far():
        found = []
        for n in range(3):
            for p, (both, down) in enumerate(portions):
                index = section if p == 0 else 1 - section
                if n < 2:
                    start = pl.multiple_of(rest + index * 256, 256)
                    source = both.at[256 * n : 256 * (n + 1), :]
                    target = targets[n].at[pl.ds(start, 256), :]
                else:
                    start = pl.multiple_of(index * 384, 128)
                    source = down
                    target = targets[n].at[pl.ds(start, 384), pl.ds(rest, 512)]
                found.append(pltpu.make_async_copy(source, target, sems.at[n, 1 + p]))
        return found

    @pl.when(section == layer)
    def _():
        for copy in near(own):
            copy.start()

    @pl.when(section != layer)
    def _():
        for copy in near(swapped):
            copy.start()

    others = far()
    for copy in others:
        copy.start()
    waits = near(own)
    return [[waits[n], others[2 * n], others[2 * n + 1]] for n in range(3)]


def finish(group):
    for copy in group:
        copy.wait()


def gated(pre_gate, pre_up):
    return pre_gate / (1.0 + jnp.exp(-pre_gate)) * pre_up


def halves(place_ref, source, near, far):
    mine = pl.multiple_of(place_ref[1] * 512, 512)
    rest = pl.multiple_of((1 - place_ref[1]) * 512, 512)
    near[:, :512] = source[:, pl.ds(mine, 512)]
    far[:, :512] = source[:, pl.ds(rest, 512)]


def first_forward_body(*refs):
    place_ref, arrived = refs[0:2]
    sources = refs[2:12]
    result, early, early_far, gate_out, up_out = refs[12:17]
    w_gate, w_up, w_down, wide, rows, sems = refs[17:]
    waits = fetch(place_ref, 0, sources, (w_gate, w_up, w_down), sems)
    to_matrix(arrived[:, :16, :].reshape(1024, 128).astype(f32), wide, rows)
    halves(place_ref, rows, early, early_far)
    finish(waits[0])
    pre_gate = dot(rows[...], w_gate[...])
    gate_out[...] = pre_gate
    finish(waits[1])
    pre_up = dot(rows[...], w_up[...])
    up_out[...] = pre_up
    acts = gated(pre_gate, pre_up).astype(bf16)
    early[:, 512:] = acts
    early_far[:, 512:] = acts
    finish(waits[2])
    result[...] = to_rows(dot(acts, w_down[...]), wide).reshape(64, 16, 128)


def expert_grads(act_grad, pre_gate, pre_up):
    sigma = 1.0 / (1.0 + jnp.exp(-pre_gate))
    gate_grad = (act_grad * pre_up * sigma * (1.0 + pre_gate * (1.0 - sigma))).astype(bf16)
    up_grad = (act_grad * pre_gate * sigma).astype(bf16)
    return (gate_grad, up_grad)


def gain_part(pick_rows, normed_rows):
    product = pick_rows.astype(f32) * normed_rows.astype(f32)
    return jnp.sum(product.reshape(-1, 8, 128), axis=0)


def second_body(*refs):
    place_ref, arrived, cot, early0, early0_far = refs[0:5]
    sources = refs[5:15]
    picked, result, kept, beside, straight, cross, late, late_far, gain_out = refs[15:24]
    w_gate, w_up, w_down, wide, rows, grads, early, early_far, sems = refs[24:]
    waits = fetch(place_ref, 1, sources, (w_gate, w_up, w_down), sems)
    normed_rows = arrived[...].reshape(1024, 128)
    to_matrix(normed_rows.astype(f32), wide, rows)
    halves(place_ref, rows, early, early_far)
    to_matrix(cot[:, 16:, :].reshape(1024, 128).astype(f32), wide, grads)
    halves(place_ref, grads, late, late_far)
    finish(waits[0])
    pre_gate = dot(rows[...], w_gate[...])
    finish(waits[1])
    pre_up = dot(rows[...], w_up[...])
    acts = gated(pre_gate, pre_up).astype(bf16)
    early[:, 512:] = acts
    early_far[:, 512:] = acts
    finish(waits[2])
    act_grad = dot_nt(grads[...], w_down[...])
    gate_grad, up_grad = expert_grads(act_grad, pre_gate, pre_up)
    for target in (late, late_far):
        target[:, 512:1280] = gate_grad
        target[:, 1280:] = up_grad
    pick_rows = to_rows(dot_nt(gate_grad, w_gate[...]) + dot_nt(up_grad, w_up[...]), wide)
    picked[...] = pick_rows.reshape(64, 16, 128)
    gain_out[...] = gain_part(pick_rows, normed_rows)
    result[...] = to_rows(dot(acts, w_down[...]), wide).reshape(64, 16, 128)

    @pl.when(place_ref[0] == 0)
    def _():
        kept[...] = early0[...]
        beside[...] = early[...]
        straight[...] = early0_far[...]
        cross[...] = early_far[...]

    @pl.when(place_ref[0] != 0)
    def _():
        kept[...] = early[...]
        beside[...] = early0[...]
        straight[...] = early_far[...]
        cross[...] = early0_far[...]


def first_backward_body(*refs):
    place_ref, arrived, normed, pre_gate, pre_up, gain_second = refs[0:6]
    sources = refs[6:16]
    picked, late, late_far = refs[16:19]
    w_gate, w_up, w_down, wide, grads, sems = refs[19:]
    waits = fetch(place_ref, 0, sources, (w_gate, w_up, w_down), sems)
    to_matrix(arrived[:, :16, :].reshape(1024, 128).astype(f32), wide, grads)
    halves(place_ref, grads, late, late_far)
    finish(waits[2])
    act_grad = dot_nt(grads[...], w_down[...])
    gate_grad, up_grad = expert_grads(act_grad, pre_gate[...], pre_up[...])
    for target in (late, late_far):
        target[:, 512:1280] = gate_grad
        target[:, 1280:] = up_grad
    finish(waits[0])
    finish(waits[1])
    pick_rows = to_rows(dot_nt(gate_grad, w_gate[...]) + dot_nt(up_grad, w_up[...]), wide)
    picked[:, :16, :] = pick_rows.reshape(64, 16, 128)
    gain_first = gain_part(pick_rows, normed[:, :16, :].reshape(1024, 128))
    both = jnp.concatenate([gain_first, gain_second[...]], axis=0).astype(bf16)
    picked[:, 16:, :] = jnp.broadcast_to(both[None], (64, 16, 128))


def combined(high_t, low_t, rows):
    return dot(high_t[...], rows) + dot(low_t[...], rows)


def between_body(returned, x_ref, gain_ref, high_t, low_t, pick, hidden, out):
    rows = returned[...].reshape(1024, 128)
    result = (x_ref[...].astype(f32) + combined(high_t, low_t, rows)).astype(bf16)
    hidden[...] = result
    out[...] = chunked(dot(pick[...], normalized(result, gain_ref[...])))


def input_gradient(rows, upstream, x_block, gain, pick_t):
    normed_grad = dot(pick_t, rows).reshape(-1, 8, 128)
    values, scaling = token_stats(x_block)
    weighted = normed_grad * gain[None]
    mean = (
        jnp.sum(jnp.sum(weighted * values, axis=2, keepdims=True), axis=1, keepdims=True) / 1024.0
    )
    change = scaling * (weighted - values * scaling * scaling * mean)
    return (upstream.astype(f32) + change.reshape(upstream.shape)).astype(bf16)


def turn_body(returned, result, x_ref, grad_ref, gain_ref, pick_t, high, low, grad_out, out):
    rows = returned[...].reshape(1024, 128)
    grad = input_gradient(rows, grad_ref[...], x_ref[...], gain_ref[...], pick_t[...])
    grad_out[...] = grad
    out[:, :16, :] = chunked(dot(high[...], grad) + dot(low[...], grad))
    out[:, 16:, :] = result[...]


def second_output_body(place_ref, arrived, x_ref, high_t, low_t, hidden, sent):
    rows = arrived[:, 16:, :].reshape(1024, 128)
    before = x_ref[...].astype(f32)
    result = before + combined(high_t, low_t, rows)
    hidden[...] = result.astype(bf16)
    sent[...] = jnp.where(place_ref[0] == 0, result, before).astype(bf16)


def arrange(section, first, second, got, wide, out):
    mine = jnp.where(section == 0, first.astype(f32), second.astype(f32))
    for index, rows in ((section, mine), (1 - section, got)):
        for j, piece in enumerate(token_matrix(rows, wide)):
            out[index, :, 128 * j : 128 * (j + 1)] = piece


def hidden_body(place_ref, first, second, got, out, wide):
    arrange(place_ref[0], first[...], second[...], got[...], wide, out)


def last_body(place_ref, returned, x_ref, grad_ref, gain_ref, pick_t, grad_out, sent, gain_out):
    rows = returned[:, :16, :].reshape(1024, 128)
    grad = input_gradient(rows, grad_ref[...], x_ref[...], gain_ref[...], pick_t[...])
    grad_out[...] = grad
    sent[...] = jnp.where(
        place_ref[0] == 0, grad_ref[...].astype(f32), grad.astype(f32)
    ).astype(bf16)
    gain_out[...] = jnp.sum(returned[:, 16:, :].astype(f32), axis=0)


def final_body(*refs):
    place_ref, first, second, got = refs[0:4]
    gain_rows, gain_beside, gain_straight, gain_cross, own_gain = refs[4:9]
    out, gain_out, wide = refs[9:]
    arrange(place_ref[0], first[...], second[...], got[...], wide, out)
    total = (gain_rows[...] + gain_beside[...]) + (gain_straight[...] + gain_cross[...])
    gain_out[...] = jnp.where(place_ref[0] == 0, total[:8], total[8:]) / own_gain[...]


def weight_body(*refs):
    place_ref = refs[0]
    early_parts, first, second = refs[1:5], refs[5:9], refs[9:13]
    outs = refs[13:16]
    early, late, gate, up, down, sems, out_sems = refs[16:]

    def copies(target, group, row):
        return [
            pltpu.make_async_copy(group[n], target.at[pl.ds(128 * n, 128), :], sems.at[row, n])
            for n in range(4)
        ]

    @pl.when(place_ref[0] == 0)
    def _():
        for copy in copies(late, first, 1):
            copy.start()

    @pl.when(place_ref[0] != 0)
    def _():
        for copy in copies(late, second, 1):
            copy.start()

    for copy in copies(early, early_parts, 0):
        copy.start()
    for copy in copies(early, early_parts, 0) + copies(late, first, 1):
        copy.wait()
    normed = early[:, :512]
    done = []
    for n, target in enumerate((gate, up, down)):
        if n < 2:
            target[...] = dot_tn(normed, late[:, 512 + 768 * n : 1280 + 768 * n])
        else:
            target[...] = dot_tn(early[:, 512:], late[:, :512])
        copy = pltpu.make_async_copy(target, outs[n], out_sems.at[n])
        copy.start()
        done.append(copy)
    for copy in done:
        copy.wait()


def after(block, other):
    return lax.optimization_barrier((block, other))[0]


def window(activations, cotangent, norm_gain, w_gate, w_up, w_down, routes, gate_weights):
    section = lax.axis_index("section")
    part = lax.axis_index("dp")
    experts = lax.axis_size("expert")
    place = jnp.stack([section, part]).astype(jnp.int32)
    micro_count, tokens, width = activations.shape
    swap = [(0, 1), (1, 0)]

    def flat(s, e, d):
        return (s * experts + e) * 2 + d

    def pairs(layer, cross):
        found = []
        for s in range(2):
            target = 1 - s if cross else s
            if layer is None or target == layer:
                found += [
                    (flat(s, e, d), flat(target, e, 1 - d))
                    for e in range(experts)
                    for d in range(2)
                ]
        return found

    def beside(block, route=swap):
        return lax.ppermute(block, "section", route)

    def away(block, layer=None, cross=False):
        return lax.ppermute(block, every, pairs(layer, cross))

    def exchange(block):
        return lax.all_to_all(block, "expert", split_axis=0, concat_axis=0, tiled=True)

    own = (w_gate[0, 0], w_up[0, 0], w_down[0, 0])
    own_gain = norm_gain.reshape(8, 128)
    own_routes = routes[0].transpose(2, 0, 1)
    own_gates = gate_weights[0].transpose(2, 0, 1)
    got_routes = beside(own_routes)
    got_gates = beside(own_gates)
    got_gain = beside(own_gain)
    swapped = tuple(beside(w) for w in own)

    big = ((64, 32, 128), bf16)
    small = ((64, 16, 128), bf16)
    block = ((128, 128), bf16)
    early_shape = ((128, 1280), bf16)
    late_shape = ((128, 2048), bf16)
    down = ((1024, 128), bf16)
    across = ((128, 1024), bf16)
    weight_scratch = [
        pltpu.VMEM((1024, 768), bf16),
        pltpu.VMEM((1024, 768), bf16),
        pltpu.VMEM((768, 1024), bf16),
    ]
    wide = pltpu.VMEM((1024, 128), f32)
    narrow = pltpu.VMEM((128, 128), f32)
    matrix = pltpu.VMEM((128, 1024), bf16)
    sems = pltpu.SemaphoreType.DMA((3, 3))

    out_first, x_first, grad_last, *maps = call(
        start_body,
        [smem] + [vmem] * 8,
        [big, block, block] + [down] * 6,
        [narrow],
        flops=10**8,
        moved=2 * 10**6,
    )(
        place,
        own_routes,
        got_routes,
        own_gates,
        got_gates,
        activations,
        cotangent,
        own_gain,
        got_gain,
    )
    _, high0, low0, pick1, _, _ = maps
    first_gain = jnp.where(section == 0, own_gain, got_gain)
    second_gain = jnp.where(section == 0, got_gain, own_gain)

    def packed(layer):
        return call(
            functools.partial(pack_body, layer),
            [smem] + [anywhere] * 6,
            [((512, 768), bf16), ((384, 512), bf16)],
            [pltpu.SemaphoreType.DMA((3,))],
            flops=1,
            moved=25 * 10**5,
        )(place, *own, *swapped)

    portions0 = [away(w) for w in packed(0)]
    portions0 += [beside(w) for w in portions0]
    arrived_first = exchange(out_first)

    flipped = call(flip_body, [vmem] * 6, [across] * 6, flops=10**6, moved=3 * 10**6)(*maps)
    pick0_t, high0_t, low0_t, pick1_t, high1_t, low1_t = flipped

    result, early0, early0_far, pre_gate, pre_up = call(
        first_forward_body,
        [smem, vmem] + [anywhere] * 10,
        [small, early_shape, early_shape, ((128, 768), f32), ((128, 768), f32)],
        weight_scratch + [wide, matrix, sems],
        flops=6 * 10**8,
        moved=6 * 10**6,
    )(place, arrived_first, *own, *swapped, *portions0)
    returned = exchange(result)

    portions1 = [away(after(w, other)) for w, other in zip(packed(1), portions0)]
    portions1 += [beside(w) for w in portions1]

    hidden_first, out_second = call(
        between_body, [vmem] * 6, [block, small], flops=10**8, moved=2 * 10**6
    )(returned, x_first, second_gain, high0_t, low0_t, pick1)
    arrived_second = exchange(out_second)

    picked, result_second, kept, sent, straight, cross, late1, late1_far, gain_second = call(
        second_body,
        [smem] + [vmem] * 4 + [anywhere] * 10,
        [small, small] + [early_shape] * 4 + [late_shape] * 2 + [((8, 128), f32)],
        weight_scratch
        + [wide, matrix, matrix, pltpu.VMEM((128, 1280), bf16), pltpu.VMEM((128, 1280), bf16), sems],
        flops=12 * 10**8,
        moved=8 * 10**6,
    )(place, arrived_second, arrived_first, early0, early0_far, *own, *swapped, *portions1)
    returned = exchange(picked)

    early_parts = (kept, beside(sent), away(straight), away(cross, cross=True))
    late1_parts = (late1, beside(late1, [(0, 1)]), away(late1_far, 1), away(late1_far, 1, True))

    grad_middle, out_third = call(
        turn_body, [vmem] * 8, [block, big], flops=10**8, moved=2 * 10**6
    )(
        returned,
        result_second,
        hidden_first,
        grad_last,
        second_gain,
        pick1_t,
        high0,
        low0,
    )
    arrived_third = exchange(out_third)

    picked, late0, late0_far = call(
        first_backward_body,
        [smem] + [vmem] * 5 + [anywhere] * 10,
        [big, late_shape, late_shape],
        weight_scratch + [wide, matrix, sems],
        flops=6 * 10**8,
        moved=8 * 10**6,
    )(
        place,
        arrived_third,
        arrived_first,
        pre_gate,
        pre_up,
        gain_second,
        *own,
        *swapped,
        *portions0,
    )
    late0_parts = (late0, beside(late0, [(1, 0)]), away(late0_far, 0), away(late0_far, 0, True))
    returned = exchange(picked)

    hidden_second, hidden_sent = call(
        second_output_body, [smem] + [vmem] * 4, [block, block], flops=10**8, moved=10**6
    )(place, arrived_third, hidden_first, high1_t, low1_t)
    both = ((micro_count, tokens, width), bf16)
    hidden = call(
        hidden_body, [smem] + [vmem] * 3, [both], [narrow], flops=10**5, moved=10**5, grant=16
    )(place, hidden_first, hidden_second, beside(hidden_sent))[0]

    weight_grads = call(
        weight_body,
        [smem] + [anywhere] * 12,
        [((512, 768), f32), ((512, 768), f32), ((768, 512), f32)],
        [
            pltpu.VMEM((512, 1280), bf16),
            pltpu.VMEM((512, 2048), bf16),
            pltpu.VMEM((512, 768), f32),
            pltpu.VMEM((512, 768), f32),
            pltpu.VMEM((768, 512), f32),
            pltpu.SemaphoreType.DMA((2, 4)),
            pltpu.SemaphoreType.DMA((3,)),
        ],
        flops=12 * 10**8,
        moved=8 * 10**6,
        out_spec=anywhere,
    )(place, *early_parts, *late0_parts, *late1_parts)

    grad_first, grad_sent, gain_rows = call(
        last_body, [smem] + [vmem] * 5, [block, block, ((16, 128), f32)], flops=10**8, moved=10**6
    )(place, returned, x_first, grad_middle, first_gain, pick0_t)
    grads, gain_grad = call(
        final_body,
        [smem] + [vmem] * 8,
        [both, ((8, 128), f32)],
        [narrow],
        flops=10**5,
        moved=10**5,
        grant=16,
    )(
        place,
        grad_first,
        grad_middle,
        beside(grad_sent),
        gain_rows,
        beside(gain_rows),
        away(gain_rows),
        away(gain_rows, cross=True),
        own_gain,
    )
    return (
        hidden[None],
        grads[None],
        gain_grad.reshape(1, width),
        weight_grads[0][None, None],
        weight_grads[1][None, None],
        weight_grads[2][None, None],
    )


def solution(mesh):
    placed = (
        P(None, ("expert", "dp"), None),
        P(None, ("expert", "dp"), None),
        P("section", None),
        P("section", "expert", "dp", None),
        P("section", "expert", "dp", None),
        P("section", "expert", None, "dp"),
        P("section", None, ("expert", "dp"), None),
        P("section", None, ("expert", "dp"), None),
    )
    return jax.shard_map(
        window,
        mesh=mesh,
        in_specs=placed,
        out_specs=(
            P("section", None, ("expert", "dp"), None),
            P("section", None, ("expert", "dp"), None),
            P("section", None),
            P("section", "expert", "dp", None),
            P("section", "expert", "dp", None),
            P("section", "expert", None, "dp"),
        ),
        check_vma=False,
    )
```

```python
import functools
import jax
import jax.numpy as jnp
from jax import lax
from jax.experimental import pallas as pl
from jax.experimental.pallas import tpu as pltpu
from jax.sharding import PartitionSpec as P

epsilon = 1e-06
f32 = jnp.float32
bf16 = jnp.bfloat16
every = ("section", "expert", "dp")
vmem = pl.BlockSpec(memory_space=pltpu.VMEM)
smem = pl.BlockSpec(memory_space=pltpu.SMEM)
anywhere = pl.BlockSpec(memory_space=pl.ANY)


def dot(left, right):
    return jnp.dot(left, right, preferred_element_type=f32)


def dot_nt(left, right):
    return lax.dot_general(left, right, (((1,), (1,)), ((), ())), preferred_element_type=f32)


def dot_tn(left, right):
    return lax.dot_general(left, right, (((0,), (0,)), ((), ())), preferred_element_type=f32)


def call(body, in_specs, outs, scratch=(), flops=0, moved=0, grant=None, out_spec=vmem):
    return pl.pallas_call(
        body,
        in_specs=in_specs,
        out_shape=[jax.ShapeDtypeStruct(shape, dtype) for shape, dtype in outs],
        out_specs=out_spec if isinstance(out_spec, list) else [out_spec] * len(outs),
        scratch_shapes=list(scratch),
        cost_estimate=pl.CostEstimate(flops=flops, bytes_accessed=moved, transcendentals=0),
        compiler_params=pltpu.CompilerParams(vmem_limit_bytes=grant and grant * 2**20),
    )


def token_rows(block, wide):
    values = block.astype(f32)
    for j in range(8):
        wide[pl.ds(j, 16, stride=8), :] = values[:, 128 * j : 128 * (j + 1)]
    return wide[...].astype(bf16)


def token_matrix(rows, wide):
    wide[...] = rows.astype(f32)
    return [wide[pl.ds(j, 16, stride=8), :].astype(bf16) for j in range(8)]


def token_stats(block):
    values = block.astype(f32).reshape(-1, 8, 128)
    mean = jnp.sum(jnp.sum(values * values, axis=2, keepdims=True), axis=1, keepdims=True) / 1024.0
    return (values, lax.rsqrt(mean + epsilon))


def normalized(block, gain):
    values, scaling = token_stats(block)
    return (values * scaling * gain[None]).astype(bf16).reshape(block.shape)


def chunked(rows):
    return rows.astype(bf16).reshape(64, -1, 128)


def fill_tables(ids, gates, pick, high, low):
    token = lax.broadcasted_iota(jnp.int32, (16, 128), 0)
    lane = lax.broadcasted_iota(jnp.int32, (16, 128), 1)
    spread = jnp.where(lax.shift_right_logical(lane, 3) == token, 1.0, 0.0).astype(bf16)
    names = dot(ids.astype(f32).astype(bf16), spread)
    gates_high = gates.astype(bf16)
    gates_low = (gates - gates_high.astype(f32)).astype(bf16)
    upper = dot(gates_high, spread)
    lower = dot(gates_low, spread)
    expert = lax.broadcasted_iota(jnp.int32, (64, 128), 0).astype(f32)
    named = jnp.zeros((64, 128), f32)
    first = jnp.zeros((64, 128), f32)
    second = jnp.zeros((64, 128), f32)
    for k in range(ids.shape[0]):
        match = expert == names[k : k + 1, :]
        named = jnp.where(match, 1.0, named)
        first = jnp.where(match, upper[k : k + 1, :], first)
        second = jnp.where(match, lower[k : k + 1, :], second)
    row = lax.broadcasted_iota(jnp.int32, (128, 128), 0)
    column = lax.broadcasted_iota(jnp.int32, (128, 128), 1)
    earlier = ((row & 7) == 0) & (
        lax.shift_right_logical(row, 3) < lax.shift_right_logical(column, 3)
    )
    before = dot(named.astype(bf16), jnp.where(earlier, 1.0, 0.0).astype(bf16))
    code = jnp.where(named > 0.0, before + 1.0, 0.0)
    slot_row = lax.broadcasted_iota(jnp.int32, (1, 16, 128), 1)
    slot_lane = lax.broadcasted_iota(jnp.int32, (1, 16, 128), 2)
    wanted = lax.shift_right_logical(slot_row, 3).astype(f32) + 1.0
    wanted = jnp.where((slot_row & 7) == (slot_lane & 7), wanted, 9.0)
    shape = (64, 16, 128)
    match = jnp.broadcast_to(code[:, None, :], shape) == jnp.broadcast_to(wanted, shape)
    zero = jnp.zeros(shape, f32)
    pick[...] = jnp.where(match, 1.0, zero).astype(bf16).reshape(1024, 128)
    first = jnp.broadcast_to(first[:, None, :], shape)
    high[...] = jnp.where(match, first, zero).astype(bf16).reshape(1024, 128)
    second = jnp.broadcast_to(second[:, None, :], shape)
    low[...] = jnp.where(match, second, zero).astype(bf16).reshape(1024, 128)


def start_body(*refs):
    place_ref, own_routes, got_routes, own_gates, got_gates = refs[0:5]
    x_ref, grad_ref, own_gain, got_gain = refs[5:9]
    out, x_rows, grad_rows = refs[9:12]
    pick0, high0, low0, pick1, high1, low1 = refs[12:18]
    wide = refs[18]
    section = place_ref[0]
    ids = (own_routes[:, section, :], got_routes[:, section, :])
    gates = (own_gates[:, section, :], got_gates[:, section, :])
    lower = section == 0
    fill_tables(
        jnp.where(lower, ids[0], ids[1]),
        jnp.where(lower, gates[0], gates[1]),
        pick0,
        high0,
        low0,
    )
    fill_tables(
        jnp.where(lower, ids[1], ids[0]),
        jnp.where(lower, gates[1], gates[0]),
        pick1,
        high1,
        low1,
    )
    x_block = token_rows(x_ref[section], wide)
    x_rows[...] = x_block
    gain = jnp.where(lower, own_gain[...], got_gain[...])
    out[:, :16, :] = chunked(dot(pick0[...], normalized(x_block, gain)))
    grad = token_rows(grad_ref[section], wide)
    grad_rows[...] = grad
    out[:, 16:, :] = chunked(dot(high1[...], grad) + dot(low1[...], grad))


def flip_body(*refs):
    for source, target in zip(refs[:6], refs[6:]):
        target[...] = source[...].astype(f32).T.astype(bf16)


def pack_body(layer, tensors, *refs):
    place_ref = refs[0]
    own, swapped = refs[1 : 1 + len(tensors)], refs[1 + len(tensors) : 1 + 2 * len(tensors)]
    outs, sems = refs[1 + 2 * len(tensors) : -1], refs[-1]
    section = place_ref[0]
    start = pl.multiple_of(section * 256, 256)
    start_down = pl.multiple_of(section * 384, 128)

    def copies(group):
        found = []
        for n, ref in zip(tensors, group):
            if n < 2:
                source, target = ref.at[pl.ds(start, 256), :], outs[0].at[256 * n : 256 * n + 256, :]
            else:
                source, target = ref.at[pl.ds(start_down, 384), :], outs[-1]
            found.append(pltpu.make_async_copy(source, target, sems.at[n]))
        return found

    @pl.when(section == layer)
    def _():
        for copy in copies(own):
            copy.start()

    @pl.when(section != layer)
    def _():
        for copy in copies(swapped):
            copy.start()

    for copy in copies(own):
        copy.wait()


def to_matrix(rows, wide, target):
    wide[...] = rows
    slots = rows.shape[0] // 8
    for j in range(8):
        target[:, 128 * j : 128 * (j + 1)] = wide[pl.ds(j, slots, stride=8), :].astype(bf16)


def to_rows(matrix, wide):
    slots = matrix.shape[0]
    for j in range(8):
        wide[pl.ds(j, slots, stride=8), :] = matrix[:, 128 * j : 128 * (j + 1)]
    return wide[...].astype(bf16)


def fetch(place_ref, layer, sources, targets, sems):
    own, swapped = sources[0:3], sources[3:6]
    section, part = place_ref[0], place_ref[1]
    mine = pl.multiple_of(part * 512, 512)
    rest = pl.multiple_of((1 - part) * 512, 512)
    downs = sources[-2:]

    def near(group, others):
        found = []
        for n in range(3):
            if n < 2:
                target = targets[n].at[pl.ds(mine, 512), :]
            else:
                target = targets[n].at[:, pl.ds(mine, 512)]
            found.append([pltpu.make_async_copy(group[n], target, sems.at[n, 0])])
        for n, source in enumerate(others):
            target = targets[n].at[pl.ds(rest, 512), :]
            found[n].append(pltpu.make_async_copy(source, target, sems.at[n, 1]))
        return found

    def far(n):
        found = []
        for p in range(2):
            index = section if p == 0 else 1 - section
            if n < 2:
                start = pl.multiple_of(rest + index * 256, 256)
                source = sources[6 + p].at[256 * n : 256 * (n + 1), :]
                target = targets[n].at[pl.ds(start, 256), :]
            else:
                start = pl.multiple_of(index * 384, 128)
                source = downs[p]
                target = targets[n].at[pl.ds(start, 384), pl.ds(rest, 512)]
            found.append(pltpu.make_async_copy(source, target, sems.at[n, 1 + p]))
        return found

    if layer == 0:
        gate_far, gate_passed, up_far, up_passed = sources[6:10]
        lower, upper = (gate_far, up_passed), (gate_passed, up_far)
        others = [[], [], far(2)]
    else:
        lower, upper = (), ()
        others = [far(0), far(1), far(2)]

    @pl.when(section == 0)
    def _():
        for copies in near(own if layer == 0 else swapped, lower):
            for copy in copies:
                copy.start()

    @pl.when(section != 0)
    def _():
        for copies in near(swapped if layer == 0 else own, upper):
            for copy in copies:
                copy.start()

    for copies in others:
        for copy in copies:
            copy.start()
    return [first + second for first, second in zip(near(own, lower), others)]


def begin(source, target, sem):
    copy = pltpu.make_async_copy(source, target, sem)
    copy.start()
    return copy


def finish(group):
    for copy in group:
        copy.wait()


def gated(pre_gate, pre_up):
    return pre_gate / (1.0 + jnp.exp(-pre_gate)) * pre_up


def halves(place_ref, source, near, far):
    mine = pl.multiple_of(place_ref[1] * 512, 512)
    rest = pl.multiple_of((1 - place_ref[1]) * 512, 512)
    near[:, :512] = source[:, pl.ds(mine, 512)]
    far[:, :512] = source[:, pl.ds(rest, 512)]


def first_forward_body(*refs):
    place_ref, arrived = refs[0:2]
    sources = refs[2:14]
    result = refs[14]
    outs = refs[15:19]
    w_gate, w_up, w_down, wide, rows = refs[19:24]
    early, early_far, gate_out, up_out, sems, more = refs[24:]
    waits = fetch(place_ref, 0, sources, (w_gate, w_up, w_down), sems)
    to_matrix(arrived[:, :16, :].reshape(1024, 128).astype(f32), wide, rows)
    halves(place_ref, rows, early, early_far)
    finish(waits[0])
    pre_gate = dot(rows[...], w_gate[...])
    gate_out[...] = pre_gate
    stores = [begin(gate_out, outs[2], more.at[2])]
    finish(waits[1])
    pre_up = dot(rows[...], w_up[...])
    up_out[...] = pre_up
    stores.append(begin(up_out, outs[3], more.at[3]))
    acts = gated(pre_gate, pre_up).astype(bf16)
    early[:, 512:] = acts
    early_far[:, 512:] = acts
    stores.append(begin(early, outs[0], more.at[0]))
    stores.append(begin(early_far, outs[1], more.at[1]))
    finish(waits[2])
    result[...] = to_rows(dot(acts, w_down[...]), wide).reshape(64, 16, 128)
    finish(stores)


def expert_grads(act_grad, pre_gate, pre_up):
    sigma = 1.0 / (1.0 + jnp.exp(-pre_gate))
    gate_grad = (act_grad * pre_up * sigma * (1.0 + pre_gate * (1.0 - sigma))).astype(bf16)
    up_grad = (act_grad * pre_gate * sigma).astype(bf16)
    return (gate_grad, up_grad)


def gain_part(pick_rows, normed_rows):
    product = pick_rows.astype(f32) * normed_rows.astype(f32)
    return jnp.sum(product.reshape(-1, 8, 128), axis=0)


def second_body(*refs):
    place_ref, arrived, cot_ref, early0_ref, early0_far_ref = refs[0:5]
    sources = refs[5:15]
    picked, result, gain_out = refs[15:18]
    outs = refs[18:24]
    w_gate, w_up, w_down, wide, rows, grads, early, early_far = refs[24:32]
    cot, early0, early0_far, late, late_far, sems, more = refs[32:]
    waits = fetch(place_ref, 1, sources, (w_gate, w_up, w_down), sems)
    loads = [
        begin(cot_ref.at[:, 16:32, :], cot, more.at[0]),
        begin(early0_ref, early0, more.at[1]),
        begin(early0_far_ref, early0_far, more.at[2]),
    ]
    normed_rows = arrived[...].reshape(1024, 128)
    to_matrix(normed_rows.astype(f32), wide, rows)
    halves(place_ref, rows, early, early_far)
    finish(loads)
    to_matrix(cot[...].reshape(1024, 128).astype(f32), wide, grads)
    halves(place_ref, grads, late, late_far)
    finish(waits[0])
    pre_gate = dot(rows[...], w_gate[...])
    finish(waits[1])
    pre_up = dot(rows[...], w_up[...])
    acts = gated(pre_gate, pre_up).astype(bf16)
    early[:, 512:] = acts
    early_far[:, 512:] = acts

    def moves(order):
        return [
            pltpu.make_async_copy(source, outs[n], more.at[3 + n])
            for n, source in enumerate(order)
        ]

    @pl.when(place_ref[0] == 0)
    def _():
        for copy in moves((early0, early, early0_far, early_far)):
            copy.start()

    @pl.when(place_ref[0] != 0)
    def _():
        for copy in moves((early, early0, early_far, early0_far)):
            copy.start()

    stores = moves((early0, early, early0_far, early_far))
    finish(waits[2])
    act_grad = dot_nt(grads[...], w_down[...])
    gate_grad, up_grad = expert_grads(act_grad, pre_gate, pre_up)
    for target in (late, late_far):
        target[:, 512:1280] = gate_grad
        target[:, 1280:] = up_grad
    stores.append(begin(late, outs[4], more.at[7]))
    stores.append(begin(late_far, outs[5], more.at[8]))
    pick_rows = to_rows(dot_nt(gate_grad, w_gate[...]) + dot_nt(up_grad, w_up[...]), wide)
    picked[...] = pick_rows.reshape(64, 16, 128)
    gain_out[...] = gain_part(pick_rows, normed_rows)
    result[...] = to_rows(dot(acts, w_down[...]), wide).reshape(64, 16, 128)
    finish(stores)


def first_backward_body(*refs):
    place_ref, gain_second, arrived_ref, normed_ref, gate_ref, up_ref = refs[0:6]
    sources = refs[6:18]
    picked = refs[18]
    outs = refs[19:21]
    w_gate, w_up, w_down, wide, grads = refs[21:26]
    arrived, normed, pre_gate, pre_up, late, late_far, sems, more = refs[26:]
    load = begin(arrived_ref.at[:, 0:16, :], arrived, more.at[0])
    waits = fetch(place_ref, 0, sources, (w_gate, w_up, w_down), sems)
    loads = [
        begin(gate_ref, pre_gate, more.at[1]),
        begin(up_ref, pre_up, more.at[2]),
        begin(normed_ref.at[:, 0:16, :], normed, more.at[3]),
    ]
    load.wait()
    to_matrix(arrived[...].reshape(1024, 128).astype(f32), wide, grads)
    halves(place_ref, grads, late, late_far)
    finish(waits[2])
    act_grad = dot_nt(grads[...], w_down[...])
    finish(loads)
    gate_grad, up_grad = expert_grads(act_grad, pre_gate[...], pre_up[...])
    for target in (late, late_far):
        target[:, 512:1280] = gate_grad
        target[:, 1280:] = up_grad
    stores = [begin(late, outs[0], more.at[4]), begin(late_far, outs[1], more.at[5])]
    finish(waits[0])
    finish(waits[1])
    pick_rows = to_rows(dot_nt(gate_grad, w_gate[...]) + dot_nt(up_grad, w_up[...]), wide)
    picked[:, :16, :] = pick_rows.reshape(64, 16, 128)
    gain_first = gain_part(pick_rows, normed[...].reshape(1024, 128))
    both = jnp.concatenate([gain_first, gain_second[...]], axis=0).astype(bf16)
    picked[:, 16:, :] = jnp.broadcast_to(both[None], (64, 16, 128))
    finish(stores)


def combined(high_t, low_t, rows):
    return dot(high_t[...], rows) + dot(low_t[...], rows)


def between_body(returned, x_ref, gain_ref, high_t, low_t, pick, hidden, out):
    rows = returned[...].reshape(1024, 128)
    result = (x_ref[...].astype(f32) + combined(high_t, low_t, rows)).astype(bf16)
    hidden[...] = result
    out[...] = chunked(dot(pick[...], normalized(result, gain_ref[...])))


def input_gradient(rows, upstream, x_block, gain, pick_t):
    normed_grad = dot(pick_t, rows).reshape(-1, 8, 128)
    values, scaling = token_stats(x_block)
    weighted = normed_grad * gain[None]
    mean = (
        jnp.sum(jnp.sum(weighted * values, axis=2, keepdims=True), axis=1, keepdims=True) / 1024.0
    )
    change = scaling * (weighted - values * scaling * scaling * mean)
    return (upstream.astype(f32) + change.reshape(upstream.shape)).astype(bf16)


def turn_body(returned, result, x_ref, grad_ref, gain_ref, pick_t, high, low, grad_out, out):
    rows = returned[...].reshape(1024, 128)
    grad = input_gradient(rows, grad_ref[...], x_ref[...], gain_ref[...], pick_t[...])
    grad_out[...] = grad
    out[:, :16, :] = chunked(dot(high[...], grad) + dot(low[...], grad))
    out[:, 16:, :] = result[...]


def second_output_body(place_ref, arrived, x_ref, high_t, low_t, hidden, sent):
    rows = arrived[:, 16:, :].reshape(1024, 128)
    before = x_ref[...].astype(f32)
    result = before + combined(high_t, low_t, rows)
    hidden[...] = result.astype(bf16)
    sent[...] = jnp.where(place_ref[0] == 0, result, before).astype(bf16)


def arrange(section, first, second, got, wide, out):
    mine = jnp.where(section == 0, first.astype(f32), second.astype(f32))
    for index, rows in ((section, mine), (1 - section, got)):
        for j, piece in enumerate(token_matrix(rows, wide)):
            out[index, :, 128 * j : 128 * (j + 1)] = piece


def hidden_body(place_ref, first, second, got, out, wide):
    arrange(place_ref[0], first[...], second[...], got[...], wide, out)


def last_body(place_ref, returned, x_ref, grad_ref, gain_ref, pick_t, grad_out, sent, gain_out):
    rows = returned[:, :16, :].reshape(1024, 128)
    grad = input_gradient(rows, grad_ref[...], x_ref[...], gain_ref[...], pick_t[...])
    grad_out[...] = grad
    gain_rows = jnp.sum(returned[:, 16:, :].astype(f32), axis=0)
    sent[:128, :] = jnp.where(place_ref[0] == 0, grad_ref[...].astype(f32), grad.astype(f32))
    sent[128:, :] = gain_rows
    gain_out[...] = gain_rows


def final_body(*refs):
    place_ref, first, second, got = refs[0:4]
    gain_rows, gain_straight, gain_cross, own_gain = refs[4:8]
    out, gain_out, wide = refs[8:]
    arrange(place_ref[0], first[...], second[...], got[:128, :], wide, out)
    total = (gain_rows[...] + got[128:, :]) + (gain_straight[...] + gain_cross[...])
    gain_out[...] = jnp.where(place_ref[0] == 0, total[:8], total[8:]) / own_gain[...]


def weight_body(*refs):
    place_ref = refs[0]
    early_parts, first, second = refs[1:5], refs[5:9], refs[9:13]
    outs = refs[13:16]
    early, late, gate, up, down, sems, out_sems = refs[16:]

    def copies(target, group, row):
        return [
            pltpu.make_async_copy(group[n], target.at[pl.ds(128 * n, 128), :], sems.at[row, n])
            for n in range(4)
        ]

    @pl.when(place_ref[0] == 0)
    def _():
        for copy in copies(late, first, 1):
            copy.start()

    @pl.when(place_ref[0] != 0)
    def _():
        for copy in copies(late, second, 1):
            copy.start()

    for copy in copies(early, early_parts, 0):
        copy.start()
    for copy in copies(early, early_parts, 0) + copies(late, first, 1):
        copy.wait()
    normed = early[:, :512]
    done = []
    for n, target in enumerate((gate, up, down)):
        if n < 2:
            target[...] = dot_tn(normed, late[:, 512 + 768 * n : 1280 + 768 * n])
        else:
            target[...] = dot_tn(early[:, 512:], late[:, :512])
        copy = pltpu.make_async_copy(target, outs[n], out_sems.at[n])
        copy.start()
        done.append(copy)
    for copy in done:
        copy.wait()


def after(block, other):
    return lax.optimization_barrier((block, other))[0]


def window(activations, cotangent, norm_gain, w_gate, w_up, w_down, routes, gate_weights):
    section = lax.axis_index("section")
    part = lax.axis_index("dp")
    experts = lax.axis_size("expert")
    place = jnp.stack([section, part]).astype(jnp.int32)
    micro_count, tokens, width = activations.shape
    swap = [(0, 1), (1, 0)]

    def flat(s, e, d):
        return (s * experts + e) * 2 + d

    def pairs(layer, cross):
        found = []
        for s in range(2):
            target = 1 - s if cross else s
            if layer is None or target == layer:
                found += [
                    (flat(s, e, d), flat(target, e, 1 - d))
                    for e in range(experts)
                    for d in range(2)
                ]
        return found

    def beside(block, route=swap):
        return lax.ppermute(block, "section", route)

    def away(block, layer=None, cross=False):
        return lax.ppermute(block, every, pairs(layer, cross))

    def exchange(block):
        return lax.all_to_all(block, "expert", split_axis=0, concat_axis=0, tiled=True)

    own = (w_gate[0, 0], w_up[0, 0], w_down[0, 0])
    own_gain = norm_gain.reshape(8, 128)
    own_routes = routes[0].transpose(2, 0, 1)
    own_gates = gate_weights[0].transpose(2, 0, 1)
    got_routes = beside(own_routes)
    got_gates = beside(own_gates)
    got_gain = beside(own_gain)
    swapped = tuple(beside(w) for w in own)

    big = ((64, 32, 128), bf16)
    small = ((64, 16, 128), bf16)
    block = ((128, 128), bf16)
    early_shape = ((128, 1280), bf16)
    late_shape = ((128, 2048), bf16)
    down = ((1024, 128), bf16)
    across = ((128, 1024), bf16)
    weight_scratch = [
        pltpu.VMEM((1024, 768), bf16),
        pltpu.VMEM((1024, 768), bf16),
        pltpu.VMEM((768, 1024), bf16),
    ]
    wide = pltpu.VMEM((1024, 128), f32)
    narrow = pltpu.VMEM((128, 128), f32)
    matrix = pltpu.VMEM((128, 1024), bf16)
    sems = pltpu.SemaphoreType.DMA((3, 3))
    early_room = pltpu.VMEM((128, 1280), bf16)
    late_room = pltpu.VMEM((128, 2048), bf16)
    plain_room = pltpu.VMEM((128, 768), f32)
    arrival = pltpu.VMEM((64, 16, 128), bf16)

    out_first, x_first, grad_last, *maps = call(
        start_body,
        [smem] + [vmem] * 8,
        [big, block, block] + [down] * 6,
        [narrow],
        flops=10**8,
        moved=2 * 10**6,
    )(
        place,
        own_routes,
        got_routes,
        own_gates,
        got_gates,
        activations,
        cotangent,
        own_gain,
        got_gain,
    )
    _, high0, low0, pick1, _, _ = maps
    first_gain = jnp.where(section == 0, own_gain, got_gain)
    second_gain = jnp.where(section == 0, got_gain, own_gain)

    def packed(layer, tensors):
        shapes = [((512, 768), bf16), ((384, 512), bf16)][-min(2, len(tensors)) :]
        return call(
            functools.partial(pack_body, layer, tensors),
            [smem] + [anywhere] * (2 * len(tensors)),
            shapes,
            [pltpu.SemaphoreType.DMA((3,))],
            flops=1,
            moved=25 * 10**5,
        )(place, *[own[n] for n in tensors], *[swapped[n] for n in tensors])

    gate_far = away(own[0], 0)
    up_far = away(swapped[1], 1)
    down_far = away(packed(0, (2,))[0])
    portions0 = (
        gate_far,
        beside(gate_far, [(0, 1)]),
        up_far,
        beside(up_far, [(1, 0)]),
        down_far,
        beside(down_far),
    )
    arrived_first = exchange(out_first)

    flipped = call(flip_body, [vmem] * 6, [across] * 6, flops=10**6, moved=3 * 10**6)(*maps)
    pick0_t, high0_t, low0_t, pick1_t, high1_t, low1_t = flipped

    portions1 = [
        away(after(w, other))
        for w, other in zip(packed(1, (0, 1, 2)), (up_far, down_far))
    ]
    portions1 = [w for far in portions1 for w in (far, beside(far))]

    result, early0, early0_far, pre_gate, pre_up = call(
        first_forward_body,
        [smem, vmem] + [anywhere] * 12,
        [small, early_shape, early_shape, ((128, 768), f32), ((128, 768), f32)],
        weight_scratch
        + [wide, matrix, early_room, early_room, plain_room, plain_room, sems]
        + [pltpu.SemaphoreType.DMA((4,))],
        flops=6 * 10**8,
        moved=6 * 10**6,
        out_spec=[vmem] + [anywhere] * 4,
    )(place, arrived_first, *own, *swapped, *portions0)
    returned = exchange(result)

    hidden_first, out_second = call(
        between_body, [vmem] * 6, [block, small], flops=10**8, moved=2 * 10**6
    )(returned, x_first, second_gain, high0_t, low0_t, pick1)
    arrived_second = exchange(out_second)

    picked, result_second, gain_second, kept, sent, straight, cross, late1, late1_far = call(
        second_body,
        [smem, vmem] + [anywhere] * 13,
        [small, small, ((8, 128), f32)] + [early_shape] * 4 + [late_shape] * 2,
        weight_scratch
        + [wide, matrix, matrix, early_room, early_room]
        + [arrival, early_room, early_room, late_room, late_room, sems]
        + [pltpu.SemaphoreType.DMA((9,))],
        flops=12 * 10**8,
        moved=8 * 10**6,
        out_spec=[vmem] * 3 + [anywhere] * 6,
    )(place, arrived_second, arrived_first, early0, early0_far, *own, *swapped, *portions1)
    returned = exchange(picked)

    early_parts = (kept, beside(sent), away(straight), away(cross, cross=True))
    late1_parts = (late1, beside(late1, [(0, 1)]), away(late1_far, 1), away(late1_far, 1, True))

    grad_middle, out_third = call(
        turn_body, [vmem] * 8, [block, big], flops=10**8, moved=2 * 10**6
    )(
        returned,
        result_second,
        hidden_first,
        grad_last,
        second_gain,
        pick1_t,
        high0,
        low0,
    )
    arrived_third = exchange(out_third)

    picked, late0, late0_far = call(
        first_backward_body,
        [smem, vmem] + [anywhere] * 16,
        [big, late_shape, late_shape],
        weight_scratch
        + [wide, matrix, arrival, arrival, plain_room, plain_room, late_room, late_room, sems]
        + [pltpu.SemaphoreType.DMA((6,))],
        flops=6 * 10**8,
        moved=8 * 10**6,
        out_spec=[vmem] + [anywhere] * 2,
    )(
        place,
        gain_second,
        arrived_third,
        arrived_first,
        pre_gate,
        pre_up,
        *own,
        *swapped,
        *portions0,
    )
    late0_parts = (late0, beside(late0, [(1, 0)]), away(late0_far, 0), away(late0_far, 0, True))
    returned = exchange(picked)

    hidden_second, hidden_sent = call(
        second_output_body, [smem] + [vmem] * 4, [block, block], flops=10**8, moved=10**6, grant=16
    )(place, arrived_third, hidden_first, high1_t, low1_t)
    both = ((micro_count, tokens, width), bf16)
    hidden = call(
        hidden_body, [smem] + [vmem] * 3, [both], [narrow], flops=10**5, moved=10**5, grant=16
    )(place, hidden_first, hidden_second, beside(hidden_sent))[0]

    weight_grads = call(
        weight_body,
        [smem] + [anywhere] * 12,
        [((512, 768), f32), ((512, 768), f32), ((768, 512), f32)],
        [
            pltpu.VMEM((512, 1280), bf16),
            pltpu.VMEM((512, 2048), bf16),
            pltpu.VMEM((512, 768), f32),
            pltpu.VMEM((512, 768), f32),
            pltpu.VMEM((768, 512), f32),
            pltpu.SemaphoreType.DMA((2, 4)),
            pltpu.SemaphoreType.DMA((3,)),
        ],
        flops=12 * 10**8,
        moved=8 * 10**6,
        grant=28,
        out_spec=anywhere,
    )(place, *early_parts, *late0_parts, *late1_parts)

    grad_first, grad_sent, gain_rows = call(
        last_body,
        [smem] + [vmem] * 5,
        [block, ((144, 128), f32), ((16, 128), f32)],
        flops=10**8,
        moved=10**6,
        grant=16,
    )(place, returned, x_first, grad_middle, first_gain, pick0_t)
    grads, gain_grad = call(
        final_body,
        [smem] + [vmem] * 7,
        [both, ((8, 128), f32)],
        [narrow],
        flops=10**5,
        moved=10**5,
        grant=16,
    )(
        place,
        grad_first,
        grad_middle,
        beside(grad_sent),
        gain_rows,
        away(gain_rows),
        away(gain_rows, cross=True),
        own_gain,
    )
    return (
        hidden[None],
        grads[None],
        gain_grad.reshape(1, width),
        weight_grads[0][None, None],
        weight_grads[1][None, None],
        weight_grads[2][None, None],
    )


def solution(mesh):
    placed = (
        P(None, ("expert", "dp"), None),
        P(None, ("expert", "dp"), None),
        P("section", None),
        P("section", "expert", "dp", None),
        P("section", "expert", "dp", None),
        P("section", "expert", None, "dp"),
        P("section", None, ("expert", "dp"), None),
        P("section", None, ("expert", "dp"), None),
    )
    return jax.shard_map(
        window,
        mesh=mesh,
        in_specs=placed,
        out_specs=(
            P("section", None, ("expert", "dp"), None),
            P("section", None, ("expert", "dp"), None),
            P("section", None),
            P("section", "expert", "dp", None),
            P("section", "expert", "dp", None),
            P("section", "expert", None, "dp"),
        ),
        check_vma=False,
    )
```

```python
import functools
import jax
import jax.numpy as jnp
from jax import lax
from jax.experimental import pallas as pl
from jax.experimental.pallas import tpu as pltpu
from jax.sharding import PartitionSpec as P

epsilon = 1e-06
f32 = jnp.float32
bf16 = jnp.bfloat16
every = ("section", "expert", "dp")
vmem = pl.BlockSpec(memory_space=pltpu.VMEM)
smem = pl.BlockSpec(memory_space=pltpu.SMEM)
anywhere = pl.BlockSpec(memory_space=pl.ANY)
hbm = pl.BlockSpec(memory_space=pltpu.HBM)


def dot(left, right):
    return jnp.dot(left, right, preferred_element_type=f32)


def dot_nt(left, right):
    return lax.dot_general(left, right, (((1,), (1,)), ((), ())), preferred_element_type=f32)


def dot_tn(left, right):
    return lax.dot_general(left, right, (((0,), (0,)), ((), ())), preferred_element_type=f32)


def call(body, in_specs, outs, scratch=(), flops=0, moved=0, grant=None, out_spec=vmem):
    return pl.pallas_call(
        body,
        in_specs=in_specs,
        out_shape=[jax.ShapeDtypeStruct(shape, dtype) for shape, dtype in outs],
        out_specs=out_spec if isinstance(out_spec, list) else [out_spec] * len(outs),
        scratch_shapes=list(scratch),
        cost_estimate=pl.CostEstimate(flops=flops, bytes_accessed=moved, transcendentals=0),
        compiler_params=pltpu.CompilerParams(vmem_limit_bytes=grant and grant * 2**20),
    )


def begin(source, target, sem):
    copy = pltpu.make_async_copy(source, target, sem)
    copy.start()
    return copy


def finish(group):
    for copy in group:
        copy.wait()


def staged_body(body, loaded, inputs, outputs, *refs):
    ins = list(refs[:inputs])
    outs = refs[inputs : inputs + outputs]
    rooms = refs[inputs + outputs : 2 * inputs + 2 * outputs - loaded]
    rest, sems = refs[2 * inputs + 2 * outputs - loaded : -1], refs[-1]
    copies = []
    for n in range(loaded, inputs):
        copies.append(begin(ins[n], rooms[n - loaded], sems.at[n - loaded]))
        ins[n] = rooms[n - loaded]
    results = rooms[inputs - loaded :]
    finish(copies)
    body(*ins, *results, *rest)
    finish(
        [
            begin(source, target, sems.at[inputs - loaded + n])
            for n, (source, target) in enumerate(zip(results, outs))
        ]
    )


def staged(body, in_specs, outs, arrays, scratch=()):
    loaded = len(in_specs)
    rooms = [pltpu.VMEM(array.shape, array.dtype) for array in arrays[loaded:]]
    rooms += [pltpu.VMEM(shape, dtype) for shape, dtype in outs]
    return call(
        functools.partial(staged_body, body, loaded, len(arrays), len(outs)),
        list(in_specs) + [hbm] * (len(arrays) - loaded),
        outs,
        rooms + list(scratch) + [pltpu.SemaphoreType.DMA((len(rooms),))],
        flops=10**8,
        moved=2 * 10**6,
        out_spec=hbm,
    )(*arrays)


def token_rows(block, wide):
    values = block.astype(f32)
    for j in range(8):
        wide[pl.ds(j, 16, stride=8), :] = values[:, 128 * j : 128 * (j + 1)]
    return wide[...].astype(bf16)


def token_matrix(rows, wide):
    wide[...] = rows.astype(f32)
    return [wide[pl.ds(j, 16, stride=8), :].astype(bf16) for j in range(8)]


def token_stats(block):
    values = block.astype(f32).reshape(-1, 8, 128)
    mean = jnp.sum(jnp.sum(values * values, axis=2, keepdims=True), axis=1, keepdims=True) / 1024.0
    return (values, lax.rsqrt(mean + epsilon))


def normalized(block, gain):
    values, scaling = token_stats(block)
    return (values * scaling * gain[None]).astype(bf16).reshape(block.shape)


def chunked(rows):
    return rows.astype(bf16).reshape(64, -1, 128)


def fill_tables(ids, gates, pick, high, low):
    token = lax.broadcasted_iota(jnp.int32, (16, 128), 0)
    lane = lax.broadcasted_iota(jnp.int32, (16, 128), 1)
    spread = jnp.where(lax.shift_right_logical(lane, 3) == token, 1.0, 0.0).astype(bf16)
    names = dot(ids.astype(f32).astype(bf16), spread)
    gates_high = gates.astype(bf16)
    gates_low = (gates - gates_high.astype(f32)).astype(bf16)
    upper = dot(gates_high, spread)
    lower = dot(gates_low, spread)
    expert = lax.broadcasted_iota(jnp.int32, (64, 128), 0).astype(f32)
    named = jnp.zeros((64, 128), f32)
    first = jnp.zeros((64, 128), f32)
    second = jnp.zeros((64, 128), f32)
    for k in range(ids.shape[0]):
        match = expert == names[k : k + 1, :]
        named = jnp.where(match, 1.0, named)
        first = jnp.where(match, upper[k : k + 1, :], first)
        second = jnp.where(match, lower[k : k + 1, :], second)
    row = lax.broadcasted_iota(jnp.int32, (128, 128), 0)
    column = lax.broadcasted_iota(jnp.int32, (128, 128), 1)
    earlier = ((row & 7) == 0) & (
        lax.shift_right_logical(row, 3) < lax.shift_right_logical(column, 3)
    )
    before = dot(named.astype(bf16), jnp.where(earlier, 1.0, 0.0).astype(bf16))
    code = jnp.where(named > 0.0, before + 1.0, 0.0)
    slot_row = lax.broadcasted_iota(jnp.int32, (1, 16, 128), 1)
    slot_lane = lax.broadcasted_iota(jnp.int32, (1, 16, 128), 2)
    wanted = lax.shift_right_logical(slot_row, 3).astype(f32) + 1.0
    wanted = jnp.where((slot_row & 7) == (slot_lane & 7), wanted, 9.0)
    shape = (64, 16, 128)
    match = jnp.broadcast_to(code[:, None, :], shape) == jnp.broadcast_to(wanted, shape)
    zero = jnp.zeros(shape, f32)
    pick[...] = jnp.where(match, 1.0, zero).astype(bf16).reshape(1024, 128)
    first = jnp.broadcast_to(first[:, None, :], shape)
    high[...] = jnp.where(match, first, zero).astype(bf16).reshape(1024, 128)
    second = jnp.broadcast_to(second[:, None, :], shape)
    low[...] = jnp.where(match, second, zero).astype(bf16).reshape(1024, 128)


def start_body(*refs):
    place_ref, own_routes, got_routes, own_gates, got_gates = refs[0:5]
    x_ref, grad_ref, own_gain, got_gain = refs[5:9]
    out, x_rows, grad_rows = refs[9:12]
    pick0, high0, low0, pick1, high1, low1 = refs[12:18]
    wide = refs[18]
    section = place_ref[0]
    ids = (own_routes[:, section, :], got_routes[:, section, :])
    gates = (own_gates[:, section, :], got_gates[:, section, :])
    lower = section == 0
    fill_tables(
        jnp.where(lower, ids[0], ids[1]),
        jnp.where(lower, gates[0], gates[1]),
        pick0,
        high0,
        low0,
    )
    fill_tables(
        jnp.where(lower, ids[1], ids[0]),
        jnp.where(lower, gates[1], gates[0]),
        pick1,
        high1,
        low1,
    )
    x_block = token_rows(x_ref[section], wide)
    x_rows[...] = x_block
    gain = jnp.where(lower, own_gain[...], got_gain[...])
    out[:, :16, :] = chunked(dot(pick0[...], normalized(x_block, gain)))
    grad = token_rows(grad_ref[section], wide)
    grad_rows[...] = grad
    out[:, 16:, :] = chunked(dot(high1[...], grad) + dot(low1[...], grad))


def flip_body(*refs):
    for source, target in zip(refs[:6], refs[6:]):
        target[...] = source[...].astype(f32).T.astype(bf16)


def pack_body(layer, tensors, *refs):
    place_ref = refs[0]
    own, swapped = refs[1 : 1 + len(tensors)], refs[1 + len(tensors) : 1 + 2 * len(tensors)]
    outs, sems = refs[1 + 2 * len(tensors) : -1], refs[-1]
    section = place_ref[0]
    start = pl.multiple_of(section * 256, 256)
    start_down = pl.multiple_of(section * 384, 128)

    def copies(group):
        found = []
        for n, ref in zip(tensors, group):
            if n < 2:
                source, target = ref.at[pl.ds(start, 256), :], outs[0].at[256 * n : 256 * n + 256, :]
            else:
                source, target = ref.at[pl.ds(start_down, 384), :], outs[-1]
            found.append(pltpu.make_async_copy(source, target, sems.at[n]))
        return found

    @pl.when(section == layer)
    def _():
        for copy in copies(own):
            copy.start()

    @pl.when(section != layer)
    def _():
        for copy in copies(swapped):
            copy.start()

    for copy in copies(own):
        copy.wait()


def to_matrix(rows, wide, target):
    wide[...] = rows
    slots = rows.shape[0] // 8
    for j in range(8):
        target[:, 128 * j : 128 * (j + 1)] = wide[pl.ds(j, slots, stride=8), :].astype(bf16)


def to_rows(matrix, wide):
    slots = matrix.shape[0]
    for j in range(8):
        wide[pl.ds(j, slots, stride=8), :] = matrix[:, 128 * j : 128 * (j + 1)]
    return wide[...].astype(bf16)


def fetch(place_ref, layer, sources, targets, sems, order=(0, 1, 2)):
    own, swapped = sources[0:3], sources[3:6]
    section, part = place_ref[0], place_ref[1]
    mine = pl.multiple_of(part * 512, 512)
    rest = pl.multiple_of((1 - part) * 512, 512)

    def near(group, others):
        found = []
        for n in range(3):
            copies = []
            for h, (sources_now, start) in enumerate(((group, mine), (others, rest))):
                if sources_now:
                    if n < 2:
                        target = targets[n].at[pl.ds(start, 512), :]
                    else:
                        target = targets[n].at[:, pl.ds(start, 512)]
                    copies.append(pltpu.make_async_copy(sources_now[n], target, sems.at[n, h]))
            found.append(copies)
        return found

    def far(n):
        found = []
        for p in range(2):
            index = section if p == 0 else 1 - section
            if n < 2:
                start = pl.multiple_of(rest + index * 256, 256)
                source = sources[6 + p].at[256 * n : 256 * (n + 1), :]
                target = targets[n].at[pl.ds(start, 256), :]
            else:
                start = pl.multiple_of(index * 384, 128)
                source = sources[8 + p]
                target = targets[n].at[pl.ds(start, 384), pl.ds(rest, 512)]
            found.append(pltpu.make_async_copy(source, target, sems.at[n, 1 + p]))
        return found

    if layer == 0:
        gate, gate_passed, up, up_passed, down, down_passed = sources[6:12]
        lower, upper = (gate, up_passed, down), (gate_passed, up, down_passed)
        others = [[], [], []]
    else:
        lower, upper = (), ()
        others = [far(0), far(1), far(2)]

    @pl.when(section == 0)
    def _():
        groups = near(own if layer == 0 else swapped, lower)
        for n in order:
            for copy in groups[n]:
                copy.start()

    @pl.when(section != 0)
    def _():
        groups = near(swapped if layer == 0 else own, upper)
        for n in order:
            for copy in groups[n]:
                copy.start()

    for n in order:
        for copy in others[n]:
            copy.start()
    return [first + second for first, second in zip(near(own, lower), others)]


def gated(pre_gate, pre_up):
    return pre_gate / (1.0 + jnp.exp(-pre_gate)) * pre_up


def halves(place_ref, source, near, far):
    mine = pl.multiple_of(place_ref[1] * 512, 512)
    rest = pl.multiple_of((1 - place_ref[1]) * 512, 512)
    near[:, :512] = source[:, pl.ds(mine, 512)]
    far[:, :512] = source[:, pl.ds(rest, 512)]


def first_forward_body(*refs):
    place_ref, arrived_ref = refs[0:2]
    sources = refs[2:14]
    outs = refs[14:19]
    w_gate, w_up, w_down, wide, rows = refs[19:24]
    early, early_far, gate_out, up_out, arrived, result, sems, more = refs[24:]
    load = begin(arrived_ref.at[:, 0:16, :], arrived, more.at[4])
    waits = fetch(place_ref, 0, sources, (w_gate, w_up, w_down), sems)
    load.wait()
    to_matrix(arrived[...].reshape(1024, 128).astype(f32), wide, rows)
    halves(place_ref, rows, early, early_far)
    finish(waits[0])
    pre_gate = dot(rows[...], w_gate[...])
    gate_out[...] = pre_gate
    stores = [begin(gate_out, outs[3], more.at[2])]
    finish(waits[1])
    pre_up = dot(rows[...], w_up[...])
    up_out[...] = pre_up
    stores.append(begin(up_out, outs[4], more.at[3]))
    acts = gated(pre_gate, pre_up).astype(bf16)
    early[:, 512:] = acts
    early_far[:, 512:] = acts
    stores.append(begin(early, outs[1], more.at[0]))
    stores.append(begin(early_far, outs[2], more.at[1]))
    finish(waits[2])
    result[...] = to_rows(dot(acts, w_down[...]), wide).reshape(64, 16, 128)
    stores.append(begin(result, outs[0], more.at[5]))
    finish(stores)


def expert_grads(act_grad, pre_gate, pre_up):
    sigma = 1.0 / (1.0 + jnp.exp(-pre_gate))
    gate_grad = (act_grad * pre_up * sigma * (1.0 + pre_gate * (1.0 - sigma))).astype(bf16)
    up_grad = (act_grad * pre_gate * sigma).astype(bf16)
    return (gate_grad, up_grad)


def gain_part(pick_rows, normed_rows):
    product = pick_rows.astype(f32) * normed_rows.astype(f32)
    return jnp.sum(product.reshape(-1, 8, 128), axis=0)


def second_body(*refs):
    place_ref, arrived, cot_ref, early0_ref, early0_far_ref = refs[0:5]
    sources = refs[5:15]
    ends = refs[15:18]
    outs = refs[18:24]
    w_gate, w_up, w_down, wide, rows, grads, early, early_far = refs[24:32]
    cot, early0, early0_far, late, late_far, picked, result, gain_out, sems, more = refs[32:]
    waits = fetch(place_ref, 1, sources, (w_gate, w_up, w_down), sems)
    loads = [
        begin(cot_ref.at[:, 16:32, :], cot, more.at[0]),
        begin(early0_ref, early0, more.at[1]),
        begin(early0_far_ref, early0_far, more.at[2]),
    ]
    normed_rows = arrived[...].reshape(1024, 128)
    to_matrix(normed_rows.astype(f32), wide, rows)
    halves(place_ref, rows, early, early_far)
    finish(loads)
    to_matrix(cot[...].reshape(1024, 128).astype(f32), wide, grads)
    halves(place_ref, grads, late, late_far)
    finish(waits[0])
    pre_gate = dot(rows[...], w_gate[...])
    finish(waits[1])
    pre_up = dot(rows[...], w_up[...])
    acts = gated(pre_gate, pre_up).astype(bf16)
    early[:, 512:] = acts
    early_far[:, 512:] = acts

    def moves(order):
        return [
            pltpu.make_async_copy(source, outs[n], more.at[3 + n])
            for n, source in enumerate(order)
        ]

    @pl.when(place_ref[0] == 0)
    def _():
        for copy in moves((early0, early, early0_far, early_far)):
            copy.start()

    @pl.when(place_ref[0] != 0)
    def _():
        for copy in moves((early, early0, early_far, early0_far)):
            copy.start()

    stores = moves((early0, early, early0_far, early_far))
    finish(waits[2])
    act_grad = dot_nt(grads[...], w_down[...])
    gate_grad, up_grad = expert_grads(act_grad, pre_gate, pre_up)
    for target in (late, late_far):
        target[:, 512:1280] = gate_grad
        target[:, 1280:] = up_grad
    stores.append(begin(late, outs[4], more.at[7]))
    stores.append(begin(late_far, outs[5], more.at[8]))
    pick_rows = to_rows(dot_nt(gate_grad, w_gate[...]) + dot_nt(up_grad, w_up[...]), wide)
    picked[...] = pick_rows.reshape(64, 16, 128)
    stores.append(begin(picked, ends[0], more.at[9]))
    gain_out[...] = gain_part(pick_rows, normed_rows)
    stores.append(begin(gain_out, ends[2], more.at[10]))
    result[...] = to_rows(dot(acts, w_down[...]), wide).reshape(64, 16, 128)
    stores.append(begin(result, ends[1], more.at[11]))
    finish(stores)


def first_backward_body(*refs):
    place_ref, gain_second, arrived_ref, normed_ref, gate_ref, up_ref = refs[0:6]
    sources = refs[6:18]
    outs = refs[18:21]
    w_gate, w_up, w_down, wide, grads = refs[21:26]
    arrived, normed, pre_gate, pre_up, late, late_far, picked, sems, more = refs[26:]
    load = begin(arrived_ref.at[:, 0:16, :], arrived, more.at[0])
    waits = fetch(place_ref, 0, sources, (w_gate, w_up, w_down), sems, (2, 0, 1))
    loads = [
        begin(gate_ref, pre_gate, more.at[1]),
        begin(up_ref, pre_up, more.at[2]),
        begin(normed_ref.at[:, 0:16, :], normed, more.at[3]),
    ]
    load.wait()
    to_matrix(arrived[...].reshape(1024, 128).astype(f32), wide, grads)
    halves(place_ref, grads, late, late_far)
    finish(waits[2])
    act_grad = dot_nt(grads[...], w_down[...])
    finish(loads)
    gate_grad, up_grad = expert_grads(act_grad, pre_gate[...], pre_up[...])
    for target in (late, late_far):
        target[:, 512:1280] = gate_grad
        target[:, 1280:] = up_grad
    stores = [begin(late, outs[1], more.at[4]), begin(late_far, outs[2], more.at[5])]
    finish(waits[0])
    finish(waits[1])
    pick_rows = to_rows(dot_nt(gate_grad, w_gate[...]) + dot_nt(up_grad, w_up[...]), wide)
    picked[:, :16, :] = pick_rows.reshape(64, 16, 128)
    gain_first = gain_part(pick_rows, normed[...].reshape(1024, 128))
    both = jnp.concatenate([gain_first, gain_second[...]], axis=0).astype(bf16)
    picked[:, 16:, :] = jnp.broadcast_to(both[None], (64, 16, 128))
    stores.append(begin(picked, outs[0], more.at[6]))
    finish(stores)


def combined(high_t, low_t, rows):
    return dot(high_t[...], rows) + dot(low_t[...], rows)


def between_body(returned, x_ref, gain_ref, high_t, low_t, pick, hidden, out):
    rows = returned[...].reshape(1024, 128)
    result = (x_ref[...].astype(f32) + combined(high_t, low_t, rows)).astype(bf16)
    hidden[...] = result
    out[...] = chunked(dot(pick[...], normalized(result, gain_ref[...])))


def input_gradient(rows, upstream, x_block, gain, pick_t):
    normed_grad = dot(pick_t, rows).reshape(-1, 8, 128)
    values, scaling = token_stats(x_block)
    weighted = normed_grad * gain[None]
    mean = (
        jnp.sum(jnp.sum(weighted * values, axis=2, keepdims=True), axis=1, keepdims=True) / 1024.0
    )
    change = scaling * (weighted - values * scaling * scaling * mean)
    return (upstream.astype(f32) + change.reshape(upstream.shape)).astype(bf16)


def turn_body(returned, result, x_ref, grad_ref, gain_ref, pick_t, high, low, grad_out, out):
    rows = returned[...].reshape(1024, 128)
    grad = input_gradient(rows, grad_ref[...], x_ref[...], gain_ref[...], pick_t[...])
    grad_out[...] = grad
    out[:, :16, :] = chunked(dot(high[...], grad) + dot(low[...], grad))
    out[:, 16:, :] = result[...]


def second_output_body(place_ref, arrived, x_ref, high_t, low_t, hidden, sent):
    rows = arrived[:, 16:, :].reshape(1024, 128)
    before = x_ref[...].astype(f32)
    result = before + combined(high_t, low_t, rows)
    hidden[...] = result.astype(bf16)
    sent[...] = jnp.where(place_ref[0] == 0, result, before).astype(bf16)


def arrange(section, first, second, got, wide, out):
    mine = jnp.where(section == 0, first.astype(f32), second.astype(f32))
    for index, rows in ((section, mine), (1 - section, got)):
        for j, piece in enumerate(token_matrix(rows, wide)):
            out[index, :, 128 * j : 128 * (j + 1)] = piece


def hidden_body(place_ref, first, second, got, out, wide):
    arrange(place_ref[0], first[...], second[...], got[...], wide, out)


def last_body(*refs):
    place_ref, returned = refs[0:2]
    grad_out, sent, gain_out = refs[6:9]
    x_ref, grad_ref, gain_ref, pick_t, sems = refs[9:]
    finish([begin(refs[2 + n], refs[9 + n], sems.at[n]) for n in range(4)])
    rows = returned[:, :16, :].reshape(1024, 128)
    grad = input_gradient(rows, grad_ref[...], x_ref[...], gain_ref[...], pick_t[...])
    grad_out[...] = grad
    gain_rows = jnp.sum(returned[:, 16:, :].astype(f32), axis=0)
    sent[:128, :] = jnp.where(place_ref[0] == 0, grad_ref[...].astype(f32), grad.astype(f32))
    sent[128:, :] = gain_rows
    gain_out[...] = gain_rows


def final_body(*refs):
    place_ref, first, second, got = refs[0:4]
    gain_rows, gain_straight, gain_cross, own_gain = refs[4:8]
    out, gain_out, wide = refs[8:]
    arrange(place_ref[0], first[...], second[...], got[:128, :], wide, out)
    total = (gain_rows[...] + got[128:, :]) + (gain_straight[...] + gain_cross[...])
    gain_out[...] = jnp.where(place_ref[0] == 0, total[:8], total[8:]) / own_gain[...]


def weight_body(*refs):
    place_ref = refs[0]
    early_parts, first, second = refs[1:5], refs[5:9], refs[9:13]
    outs = refs[13:16]
    early, late, gate, up, down, sems, out_sems = refs[16:]

    def copies(target, group, row):
        return [
            pltpu.make_async_copy(group[n], target.at[pl.ds(128 * n, 128), :], sems.at[row, n])
            for n in range(4)
        ]

    @pl.when(place_ref[0] == 0)
    def _():
        for copy in copies(late, first, 1):
            copy.start()

    @pl.when(place_ref[0] != 0)
    def _():
        for copy in copies(late, second, 1):
            copy.start()

    for copy in copies(early, early_parts, 0):
        copy.start()
    for copy in copies(early, early_parts, 0) + copies(late, first, 1):
        copy.wait()
    normed = early[:, :512]
    done = []
    for n, target in enumerate((gate, up, down)):
        if n < 2:
            target[...] = dot_tn(normed, late[:, 512 + 768 * n : 1280 + 768 * n])
        else:
            target[...] = dot_tn(early[:, 512:], late[:, :512])
        copy = pltpu.make_async_copy(target, outs[n], out_sems.at[n])
        copy.start()
        done.append(copy)
    for copy in done:
        copy.wait()


def after(block, other):
    return lax.optimization_barrier((block, other))[0]


def window(activations, cotangent, norm_gain, w_gate, w_up, w_down, routes, gate_weights):
    section = lax.axis_index("section")
    part = lax.axis_index("dp")
    experts = lax.axis_size("expert")
    place = jnp.stack([section, part]).astype(jnp.int32)
    micro_count, tokens, width = activations.shape
    swap = [(0, 1), (1, 0)]

    def flat(s, e, d):
        return (s * experts + e) * 2 + d

    def pairs(layer, cross):
        found = []
        for s in range(2):
            target = 1 - s if cross else s
            if layer is None or target == layer:
                found += [
                    (flat(s, e, d), flat(target, e, 1 - d))
                    for e in range(experts)
                    for d in range(2)
                ]
        return found

    def beside(block, route=swap):
        return lax.ppermute(block, "section", route)

    def away(block, layer=None, cross=False):
        return lax.ppermute(block, every, pairs(layer, cross))

    def exchange(block):
        return lax.all_to_all(block, "expert", split_axis=0, concat_axis=0, tiled=True)

    own = (w_gate[0, 0], w_up[0, 0], w_down[0, 0])
    own_gain = norm_gain.reshape(8, 128)
    own_routes = routes[0].transpose(2, 0, 1)
    own_gates = gate_weights[0].transpose(2, 0, 1)
    got_routes = beside(own_routes)
    got_gates = beside(own_gates)
    got_gain = beside(own_gain)
    swapped = tuple(beside(w) for w in own)

    big = ((64, 32, 128), bf16)
    small = ((64, 16, 128), bf16)
    block = ((128, 128), bf16)
    early_shape = ((128, 1280), bf16)
    late_shape = ((128, 2048), bf16)
    down = ((1024, 128), bf16)
    across = ((128, 1024), bf16)
    weight_scratch = [
        pltpu.VMEM((1024, 768), bf16),
        pltpu.VMEM((1024, 768), bf16),
        pltpu.VMEM((768, 1024), bf16),
    ]
    wide = pltpu.VMEM((1024, 128), f32)
    narrow = pltpu.VMEM((128, 128), f32)
    matrix = pltpu.VMEM((128, 1024), bf16)
    sems = pltpu.SemaphoreType.DMA((3, 3))
    early_room = pltpu.VMEM((128, 1280), bf16)
    late_room = pltpu.VMEM((128, 2048), bf16)
    plain_room = pltpu.VMEM((128, 768), f32)
    arrival = pltpu.VMEM((64, 16, 128), bf16)

    out_first, x_first, grad_last, *maps = staged(
        start_body,
        [smem] + [vmem] * 8,
        [big, block, block] + [down] * 6,
        [place, own_routes, got_routes, own_gates, got_gates]
        + [activations, cotangent, own_gain, got_gain],
        [narrow],
    )
    _, high0, low0, pick1, _, _ = maps
    first_gain = jnp.where(section == 0, own_gain, got_gain)
    second_gain = jnp.where(section == 0, got_gain, own_gain)

    def packed(layer, tensors):
        shapes = [((512, 768), bf16), ((384, 512), bf16)][-min(2, len(tensors)) :]
        return call(
            functools.partial(pack_body, layer, tensors),
            [smem] + [anywhere] * (2 * len(tensors)),
            shapes,
            [pltpu.SemaphoreType.DMA((3,))],
            flops=1,
            moved=25 * 10**5,
        )(place, *[own[n] for n in tensors], *[swapped[n] for n in tensors])

    gate_far = away(own[0], 0)
    up_far = away(swapped[1], 1)
    down_far = away(own[2], 0)
    portions0 = (
        gate_far,
        beside(gate_far, [(0, 1)]),
        up_far,
        beside(up_far, [(1, 0)]),
        down_far,
        beside(down_far, [(0, 1)]),
    )
    arrived_first = exchange(out_first)

    flipped = call(flip_body, [vmem] * 6, [across] * 6, flops=10**6, moved=3 * 10**6)(*maps)
    pick0_t, high0_t, low0_t, pick1_t, high1_t, low1_t = flipped

    portions1 = [
        away(after(w, other))
        for w, other in zip(packed(1, (0, 1, 2)), (up_far, down_far))
    ]
    portions1 = [w for far in portions1 for w in (far, beside(far))]

    result, early0, early0_far, pre_gate, pre_up = call(
        first_forward_body,
        [smem] + [hbm] * 13,
        [small, early_shape, early_shape, ((128, 768), f32), ((128, 768), f32)],
        weight_scratch
        + [wide, matrix, early_room, early_room, plain_room, plain_room, arrival, arrival, sems]
        + [pltpu.SemaphoreType.DMA((6,))],
        flops=6 * 10**8,
        moved=6 * 10**6,
        out_spec=hbm,
    )(place, arrived_first, *own, *swapped, *portions0)
    returned = exchange(result)

    hidden_first, out_second = staged(
        between_body,
        [vmem],
        [block, small],
        [returned, x_first, second_gain, high0_t, low0_t, pick1],
    )
    arrived_second = exchange(out_second)

    picked, result_second, gain_second, kept, sent, straight, cross, late1, late1_far = call(
        second_body,
        [smem, vmem] + [hbm] * 13,
        [small, small, ((8, 128), f32)] + [early_shape] * 4 + [late_shape] * 2,
        weight_scratch
        + [wide, matrix, matrix, early_room, early_room]
        + [arrival, early_room, early_room, late_room, late_room, arrival, arrival]
        + [pltpu.VMEM((8, 128), f32), sems, pltpu.SemaphoreType.DMA((12,))],
        flops=12 * 10**8,
        moved=8 * 10**6,
        out_spec=hbm,
    )(place, arrived_second, arrived_first, early0, early0_far, *own, *swapped, *portions1)
    returned = exchange(picked)

    early_parts = (kept, beside(sent), away(straight), away(cross, cross=True))
    late1_parts = (late1, beside(late1, [(0, 1)]), away(late1_far, 1), away(late1_far, 1, True))

    grad_middle, out_third = staged(
        turn_body,
        [vmem],
        [block, big],
        [returned, result_second, hidden_first, grad_last, second_gain, pick1_t, high0, low0],
    )
    arrived_third = exchange(out_third)

    picked, late0, late0_far = call(
        first_backward_body,
        [smem, vmem] + [hbm] * 16,
        [big, late_shape, late_shape],
        weight_scratch
        + [wide, matrix, arrival, arrival, plain_room, plain_room, late_room, late_room]
        + [pltpu.VMEM((64, 32, 128), bf16), sems, pltpu.SemaphoreType.DMA((7,))],
        flops=6 * 10**8,
        moved=8 * 10**6,
        out_spec=hbm,
    )(
        place,
        gain_second,
        arrived_third,
        arrived_first,
        pre_gate,
        pre_up,
        *own,
        *swapped,
        *portions0,
    )
    late0_parts = (late0, beside(late0, [(1, 0)]), away(late0_far, 0), away(late0_far, 0, True))
    returned = exchange(picked)

    hidden_second, hidden_sent = call(
        second_output_body, [smem] + [vmem] * 4, [block, block], flops=10**8, moved=10**6, grant=16
    )(place, arrived_third, hidden_first, high1_t, low1_t)
    both = ((micro_count, tokens, width), bf16)
    hidden = call(
        hidden_body, [smem] + [vmem] * 3, [both], [narrow], flops=10**5, moved=10**5, grant=16
    )(place, hidden_first, hidden_second, beside(hidden_sent))[0]

    weight_grads = call(
        weight_body,
        [smem] + [anywhere] * 12,
        [((512, 768), f32), ((512, 768), f32), ((768, 512), f32)],
        [
            pltpu.VMEM((512, 1280), bf16),
            pltpu.VMEM((512, 2048), bf16),
            pltpu.VMEM((512, 768), f32),
            pltpu.VMEM((512, 768), f32),
            pltpu.VMEM((768, 512), f32),
            pltpu.SemaphoreType.DMA((2, 4)),
            pltpu.SemaphoreType.DMA((3,)),
        ],
        flops=12 * 10**8,
        moved=8 * 10**6,
        grant=28,
        out_spec=anywhere,
    )(place, *early_parts, *late0_parts, *late1_parts)

    grad_first, grad_sent, gain_rows = call(
        last_body,
        [smem, vmem] + [hbm] * 4,
        [block, ((144, 128), f32), ((16, 128), f32)],
        [
            pltpu.VMEM((128, 128), bf16),
            pltpu.VMEM((128, 128), bf16),
            pltpu.VMEM((8, 128), f32),
            matrix,
            pltpu.SemaphoreType.DMA((4,)),
        ],
        flops=10**8,
        moved=10**6,
        grant=16,
    )(place, returned, x_first, grad_middle, first_gain, pick0_t)
    grads, gain_grad = call(
        final_body,
        [smem] + [vmem] * 7,
        [both, ((8, 128), f32)],
        [narrow],
        flops=10**5,
        moved=10**5,
        grant=16,
    )(
        place,
        grad_first,
        grad_middle,
        beside(grad_sent),
        gain_rows,
        away(gain_rows),
        away(gain_rows, cross=True),
        own_gain,
    )
    return (
        hidden[None],
        grads[None],
        gain_grad.reshape(1, width),
        weight_grads[0][None, None],
        weight_grads[1][None, None],
        weight_grads[2][None, None],
    )


def solution(mesh):
    placed = (
        P(None, ("expert", "dp"), None),
        P(None, ("expert", "dp"), None),
        P("section", None),
        P("section", "expert", "dp", None),
        P("section", "expert", "dp", None),
        P("section", "expert", None, "dp"),
        P("section", None, ("expert", "dp"), None),
        P("section", None, ("expert", "dp"), None),
    )
    return jax.shard_map(
        window,
        mesh=mesh,
        in_specs=placed,
        out_specs=(
            P("section", None, ("expert", "dp"), None),
            P("section", None, ("expert", "dp"), None),
            P("section", None),
            P("section", "expert", "dp", None),
            P("section", "expert", "dp", None),
            P("section", "expert", None, "dp"),
        ),
        check_vma=False,
    )
```

```python
import functools
import jax
import jax.numpy as jnp
from jax import lax
from jax.experimental import pallas as pl
from jax.experimental.pallas import tpu as pltpu
from jax.sharding import PartitionSpec as P

epsilon = 1e-06
f32 = jnp.float32
bf16 = jnp.bfloat16
every = ("section", "expert", "dp")
vmem = pl.BlockSpec(memory_space=pltpu.VMEM)
smem = pl.BlockSpec(memory_space=pltpu.SMEM)
anywhere = pl.BlockSpec(memory_space=pl.ANY)
hbm = pl.BlockSpec(memory_space=pltpu.HBM)


def dot(left, right):
    return jnp.dot(left, right, preferred_element_type=f32)


def dot_nt(left, right):
    return lax.dot_general(left, right, (((1,), (1,)), ((), ())), preferred_element_type=f32)


def dot_tn(left, right):
    return lax.dot_general(left, right, (((0,), (0,)), ((), ())), preferred_element_type=f32)


def call(body, in_specs, outs, scratch=(), flops=0, moved=0, grant=None, out_spec=vmem):
    return pl.pallas_call(
        body,
        in_specs=in_specs,
        out_shape=[jax.ShapeDtypeStruct(shape, dtype) for shape, dtype in outs],
        out_specs=out_spec if isinstance(out_spec, list) else [out_spec] * len(outs),
        scratch_shapes=list(scratch),
        cost_estimate=pl.CostEstimate(flops=flops, bytes_accessed=moved, transcendentals=0),
        compiler_params=pltpu.CompilerParams(vmem_limit_bytes=grant and grant * 2**20),
    )


def begin(source, target, sem):
    copy = pltpu.make_async_copy(source, target, sem)
    copy.start()
    return copy


def finish(group):
    for copy in group:
        copy.wait()


def plain(body, in_specs, outs, arrays, scratch=()):
    specs = list(in_specs) + [vmem] * (len(arrays) - len(in_specs))
    return call(body, specs, outs, scratch, flops=10**8, moved=2 * 10**6)(*arrays)


def token_rows(block, wide):
    values = block.astype(f32)
    for j in range(8):
        wide[pl.ds(j, 16, stride=8), :] = values[:, 128 * j : 128 * (j + 1)]
    return wide[...].astype(bf16)


def token_matrix(rows, wide):
    wide[...] = rows.astype(f32)
    return [wide[pl.ds(j, 16, stride=8), :].astype(bf16) for j in range(8)]


def token_stats(block):
    values = block.astype(f32).reshape(-1, 8, 128)
    mean = jnp.sum(jnp.sum(values * values, axis=2, keepdims=True), axis=1, keepdims=True) / 1024.0
    return (values, lax.rsqrt(mean + epsilon))


def normalized(block, gain):
    values, scaling = token_stats(block)
    return (values * scaling * gain[None]).astype(bf16).reshape(block.shape)


def chunked(rows):
    return rows.astype(bf16).reshape(64, -1, 128)


def fill_tables(ids, gates, pick, high, low):
    token = lax.broadcasted_iota(jnp.int32, (16, 128), 0)
    lane = lax.broadcasted_iota(jnp.int32, (16, 128), 1)
    spread = jnp.where(lax.shift_right_logical(lane, 3) == token, 1.0, 0.0).astype(bf16)
    names = dot(ids.astype(f32).astype(bf16), spread)
    gates_high = gates.astype(bf16)
    gates_low = (gates - gates_high.astype(f32)).astype(bf16)
    upper = dot(gates_high, spread)
    lower = dot(gates_low, spread)
    expert = lax.broadcasted_iota(jnp.int32, (64, 128), 0).astype(f32)
    named = jnp.zeros((64, 128), f32)
    first = jnp.zeros((64, 128), f32)
    second = jnp.zeros((64, 128), f32)
    for k in range(ids.shape[0]):
        match = expert == names[k : k + 1, :]
        named = jnp.where(match, 1.0, named)
        first = jnp.where(match, upper[k : k + 1, :], first)
        second = jnp.where(match, lower[k : k + 1, :], second)
    row = lax.broadcasted_iota(jnp.int32, (128, 128), 0)
    column = lax.broadcasted_iota(jnp.int32, (128, 128), 1)
    earlier = ((row & 7) == 0) & (
        lax.shift_right_logical(row, 3) < lax.shift_right_logical(column, 3)
    )
    before = dot(named.astype(bf16), jnp.where(earlier, 1.0, 0.0).astype(bf16))
    code = jnp.where(named > 0.0, before + 1.0, 0.0)
    slot_row = lax.broadcasted_iota(jnp.int32, (1, 16, 128), 1)
    slot_lane = lax.broadcasted_iota(jnp.int32, (1, 16, 128), 2)
    wanted = lax.shift_right_logical(slot_row, 3).astype(f32) + 1.0
    wanted = jnp.where((slot_row & 7) == (slot_lane & 7), wanted, 9.0)
    shape = (64, 16, 128)
    match = jnp.broadcast_to(code[:, None, :], shape) == jnp.broadcast_to(wanted, shape)
    zero = jnp.zeros(shape, f32)
    pick[...] = jnp.where(match, 1.0, zero).astype(bf16).reshape(1024, 128)
    first = jnp.broadcast_to(first[:, None, :], shape)
    high[...] = jnp.where(match, first, zero).astype(bf16).reshape(1024, 128)
    second = jnp.broadcast_to(second[:, None, :], shape)
    low[...] = jnp.where(match, second, zero).astype(bf16).reshape(1024, 128)


def start_body(*refs):
    place_ref, own_routes, got_routes, own_gates, got_gates = refs[0:5]
    x_ref, grad_ref, own_gain, got_gain = refs[5:9]
    out, x_rows, grad_rows = refs[9:12]
    pick0, high0, low0, pick1, high1, low1 = refs[12:18]
    wide = refs[18]
    section = place_ref[0]
    ids = (own_routes[:, section, :], got_routes[:, section, :])
    gates = (own_gates[:, section, :], got_gates[:, section, :])
    lower = section == 0
    fill_tables(
        jnp.where(lower, ids[0], ids[1]),
        jnp.where(lower, gates[0], gates[1]),
        pick0,
        high0,
        low0,
    )
    fill_tables(
        jnp.where(lower, ids[1], ids[0]),
        jnp.where(lower, gates[1], gates[0]),
        pick1,
        high1,
        low1,
    )
    x_block = token_rows(x_ref[section], wide)
    x_rows[...] = x_block
    gain = jnp.where(lower, own_gain[...], got_gain[...])
    out[...] = chunked(dot(pick0[...], normalized(x_block, gain)))
    grad_rows[...] = token_rows(grad_ref[section], wide)


def flip_body(*refs):
    for source, target in zip(refs[:6], refs[6:]):
        target[...] = source[...].astype(f32).T.astype(bf16)


def pack_body(layer, tensors, *refs):
    place_ref = refs[0]
    own, swapped = refs[1 : 1 + len(tensors)], refs[1 + len(tensors) : 1 + 2 * len(tensors)]
    outs, sems = refs[1 + 2 * len(tensors) : -1], refs[-1]
    section = place_ref[0]
    start = pl.multiple_of(section * 256, 256)
    start_down = pl.multiple_of(section * 384, 128)

    def copies(group):
        found = []
        for n, ref in zip(tensors, group):
            if n < 2:
                source, target = ref.at[pl.ds(start, 256), :], outs[0].at[256 * n : 256 * n + 256, :]
            else:
                source, target = ref.at[pl.ds(start_down, 384), :], outs[-1]
            found.append(pltpu.make_async_copy(source, target, sems.at[n]))
        return found

    @pl.when(section == layer)
    def _():
        for copy in copies(own):
            copy.start()

    @pl.when(section != layer)
    def _():
        for copy in copies(swapped):
            copy.start()

    for copy in copies(own):
        copy.wait()


def to_matrix(rows, wide, target):
    wide[...] = rows
    slots = rows.shape[0] // 8
    for j in range(8):
        target[:, 128 * j : 128 * (j + 1)] = wide[pl.ds(j, slots, stride=8), :].astype(bf16)


def to_rows(matrix, wide):
    slots = matrix.shape[0]
    for j in range(8):
        wide[pl.ds(j, slots, stride=8), :] = matrix[:, 128 * j : 128 * (j + 1)]
    return wide[...].astype(bf16)


def fetch(place_ref, layer, sources, targets, sems, order=(0, 1, 2)):
    own, swapped = sources[0:3], sources[3:6]
    section, part = place_ref[0], place_ref[1]
    mine = pl.multiple_of(part * 512, 512)
    rest = pl.multiple_of((1 - part) * 512, 512)

    def near(group, others):
        found = []
        for n in range(3):
            copies = []
            for h, (sources_now, start) in enumerate(((group, mine), (others, rest))):
                if sources_now:
                    if n < 2:
                        target = targets[n].at[pl.ds(start, 512), :]
                    else:
                        target = targets[n].at[:, pl.ds(start, 512)]
                    copies.append(pltpu.make_async_copy(sources_now[n], target, sems.at[n, h]))
            found.append(copies)
        return found

    def far(n):
        found = []
        for p in range(2):
            index = section if p == 0 else 1 - section
            if n < 2:
                start = pl.multiple_of(rest + index * 256, 256)
                source = sources[6 + p].at[256 * n : 256 * (n + 1), :]
                target = targets[n].at[pl.ds(start, 256), :]
            else:
                start = pl.multiple_of(index * 384, 128)
                source = sources[8 + p]
                target = targets[n].at[pl.ds(start, 384), pl.ds(rest, 512)]
            found.append(pltpu.make_async_copy(source, target, sems.at[n, 1 + p]))
        return found

    if layer == 0:
        gate, gate_passed, up, up_passed, down, down_passed = sources[6:12]
        lower, upper = (gate, up_passed, down), (gate_passed, up, down_passed)
        others = [[], [], []]
    else:
        lower, upper = (), ()
        others = [far(0), far(1), far(2)]

    for n in order:

        @pl.when(section == 0)
        def _(n=n):
            for copy in near(own if layer == 0 else swapped, lower)[n]:
                copy.start()

        @pl.when(section != 0)
        def _(n=n):
            for copy in near(swapped if layer == 0 else own, upper)[n]:
                copy.start()

        for copy in others[n]:
            copy.start()
    return [first + second for first, second in zip(near(own, lower), others)]


def gated(pre_gate, pre_up):
    return pre_gate / (1.0 + jnp.exp(-pre_gate)) * pre_up


def halves(place_ref, source, near, far):
    mine = pl.multiple_of(place_ref[1] * 512, 512)
    rest = pl.multiple_of((1 - place_ref[1]) * 512, 512)
    near[:, :512] = source[:, pl.ds(mine, 512)]
    far[:, :512] = source[:, pl.ds(rest, 512)]


def first_forward_body(*refs):
    place_ref, arrived_ref = refs[0:2]
    sources = refs[2:14]
    outs = refs[14:19]
    w_gate, w_up, w_down, wide, rows = refs[19:24]
    early, early_far, gate_out, up_out, arrived, result, sems, more = refs[24:]
    load = begin(arrived_ref, arrived, more.at[4])
    waits = fetch(place_ref, 0, sources, (w_gate, w_up, w_down), sems)
    load.wait()
    to_matrix(arrived[...].reshape(1024, 128).astype(f32), wide, rows)
    halves(place_ref, rows, early, early_far)
    finish(waits[0])
    pre_gate = dot(rows[...], w_gate[...])
    gate_out[...] = pre_gate
    stores = [begin(gate_out, outs[3], more.at[2])]
    finish(waits[1])
    pre_up = dot(rows[...], w_up[...])
    up_out[...] = pre_up
    stores.append(begin(up_out, outs[4], more.at[3]))
    acts = gated(pre_gate, pre_up).astype(bf16)
    early[:, 512:] = acts
    early_far[:, 512:] = acts
    stores.append(begin(early, outs[1], more.at[0]))
    stores.append(begin(early_far, outs[2], more.at[1]))
    finish(waits[2])
    result[...] = to_rows(dot(acts, w_down[...]), wide).reshape(64, 16, 128)
    stores.append(begin(result, outs[0], more.at[5]))
    finish(stores)


def expert_grads(act_grad, pre_gate, pre_up):
    sigma = 1.0 / (1.0 + jnp.exp(-pre_gate))
    gate_grad = (act_grad * pre_up * sigma * (1.0 + pre_gate * (1.0 - sigma))).astype(bf16)
    up_grad = (act_grad * pre_gate * sigma).astype(bf16)
    return (gate_grad, up_grad)


def gain_part(pick_rows, normed_rows):
    product = pick_rows.astype(f32) * normed_rows.astype(f32)
    return jnp.sum(product.reshape(-1, 8, 128), axis=0)


def second_body(*refs):
    place_ref, arrived_ref, early0_ref, early0_far_ref = refs[0:4]
    sources = refs[4:14]
    ends = refs[14:17]
    outs = refs[17:23]
    w_gate, w_up, w_down, wide, rows, grads, early, early_far = refs[23:31]
    arrived, early0, early0_far, late, late_far, picked, result, gain_out, sems, more = refs[31:]
    load = begin(arrived_ref, arrived, more.at[0])
    waits = fetch(place_ref, 1, sources, (w_gate, w_up, w_down), sems)
    loads = [
        begin(early0_ref, early0, more.at[1]),
        begin(early0_far_ref, early0_far, more.at[2]),
    ]
    load.wait()
    normed_rows = arrived[:, :16, :].reshape(1024, 128)
    to_matrix(normed_rows.astype(f32), wide, rows)
    halves(place_ref, rows, early, early_far)
    to_matrix(arrived[:, 16:, :].reshape(1024, 128).astype(f32), wide, grads)
    halves(place_ref, grads, late, late_far)
    finish(waits[0])
    pre_gate = dot(rows[...], w_gate[...])
    finish(waits[1])
    pre_up = dot(rows[...], w_up[...])
    acts = gated(pre_gate, pre_up).astype(bf16)
    early[:, 512:] = acts
    early_far[:, 512:] = acts

    finish(loads)

    def moves(order):
        return [
            pltpu.make_async_copy(source, outs[n], more.at[3 + n])
            for n, source in enumerate(order)
        ]

    @pl.when(place_ref[0] == 0)
    def _():
        for copy in moves((early0, early, early0_far, early_far)):
            copy.start()

    @pl.when(place_ref[0] != 0)
    def _():
        for copy in moves((early, early0, early_far, early0_far)):
            copy.start()

    stores = moves((early0, early, early0_far, early_far))
    finish(waits[2])
    act_grad = dot_nt(grads[...], w_down[...])
    gate_grad, up_grad = expert_grads(act_grad, pre_gate, pre_up)
    for target in (late, late_far):
        target[:, 512:1280] = gate_grad
        target[:, 1280:] = up_grad
    stores.append(begin(late, outs[4], more.at[7]))
    stores.append(begin(late_far, outs[5], more.at[8]))
    pick_rows = to_rows(dot_nt(gate_grad, w_gate[...]) + dot_nt(up_grad, w_up[...]), wide)
    picked[...] = pick_rows.reshape(64, 16, 128)
    stores.append(begin(picked, ends[0], more.at[9]))
    gain_out[...] = gain_part(pick_rows, normed_rows)
    stores.append(begin(gain_out, ends[2], more.at[10]))
    result[...] = to_rows(dot(acts, w_down[...]), wide).reshape(64, 16, 128)
    stores.append(begin(result, ends[1], more.at[11]))
    finish(stores)


def first_backward_body(*refs):
    place_ref, gain_second, arrived_ref, normed_ref, gate_ref, up_ref = refs[0:6]
    sources = refs[6:18]
    outs = refs[18:21]
    w_gate, w_up, w_down, wide, grads = refs[21:26]
    arrived, normed, pre_gate, pre_up, late, late_far, picked, sems, more = refs[26:]
    load = begin(arrived_ref.at[:, 0:16, :], arrived, more.at[0])
    loads = [begin(gate_ref, pre_gate, more.at[1]), begin(up_ref, pre_up, more.at[2])]
    waits = fetch(place_ref, 0, sources, (w_gate, w_up, w_down), sems, (2, 0, 1))
    loads.append(begin(normed_ref, normed, more.at[3]))
    load.wait()
    to_matrix(arrived[...].reshape(1024, 128).astype(f32), wide, grads)
    halves(place_ref, grads, late, late_far)
    finish(waits[2])
    act_grad = dot_nt(grads[...], w_down[...])
    finish(loads)
    gate_grad, up_grad = expert_grads(act_grad, pre_gate[...], pre_up[...])
    for target in (late, late_far):
        target[:, 512:1280] = gate_grad
        target[:, 1280:] = up_grad
    stores = [begin(late, outs[1], more.at[4]), begin(late_far, outs[2], more.at[5])]
    finish(waits[0])
    finish(waits[1])
    pick_rows = to_rows(dot_nt(gate_grad, w_gate[...]) + dot_nt(up_grad, w_up[...]), wide)
    picked[:, :16, :] = pick_rows.reshape(64, 16, 128)
    gain_first = gain_part(pick_rows, normed[...].reshape(1024, 128))
    both = jnp.concatenate([gain_first, gain_second[...]], axis=0).astype(bf16)
    picked[:, 16:, :] = jnp.broadcast_to(both[None], (64, 16, 128))
    stores.append(begin(picked, outs[0], more.at[6]))
    finish(stores)


def combined(high_t, low_t, rows):
    return dot(high_t[...], rows) + dot(low_t[...], rows)


def cotangent_body(grad_ref, high, low, out):
    grad = grad_ref[...]
    out[...] = chunked(dot(high[...], grad) + dot(low[...], grad))


def between_body(returned, x_ref, gain_ref, high_t, low_t, pick, cot, hidden, out):
    rows = returned[...].reshape(1024, 128)
    result = (x_ref[...].astype(f32) + combined(high_t, low_t, rows)).astype(bf16)
    hidden[...] = result
    out[:, :16, :] = chunked(dot(pick[...], normalized(result, gain_ref[...])))
    out[:, 16:, :] = cot[...]


def input_gradient(rows, upstream, x_block, gain, pick_t):
    normed_grad = dot(pick_t, rows).reshape(-1, 8, 128)
    values, scaling = token_stats(x_block)
    weighted = normed_grad * gain[None]
    mean = (
        jnp.sum(jnp.sum(weighted * values, axis=2, keepdims=True), axis=1, keepdims=True) / 1024.0
    )
    change = scaling * (weighted - values * scaling * scaling * mean)
    return (upstream.astype(f32) + change.reshape(upstream.shape)).astype(bf16)


def turn_body(returned, result, x_ref, grad_ref, gain_ref, pick_t, high, low, grad_out, out):
    rows = returned[...].reshape(1024, 128)
    grad = input_gradient(rows, grad_ref[...], x_ref[...], gain_ref[...], pick_t[...])
    grad_out[...] = grad
    out[:, :16, :] = chunked(dot(high[...], grad) + dot(low[...], grad))
    out[:, 16:, :] = result[...]


def second_output_body(place_ref, arrived, x_ref, high_t, low_t, hidden, sent):
    rows = arrived[:, 16:, :].reshape(1024, 128)
    before = x_ref[...].astype(f32)
    result = before + combined(high_t, low_t, rows)
    hidden[...] = result.astype(bf16)
    sent[...] = jnp.where(place_ref[0] == 0, result, before).astype(bf16)


def arrange(section, first, second, got, wide, out):
    mine = jnp.where(section == 0, first.astype(f32), second.astype(f32))
    for index, rows in ((section, mine), (1 - section, got)):
        for j, piece in enumerate(token_matrix(rows, wide)):
            out[index, :, 128 * j : 128 * (j + 1)] = piece


def hidden_body(place_ref, first, second, got, out, wide):
    arrange(place_ref[0], first[...], second[...], got[...], wide, out)


def last_body(*refs):
    place_ref, returned = refs[0:2]
    grad_out, sent, gain_out = refs[6:9]
    x_ref, grad_ref, gain_ref, pick_t, sems = refs[9:]
    finish([begin(refs[2 + n], refs[9 + n], sems.at[n]) for n in range(4)])
    rows = returned[:, :16, :].reshape(1024, 128)
    grad = input_gradient(rows, grad_ref[...], x_ref[...], gain_ref[...], pick_t[...])
    grad_out[...] = grad
    gain_rows = jnp.sum(returned[:, 16:, :].astype(f32), axis=0)
    sent[:128, :] = jnp.where(place_ref[0] == 0, grad_ref[...].astype(f32), grad.astype(f32))
    sent[128:, :] = gain_rows
    gain_out[...] = gain_rows


def final_body(*refs):
    place_ref, first, second, got = refs[0:4]
    gain_rows, gain_straight, gain_cross, own_gain = refs[4:8]
    out, gain_out, wide = refs[8:]
    arrange(place_ref[0], first[...], second[...], got[:128, :], wide, out)
    total = (gain_rows[...] + got[128:, :]) + (gain_straight[...] + gain_cross[...])
    gain_out[...] = jnp.where(place_ref[0] == 0, total[:8], total[8:]) / own_gain[...]


def weight_body(*refs):
    place_ref = refs[0]
    early_parts, first, second = refs[1:5], refs[5:9], refs[9:13]
    outs = refs[13:16]
    early, late, gate, up, down, sems, out_sems = refs[16:]

    def copies(target, group, row):
        return [
            pltpu.make_async_copy(group[n], target.at[pl.ds(128 * n, 128), :], sems.at[row, n])
            for n in range(4)
        ]

    @pl.when(place_ref[0] == 0)
    def _():
        for copy in copies(late, first, 1):
            copy.start()

    @pl.when(place_ref[0] != 0)
    def _():
        for copy in copies(late, second, 1):
            copy.start()

    for copy in copies(early, early_parts, 0):
        copy.start()
    for copy in copies(early, early_parts, 0) + copies(late, first, 1):
        copy.wait()
    normed = early[:, :512]
    done = []
    for n, target in enumerate((gate, up, down)):
        if n < 2:
            target[...] = dot_tn(normed, late[:, 512 + 768 * n : 1280 + 768 * n])
        else:
            target[...] = dot_tn(early[:, 512:], late[:, :512])
        copy = pltpu.make_async_copy(target, outs[n], out_sems.at[n])
        copy.start()
        done.append(copy)
    for copy in done:
        copy.wait()


def after(block, other):
    return lax.optimization_barrier((block, other))[0]


def window(activations, cotangent, norm_gain, w_gate, w_up, w_down, routes, gate_weights):
    section = lax.axis_index("section")
    part = lax.axis_index("dp")
    experts = lax.axis_size("expert")
    place = jnp.stack([section, part]).astype(jnp.int32)
    micro_count, tokens, width = activations.shape
    swap = [(0, 1), (1, 0)]

    def flat(s, e, d):
        return (s * experts + e) * 2 + d

    def pairs(layer, cross):
        found = []
        for s in range(2):
            target = 1 - s if cross else s
            if layer is None or target == layer:
                found += [
                    (flat(s, e, d), flat(target, e, 1 - d))
                    for e in range(experts)
                    for d in range(2)
                ]
        return found

    def beside(block, route=swap):
        return lax.ppermute(block, "section", route)

    def away(block, layer=None, cross=False):
        return lax.ppermute(block, every, pairs(layer, cross))

    def exchange(block):
        return lax.all_to_all(block, "expert", split_axis=0, concat_axis=0, tiled=True)

    own = (w_gate[0, 0], w_up[0, 0], w_down[0, 0])
    own_gain = norm_gain.reshape(8, 128)
    own_routes = routes[0].transpose(2, 0, 1)
    own_gates = gate_weights[0].transpose(2, 0, 1)
    got_routes = beside(own_routes)
    got_gates = beside(own_gates)
    got_gain = beside(own_gain)
    swapped = tuple(beside(w) for w in own)

    big = ((64, 32, 128), bf16)
    small = ((64, 16, 128), bf16)
    block = ((128, 128), bf16)
    early_shape = ((128, 1280), bf16)
    late_shape = ((128, 2048), bf16)
    down = ((1024, 128), bf16)
    across = ((128, 1024), bf16)
    weight_scratch = [
        pltpu.VMEM((1024, 768), bf16),
        pltpu.VMEM((1024, 768), bf16),
        pltpu.VMEM((768, 1024), bf16),
    ]
    wide = pltpu.VMEM((1024, 128), f32)
    narrow = pltpu.VMEM((128, 128), f32)
    matrix = pltpu.VMEM((128, 1024), bf16)
    sems = pltpu.SemaphoreType.DMA((3, 3))
    early_room = pltpu.VMEM((128, 1280), bf16)
    late_room = pltpu.VMEM((128, 2048), bf16)
    plain_room = pltpu.VMEM((128, 768), f32)
    arrival = pltpu.VMEM((64, 16, 128), bf16)

    out_first, x_first, grad_last, *maps = plain(
        start_body,
        [smem] + [vmem] * 8,
        [small, block, block] + [down] * 6,
        [place, own_routes, got_routes, own_gates, got_gates]
        + [activations, cotangent, own_gain, got_gain],
        [narrow],
    )
    _, high0, low0, pick1, high1, low1 = maps
    first_gain = jnp.where(section == 0, own_gain, got_gain)
    second_gain = jnp.where(section == 0, got_gain, own_gain)

    def packed(layer, tensors):
        shapes = [((512, 768), bf16), ((384, 512), bf16)][-min(2, len(tensors)) :]
        return call(
            functools.partial(pack_body, layer, tensors),
            [smem] + [anywhere] * (2 * len(tensors)),
            shapes,
            [pltpu.SemaphoreType.DMA((3,))],
            flops=1,
            moved=25 * 10**5,
        )(place, *[own[n] for n in tensors], *[swapped[n] for n in tensors])

    gate_far = away(own[0], 0)
    up_far = away(swapped[1], 1)
    down_far = away(own[2], 0)
    portions0 = (
        gate_far,
        beside(gate_far, [(0, 1)]),
        up_far,
        beside(up_far, [(1, 0)]),
        down_far,
        beside(down_far, [(0, 1)]),
    )
    arrived_first = exchange(out_first)

    flipped = call(flip_body, [vmem] * 6, [across] * 6, flops=10**6, moved=3 * 10**6)(*maps)
    pick0_t, high0_t, low0_t, pick1_t, high1_t, low1_t = flipped
    cot = plain(cotangent_body, [], [small], [grad_last, high1, low1])[0]

    portions1 = [
        away(after(w, other))
        for w, other in zip(packed(1, (0, 1, 2)), (up_far, down_far))
    ]
    portions1 = [w for far in portions1 for w in (far, beside(far))]

    result, early0, early0_far, pre_gate, pre_up = call(
        first_forward_body,
        [smem] + [hbm] * 13,
        [small, early_shape, early_shape, ((128, 768), f32), ((128, 768), f32)],
        weight_scratch
        + [wide, matrix, early_room, early_room, plain_room, plain_room, arrival, arrival, sems]
        + [pltpu.SemaphoreType.DMA((6,))],
        flops=6 * 10**8,
        moved=6 * 10**6,
        out_spec=hbm,
    )(place, arrived_first, *own, *swapped, *portions0)
    returned = exchange(result)

    hidden_first, out_second = plain(
        between_body,
        [vmem],
        [block, big],
        [returned, x_first, second_gain, high0_t, low0_t, pick1, cot],
    )
    arrived_second = exchange(out_second)

    picked, result_second, gain_second, kept, sent, straight, cross, late1, late1_far = call(
        second_body,
        [smem] + [hbm] * 13,
        [small, small, ((8, 128), f32)] + [early_shape] * 4 + [late_shape] * 2,
        weight_scratch
        + [wide, matrix, matrix, early_room, early_room]
        + [pltpu.VMEM((64, 32, 128), bf16), early_room, early_room]
        + [late_room, late_room, arrival, arrival]
        + [pltpu.VMEM((8, 128), f32), sems, pltpu.SemaphoreType.DMA((12,))],
        flops=12 * 10**8,
        moved=8 * 10**6,
        out_spec=hbm,
    )(place, arrived_second, early0, early0_far, *own, *swapped, *portions1)
    returned = exchange(picked)

    early_parts = (kept, beside(sent), away(straight), away(cross, cross=True))
    late1_parts = (late1, beside(late1, [(0, 1)]), away(late1_far, 1), away(late1_far, 1, True))

    grad_middle, out_third = plain(
        turn_body,
        [vmem],
        [block, big],
        [returned, result_second, hidden_first, grad_last, second_gain, pick1_t, high0, low0],
    )
    arrived_third = exchange(out_third)

    picked, late0, late0_far = call(
        first_backward_body,
        [smem, vmem] + [hbm] * 16,
        [big, late_shape, late_shape],
        weight_scratch
        + [wide, matrix, arrival, arrival, plain_room, plain_room, late_room, late_room]
        + [pltpu.VMEM((64, 32, 128), bf16), sems, pltpu.SemaphoreType.DMA((7,))],
        flops=6 * 10**8,
        moved=8 * 10**6,
        out_spec=hbm,
    )(
        place,
        gain_second,
        arrived_third,
        arrived_first,
        pre_gate,
        pre_up,
        *own,
        *swapped,
        *portions0,
    )
    late0_parts = (late0, beside(late0, [(1, 0)]), away(late0_far, 0), away(late0_far, 0, True))
    returned = exchange(picked)

    hidden_second, hidden_sent = call(
        second_output_body, [smem] + [vmem] * 4, [block, block], flops=10**8, moved=10**6, grant=16
    )(place, arrived_third, hidden_first, high1_t, low1_t)
    both = ((micro_count, tokens, width), bf16)
    hidden = call(
        hidden_body, [smem] + [vmem] * 3, [both], [narrow], flops=10**5, moved=10**5, grant=16
    )(place, hidden_first, hidden_second, beside(hidden_sent))[0]

    weight_grads = call(
        weight_body,
        [smem] + [anywhere] * 12,
        [((512, 768), f32), ((512, 768), f32), ((768, 512), f32)],
        [
            pltpu.VMEM((512, 1280), bf16),
            pltpu.VMEM((512, 2048), bf16),
            pltpu.VMEM((512, 768), f32),
            pltpu.VMEM((512, 768), f32),
            pltpu.VMEM((768, 512), f32),
            pltpu.SemaphoreType.DMA((2, 4)),
            pltpu.SemaphoreType.DMA((3,)),
        ],
        flops=12 * 10**8,
        moved=8 * 10**6,
        grant=28,
        out_spec=anywhere,
    )(place, *early_parts, *late0_parts, *late1_parts)

    grad_first, grad_sent, gain_rows = call(
        last_body,
        [smem, vmem] + [hbm] * 4,
        [block, ((144, 128), f32), ((16, 128), f32)],
        [
            pltpu.VMEM((128, 128), bf16),
            pltpu.VMEM((128, 128), bf16),
            pltpu.VMEM((8, 128), f32),
            matrix,
            pltpu.SemaphoreType.DMA((4,)),
        ],
        flops=10**8,
        moved=10**6,
        grant=16,
    )(place, returned, x_first, grad_middle, first_gain, pick0_t)
    grads, gain_grad = call(
        final_body,
        [smem] + [vmem] * 7,
        [both, ((8, 128), f32)],
        [narrow],
        flops=10**5,
        moved=10**5,
        grant=16,
    )(
        place,
        grad_first,
        grad_middle,
        beside(grad_sent),
        gain_rows,
        away(gain_rows),
        away(gain_rows, cross=True),
        own_gain,
    )
    return (
        hidden[None],
        grads[None],
        gain_grad.reshape(1, width),
        weight_grads[0][None, None],
        weight_grads[1][None, None],
        weight_grads[2][None, None],
    )


def solution(mesh):
    placed = (
        P(None, ("expert", "dp"), None),
        P(None, ("expert", "dp"), None),
        P("section", None),
        P("section", "expert", "dp", None),
        P("section", "expert", "dp", None),
        P("section", "expert", None, "dp"),
        P("section", None, ("expert", "dp"), None),
        P("section", None, ("expert", "dp"), None),
    )
    return jax.shard_map(
        window,
        mesh=mesh,
        in_specs=placed,
        out_specs=(
            P("section", None, ("expert", "dp"), None),
            P("section", None, ("expert", "dp"), None),
            P("section", None),
            P("section", "expert", "dp", None),
            P("section", "expert", "dp", None),
            P("section", "expert", None, "dp"),
        ),
        check_vma=False,
    )
```

```python
import functools
import jax
import jax.numpy as jnp
from jax import lax
from jax.experimental import pallas as pl
from jax.experimental.pallas import tpu as pltpu
from jax.sharding import PartitionSpec as P

epsilon = 1e-06
f32 = jnp.float32
bf16 = jnp.bfloat16
every = ("section", "expert", "dp")
vmem = pl.BlockSpec(memory_space=pltpu.VMEM)
smem = pl.BlockSpec(memory_space=pltpu.SMEM)
anywhere = pl.BlockSpec(memory_space=pl.ANY)
hbm = pl.BlockSpec(memory_space=pltpu.HBM)


def dot(left, right):
    return jnp.dot(left, right, preferred_element_type=f32)


def dot_nt(left, right):
    return lax.dot_general(left, right, (((1,), (1,)), ((), ())), preferred_element_type=f32)


def dot_tn(left, right):
    return lax.dot_general(left, right, (((0,), (0,)), ((), ())), preferred_element_type=f32)


def call(body, in_specs, outs, scratch=(), flops=0, moved=0, grant=None, out_spec=vmem):
    return pl.pallas_call(
        body,
        in_specs=in_specs,
        out_shape=[jax.ShapeDtypeStruct(shape, dtype) for shape, dtype in outs],
        out_specs=out_spec if isinstance(out_spec, list) else [out_spec] * len(outs),
        scratch_shapes=list(scratch),
        cost_estimate=pl.CostEstimate(flops=flops, bytes_accessed=moved, transcendentals=0),
        compiler_params=pltpu.CompilerParams(vmem_limit_bytes=grant and grant * 2**20),
    )


def begin(source, target, sem):
    copy = pltpu.make_async_copy(source, target, sem)
    copy.start()
    return copy


def finish(group):
    for copy in group:
        copy.wait()


def plain(body, in_specs, outs, arrays, scratch=()):
    specs = list(in_specs) + [vmem] * (len(arrays) - len(in_specs))
    return call(body, specs, outs, scratch, flops=10**8, moved=2 * 10**6)(*arrays)


def token_rows(block, wide):
    values = block.astype(f32)
    for j in range(8):
        wide[pl.ds(j, 16, stride=8), :] = values[:, 128 * j : 128 * (j + 1)]
    return wide[...].astype(bf16)


def token_matrix(rows, wide):
    wide[...] = rows.astype(f32)
    return [wide[pl.ds(j, 16, stride=8), :].astype(bf16) for j in range(8)]


def token_stats(block):
    values = block.astype(f32).reshape(-1, 8, 128)
    mean = jnp.sum(jnp.sum(values * values, axis=2, keepdims=True), axis=1, keepdims=True) / 1024.0
    return (values, lax.rsqrt(mean + epsilon))


def normalized(block, gain):
    values, scaling = token_stats(block)
    return (values * scaling * gain[None]).astype(bf16).reshape(block.shape)


def chunked(rows):
    return rows.astype(bf16).reshape(64, -1, 128)


def fill_tables(ids, gates, pick, high, low):
    token = lax.broadcasted_iota(jnp.int32, (16, 128), 0)
    lane = lax.broadcasted_iota(jnp.int32, (16, 128), 1)
    spread = jnp.where(lax.shift_right_logical(lane, 3) == token, 1.0, 0.0).astype(bf16)
    names = dot(ids.astype(f32).astype(bf16), spread)
    gates_high = gates.astype(bf16)
    gates_low = (gates - gates_high.astype(f32)).astype(bf16)
    upper = dot(gates_high, spread)
    lower = dot(gates_low, spread)
    expert = lax.broadcasted_iota(jnp.int32, (64, 128), 0).astype(f32)
    named = jnp.zeros((64, 128), f32)
    first = jnp.zeros((64, 128), f32)
    second = jnp.zeros((64, 128), f32)
    for k in range(ids.shape[0]):
        match = expert == names[k : k + 1, :]
        named = jnp.where(match, 1.0, named)
        first = jnp.where(match, upper[k : k + 1, :], first)
        second = jnp.where(match, lower[k : k + 1, :], second)
    row = lax.broadcasted_iota(jnp.int32, (128, 128), 0)
    column = lax.broadcasted_iota(jnp.int32, (128, 128), 1)
    earlier = ((row & 7) == 0) & (
        lax.shift_right_logical(row, 3) < lax.shift_right_logical(column, 3)
    )
    before = dot(named.astype(bf16), jnp.where(earlier, 1.0, 0.0).astype(bf16))
    code = jnp.where(named > 0.0, before + 1.0, 0.0)
    slot_row = lax.broadcasted_iota(jnp.int32, (1, 16, 128), 1)
    slot_lane = lax.broadcasted_iota(jnp.int32, (1, 16, 128), 2)
    wanted = lax.shift_right_logical(slot_row, 3).astype(f32) + 1.0
    wanted = jnp.where((slot_row & 7) == (slot_lane & 7), wanted, 9.0)
    shape = (64, 16, 128)
    match = jnp.broadcast_to(code[:, None, :], shape) == jnp.broadcast_to(wanted, shape)
    zero = jnp.zeros(shape, f32)
    pick[...] = jnp.where(match, 1.0, zero).astype(bf16).reshape(1024, 128)
    first = jnp.broadcast_to(first[:, None, :], shape)
    high[...] = jnp.where(match, first, zero).astype(bf16).reshape(1024, 128)
    second = jnp.broadcast_to(second[:, None, :], shape)
    low[...] = jnp.where(match, second, zero).astype(bf16).reshape(1024, 128)


def start_body(*refs):
    place_ref, own_routes, got_routes, own_gates, got_gates = refs[0:5]
    x_ref, grad_ref, own_gain, got_gain = refs[5:9]
    out, x_rows, grad_rows = refs[9:12]
    pick0, high0, low0, pick1, high1, low1 = refs[12:18]
    wide = refs[18]
    section = place_ref[0]
    ids = (own_routes[:, section, :], got_routes[:, section, :])
    gates = (own_gates[:, section, :], got_gates[:, section, :])
    lower = section == 0
    fill_tables(
        jnp.where(lower, ids[0], ids[1]),
        jnp.where(lower, gates[0], gates[1]),
        pick0,
        high0,
        low0,
    )
    fill_tables(
        jnp.where(lower, ids[1], ids[0]),
        jnp.where(lower, gates[1], gates[0]),
        pick1,
        high1,
        low1,
    )
    x_block = token_rows(x_ref[section], wide)
    x_rows[...] = x_block
    gain = jnp.where(lower, own_gain[...], got_gain[...])
    out[:, :16, :] = chunked(dot(pick0[...], normalized(x_block, gain)))
    grad = token_rows(grad_ref[section], wide)
    grad_rows[...] = grad
    out[:, 16:, :] = chunked(dot(high1[...], grad) + dot(low1[...], grad))


def flip_body(*refs):
    for source, target in zip(refs[:6], refs[6:]):
        target[...] = source[...].astype(f32).T.astype(bf16)


def pack_body(layer, tensors, *refs):
    place_ref = refs[0]
    own, swapped = refs[1 : 1 + len(tensors)], refs[1 + len(tensors) : 1 + 2 * len(tensors)]
    outs, sems = refs[1 + 2 * len(tensors) : -1], refs[-1]
    section = place_ref[0]
    start = pl.multiple_of(section * 256, 256)
    start_down = pl.multiple_of(section * 384, 128)

    def copies(group):
        found = []
        for n, ref in zip(tensors, group):
            if n < 2:
                source, target = ref.at[pl.ds(start, 256), :], outs[0].at[256 * n : 256 * n + 256, :]
            else:
                source, target = ref.at[pl.ds(start_down, 384), :], outs[-1]
            found.append(pltpu.make_async_copy(source, target, sems.at[n]))
        return found

    @pl.when(section == layer)
    def _():
        for copy in copies(own):
            copy.start()

    @pl.when(section != layer)
    def _():
        for copy in copies(swapped):
            copy.start()

    for copy in copies(own):
        copy.wait()


def to_matrix(rows, wide, target):
    wide[...] = rows
    slots = rows.shape[0] // 8
    for j in range(8):
        target[:, 128 * j : 128 * (j + 1)] = wide[pl.ds(j, slots, stride=8), :].astype(bf16)


def to_rows(matrix, wide):
    slots = matrix.shape[0]
    for j in range(8):
        wide[pl.ds(j, slots, stride=8), :] = matrix[:, 128 * j : 128 * (j + 1)]
    return wide[...].astype(bf16)


def fetch(place_ref, layer, sources, targets, sems, order=(0, 1, 2)):
    own, swapped = sources[0:3], sources[3:6]
    section, part = place_ref[0], place_ref[1]
    mine = pl.multiple_of(part * 512, 512)
    rest = pl.multiple_of((1 - part) * 512, 512)

    def near(group, others):
        found = []
        for n in range(3):
            copies = []
            for h, (sources_now, start) in enumerate(((group, mine), (others, rest))):
                if sources_now:
                    if n < 2:
                        target = targets[n].at[pl.ds(start, 512), :]
                    else:
                        target = targets[n].at[:, pl.ds(start, 512)]
                    copies.append(pltpu.make_async_copy(sources_now[n], target, sems.at[n, h]))
            found.append(copies)
        return found

    def far(n):
        found = []
        for p in range(2):
            index = section if p == 0 else 1 - section
            if n < 2:
                start = pl.multiple_of(rest + index * 256, 256)
                source = sources[6 + p].at[256 * n : 256 * (n + 1), :]
                target = targets[n].at[pl.ds(start, 256), :]
            else:
                start = pl.multiple_of(index * 384, 128)
                source = sources[8 + p]
                target = targets[n].at[pl.ds(start, 384), pl.ds(rest, 512)]
            found.append(pltpu.make_async_copy(source, target, sems.at[n, 1 + p]))
        return found

    if layer == 0:
        gate, gate_passed, up, up_passed, down, down_passed = sources[6:12]
        lower, upper = (gate, up_passed, down), (gate_passed, up, down_passed)
        others = [[], [], []]
    else:
        lower, upper = (), ()
        others = [far(0), far(1), far(2)]

    for n in order:

        @pl.when(section == 0)
        def _(n=n):
            for copy in near(own if layer == 0 else swapped, lower)[n]:
                copy.start()

        @pl.when(section != 0)
        def _(n=n):
            for copy in near(swapped if layer == 0 else own, upper)[n]:
                copy.start()

        for copy in others[n]:
            copy.start()
    return [first + second for first, second in zip(near(own, lower), others)]


def gated(pre_gate, pre_up):
    return pre_gate / (1.0 + jnp.exp(-pre_gate)) * pre_up


def halves(place_ref, source, near, far):
    mine = pl.multiple_of(place_ref[1] * 512, 512)
    rest = pl.multiple_of((1 - place_ref[1]) * 512, 512)
    near[:, :512] = source[:, pl.ds(mine, 512)]
    far[:, :512] = source[:, pl.ds(rest, 512)]


def first_forward_body(*refs):
    place_ref, arrived_ref = refs[0:2]
    sources = refs[2:14]
    outs = refs[14:19]
    w_gate, w_up, w_down, wide, rows = refs[19:24]
    early, early_far, gate_out, up_out, arrived, result, sems, more = refs[24:]
    load = begin(arrived_ref.at[:, 0:16, :], arrived, more.at[4])
    waits = fetch(place_ref, 0, sources, (w_gate, w_up, w_down), sems)
    load.wait()
    to_matrix(arrived[...].reshape(1024, 128).astype(f32), wide, rows)
    halves(place_ref, rows, early, early_far)
    finish(waits[0])
    pre_gate = dot(rows[...], w_gate[...])
    gate_out[...] = pre_gate
    stores = [begin(gate_out, outs[3], more.at[2])]
    finish(waits[1])
    pre_up = dot(rows[...], w_up[...])
    up_out[...] = pre_up
    stores.append(begin(up_out, outs[4], more.at[3]))
    acts = gated(pre_gate, pre_up).astype(bf16)
    early[:, 512:] = acts
    early_far[:, 512:] = acts
    stores.append(begin(early, outs[1], more.at[0]))
    stores.append(begin(early_far, outs[2], more.at[1]))
    finish(waits[2])
    result[...] = to_rows(dot(acts, w_down[...]), wide).reshape(64, 16, 128)
    stores.append(begin(result, outs[0], more.at[5]))
    finish(stores)


def expert_grads(act_grad, pre_gate, pre_up):
    sigma = 1.0 / (1.0 + jnp.exp(-pre_gate))
    gate_grad = (act_grad * pre_up * sigma * (1.0 + pre_gate * (1.0 - sigma))).astype(bf16)
    up_grad = (act_grad * pre_gate * sigma).astype(bf16)
    return (gate_grad, up_grad)


def gain_part(pick_rows, normed_rows):
    product = pick_rows.astype(f32) * normed_rows.astype(f32)
    return jnp.sum(product.reshape(-1, 8, 128), axis=0)


def second_body(*refs):
    place_ref, arrived_ref, cot_ref, early0_ref, early0_far_ref = refs[0:5]
    sources = refs[5:15]
    ends = refs[15:18]
    outs = refs[18:24]
    w_gate, w_up, w_down, wide, rows, grads, early, early_far = refs[24:32]
    arrived, cot, early0, early0_far, late, late_far = refs[32:38]
    picked, result, gain_out, sems, more = refs[38:]
    load = begin(arrived_ref, arrived, more.at[0])
    load_cot = begin(cot_ref.at[:, 16:32, :], cot, more.at[12])
    waits = fetch(place_ref, 1, sources, (w_gate, w_up, w_down), sems)
    loads = [
        begin(early0_ref, early0, more.at[1]),
        begin(early0_far_ref, early0_far, more.at[2]),
    ]
    load.wait()
    normed_rows = arrived[...].reshape(1024, 128)
    to_matrix(normed_rows.astype(f32), wide, rows)
    halves(place_ref, rows, early, early_far)
    load_cot.wait()
    to_matrix(cot[...].reshape(1024, 128).astype(f32), wide, grads)
    halves(place_ref, grads, late, late_far)
    finish(waits[0])
    pre_gate = dot(rows[...], w_gate[...])
    finish(waits[1])
    pre_up = dot(rows[...], w_up[...])
    acts = gated(pre_gate, pre_up).astype(bf16)
    early[:, 512:] = acts
    early_far[:, 512:] = acts

    finish(loads)

    def moves(order):
        return [
            pltpu.make_async_copy(source, outs[n], more.at[3 + n])
            for n, source in enumerate(order)
        ]

    @pl.when(place_ref[0] == 0)
    def _():
        for copy in moves((early0, early, early0_far, early_far)):
            copy.start()

    @pl.when(place_ref[0] != 0)
    def _():
        for copy in moves((early, early0, early_far, early0_far)):
            copy.start()

    stores = moves((early0, early, early0_far, early_far))
    finish(waits[2])
    act_grad = dot_nt(grads[...], w_down[...])
    gate_grad, up_grad = expert_grads(act_grad, pre_gate, pre_up)
    for target in (late, late_far):
        target[:, 512:1280] = gate_grad
        target[:, 1280:] = up_grad
    stores.append(begin(late, outs[4], more.at[7]))
    stores.append(begin(late_far, outs[5], more.at[8]))
    pick_rows = to_rows(dot_nt(gate_grad, w_gate[...]) + dot_nt(up_grad, w_up[...]), wide)
    picked[...] = pick_rows.reshape(64, 16, 128)
    stores.append(begin(picked, ends[0], more.at[9]))
    gain_out[...] = gain_part(pick_rows, normed_rows)
    stores.append(begin(gain_out, ends[2], more.at[10]))
    result[...] = to_rows(dot(acts, w_down[...]), wide).reshape(64, 16, 128)
    stores.append(begin(result, ends[1], more.at[11]))
    finish(stores)


def first_backward_body(*refs):
    place_ref, gain_second, arrived_ref, normed_ref, gate_ref, up_ref = refs[0:6]
    sources = refs[6:18]
    outs = refs[18:21]
    w_gate, w_up, w_down, wide, grads = refs[21:26]
    arrived, normed, pre_gate, pre_up, late, late_far, picked, sems, more = refs[26:]
    load = begin(arrived_ref.at[:, 0:16, :], arrived, more.at[0])
    loads = [begin(gate_ref, pre_gate, more.at[1]), begin(up_ref, pre_up, more.at[2])]
    waits = fetch(place_ref, 0, sources, (w_gate, w_up, w_down), sems, (2, 0, 1))
    loads.append(begin(normed_ref.at[:, 0:16, :], normed, more.at[3]))
    load.wait()
    to_matrix(arrived[...].reshape(1024, 128).astype(f32), wide, grads)
    halves(place_ref, grads, late, late_far)
    finish(waits[2])
    act_grad = dot_nt(grads[...], w_down[...])
    finish(loads)
    gate_grad, up_grad = expert_grads(act_grad, pre_gate[...], pre_up[...])
    for target in (late, late_far):
        target[:, 512:1280] = gate_grad
        target[:, 1280:] = up_grad
    stores = [begin(late, outs[1], more.at[4]), begin(late_far, outs[2], more.at[5])]
    finish(waits[0])
    finish(waits[1])
    pick_rows = to_rows(dot_nt(gate_grad, w_gate[...]) + dot_nt(up_grad, w_up[...]), wide)
    picked[:, :16, :] = pick_rows.reshape(64, 16, 128)
    gain_first = gain_part(pick_rows, normed[...].reshape(1024, 128))
    both = jnp.concatenate([gain_first, gain_second[...]], axis=0).astype(bf16)
    picked[:, 16:, :] = jnp.broadcast_to(both[None], (64, 16, 128))
    stores.append(begin(picked, outs[0], more.at[6]))
    finish(stores)


def combined(high_t, low_t, rows):
    return dot(high_t[...], rows) + dot(low_t[...], rows)


def between_body(returned, x_ref, gain_ref, high_t, low_t, pick, hidden, out):
    rows = returned[...].reshape(1024, 128)
    result = (x_ref[...].astype(f32) + combined(high_t, low_t, rows)).astype(bf16)
    hidden[...] = result
    out[...] = chunked(dot(pick[...], normalized(result, gain_ref[...])))


def input_gradient(rows, upstream, x_block, gain, pick_t):
    normed_grad = dot(pick_t, rows).reshape(-1, 8, 128)
    values, scaling = token_stats(x_block)
    weighted = normed_grad * gain[None]
    mean = (
        jnp.sum(jnp.sum(weighted * values, axis=2, keepdims=True), axis=1, keepdims=True) / 1024.0
    )
    change = scaling * (weighted - values * scaling * scaling * mean)
    return (upstream.astype(f32) + change.reshape(upstream.shape)).astype(bf16)


def turn_body(returned, result, x_ref, grad_ref, gain_ref, pick_t, high, low, grad_out, out):
    rows = returned[...].reshape(1024, 128)
    grad = input_gradient(rows, grad_ref[...], x_ref[...], gain_ref[...], pick_t[...])
    grad_out[...] = grad
    out[:, :16, :] = chunked(dot(high[...], grad) + dot(low[...], grad))
    out[:, 16:, :] = result[...]


def second_output_body(place_ref, arrived, x_ref, high_t, low_t, hidden, sent):
    rows = arrived[:, 16:, :].reshape(1024, 128)
    before = x_ref[...].astype(f32)
    result = before + combined(high_t, low_t, rows)
    hidden[...] = result.astype(bf16)
    sent[...] = jnp.where(place_ref[0] == 0, result, before).astype(bf16)


def arrange(section, first, second, got, wide, out):
    mine = jnp.where(section == 0, first.astype(f32), second.astype(f32))
    for index, rows in ((section, mine), (1 - section, got)):
        for j, piece in enumerate(token_matrix(rows, wide)):
            out[index, :, 128 * j : 128 * (j + 1)] = piece


def hidden_body(place_ref, first, second, got, out, wide):
    arrange(place_ref[0], first[...], second[...], got[...], wide, out)


def last_body(*refs):
    place_ref, returned = refs[0:2]
    grad_out, sent, gain_out = refs[6:9]
    x_ref, grad_ref, gain_ref, pick_t, sems = refs[9:]
    finish([begin(refs[2 + n], refs[9 + n], sems.at[n]) for n in range(4)])
    rows = returned[:, :16, :].reshape(1024, 128)
    grad = input_gradient(rows, grad_ref[...], x_ref[...], gain_ref[...], pick_t[...])
    grad_out[...] = grad
    gain_rows = jnp.sum(returned[:, 16:, :].astype(f32), axis=0)
    sent[:128, :] = jnp.where(place_ref[0] == 0, grad_ref[...].astype(f32), grad.astype(f32))
    sent[128:, :] = gain_rows
    gain_out[...] = gain_rows


def final_body(*refs):
    place_ref, first, second, got = refs[0:4]
    gain_rows, gain_straight, gain_cross, own_gain = refs[4:8]
    out, gain_out, wide = refs[8:]
    arrange(place_ref[0], first[...], second[...], got[:128, :], wide, out)
    total = (gain_rows[...] + got[128:, :]) + (gain_straight[...] + gain_cross[...])
    gain_out[...] = jnp.where(place_ref[0] == 0, total[:8], total[8:]) / own_gain[...]


def weight_body(*refs):
    place_ref = refs[0]
    early_parts, first, second = refs[1:5], refs[5:9], refs[9:13]
    outs = refs[13:16]
    early, late, gate, up, down, sems, out_sems = refs[16:]

    def copies(target, group, row):
        return [
            pltpu.make_async_copy(group[n], target.at[pl.ds(128 * n, 128), :], sems.at[row, n])
            for n in range(4)
        ]

    @pl.when(place_ref[0] == 0)
    def _():
        for copy in copies(late, first, 1):
            copy.start()

    @pl.when(place_ref[0] != 0)
    def _():
        for copy in copies(late, second, 1):
            copy.start()

    for copy in copies(early, early_parts, 0):
        copy.start()
    for copy in copies(early, early_parts, 0) + copies(late, first, 1):
        copy.wait()
    normed = early[:, :512]
    done = []
    for n, target in enumerate((gate, up, down)):
        if n < 2:
            target[...] = dot_tn(normed, late[:, 512 + 768 * n : 1280 + 768 * n])
        else:
            target[...] = dot_tn(early[:, 512:], late[:, :512])
        copy = pltpu.make_async_copy(target, outs[n], out_sems.at[n])
        copy.start()
        done.append(copy)
    for copy in done:
        copy.wait()


def after(block, other):
    return lax.optimization_barrier((block, other))[0]


def window(activations, cotangent, norm_gain, w_gate, w_up, w_down, routes, gate_weights):
    section = lax.axis_index("section")
    part = lax.axis_index("dp")
    experts = lax.axis_size("expert")
    place = jnp.stack([section, part]).astype(jnp.int32)
    micro_count, tokens, width = activations.shape
    swap = [(0, 1), (1, 0)]

    def flat(s, e, d):
        return (s * experts + e) * 2 + d

    def pairs(layer, cross):
        found = []
        for s in range(2):
            target = 1 - s if cross else s
            if layer is None or target == layer:
                found += [
                    (flat(s, e, d), flat(target, e, 1 - d))
                    for e in range(experts)
                    for d in range(2)
                ]
        return found

    def beside(block, route=swap):
        return lax.ppermute(block, "section", route)

    def away(block, layer=None, cross=False):
        return lax.ppermute(block, every, pairs(layer, cross))

    def exchange(block):
        return lax.all_to_all(block, "expert", split_axis=0, concat_axis=0, tiled=True)

    own = (w_gate[0, 0], w_up[0, 0], w_down[0, 0])
    own_gain = norm_gain.reshape(8, 128)
    own_routes = routes[0].transpose(2, 0, 1)
    own_gates = gate_weights[0].transpose(2, 0, 1)
    got_routes = beside(own_routes)
    got_gates = beside(own_gates)
    got_gain = beside(own_gain)
    swapped = tuple(beside(w) for w in own)

    big = ((64, 32, 128), bf16)
    small = ((64, 16, 128), bf16)
    block = ((128, 128), bf16)
    early_shape = ((128, 1280), bf16)
    late_shape = ((128, 2048), bf16)
    down = ((1024, 128), bf16)
    across = ((128, 1024), bf16)
    weight_scratch = [
        pltpu.VMEM((1024, 768), bf16),
        pltpu.VMEM((1024, 768), bf16),
        pltpu.VMEM((768, 1024), bf16),
    ]
    wide = pltpu.VMEM((1024, 128), f32)
    narrow = pltpu.VMEM((128, 128), f32)
    matrix = pltpu.VMEM((128, 1024), bf16)
    sems = pltpu.SemaphoreType.DMA((3, 3))
    early_room = pltpu.VMEM((128, 1280), bf16)
    late_room = pltpu.VMEM((128, 2048), bf16)
    plain_room = pltpu.VMEM((128, 768), f32)
    arrival = pltpu.VMEM((64, 16, 128), bf16)

    out_first, x_first, grad_last, *maps = plain(
        start_body,
        [smem] + [vmem] * 8,
        [big, block, block] + [down] * 6,
        [place, own_routes, got_routes, own_gates, got_gates]
        + [activations, cotangent, own_gain, got_gain],
        [narrow],
    )
    _, high0, low0, pick1, _, _ = maps
    first_gain = jnp.where(section == 0, own_gain, got_gain)
    second_gain = jnp.where(section == 0, got_gain, own_gain)

    def packed(layer, tensors):
        shapes = [((512, 768), bf16), ((384, 512), bf16)][-min(2, len(tensors)) :]
        return call(
            functools.partial(pack_body, layer, tensors),
            [smem] + [anywhere] * (2 * len(tensors)),
            shapes,
            [pltpu.SemaphoreType.DMA((3,))],
            flops=1,
            moved=25 * 10**5,
        )(place, *[own[n] for n in tensors], *[swapped[n] for n in tensors])

    gate_far = away(own[0], 0)
    up_far = away(swapped[1], 1)
    down_far = away(own[2], 0)
    portions0 = (
        gate_far,
        beside(gate_far, [(0, 1)]),
        up_far,
        beside(up_far, [(1, 0)]),
        down_far,
        beside(down_far, [(0, 1)]),
    )
    arrived_first = exchange(out_first)

    flipped = call(flip_body, [vmem] * 6, [across] * 6, flops=10**6, moved=3 * 10**6)(*maps)
    pick0_t, high0_t, low0_t, pick1_t, high1_t, low1_t = flipped

    portions1 = [
        away(after(w, other))
        for w, other in zip(packed(1, (0, 1, 2)), (up_far, down_far))
    ]
    portions1 = [w for far in portions1 for w in (far, beside(far))]

    result, early0, early0_far, pre_gate, pre_up = call(
        first_forward_body,
        [smem] + [hbm] * 13,
        [small, early_shape, early_shape, ((128, 768), f32), ((128, 768), f32)],
        weight_scratch
        + [wide, matrix, early_room, early_room, plain_room, plain_room, arrival, arrival, sems]
        + [pltpu.SemaphoreType.DMA((6,))],
        flops=6 * 10**8,
        moved=6 * 10**6,
        out_spec=hbm,
    )(place, arrived_first, *own, *swapped, *portions0)
    returned = exchange(result)

    hidden_first, out_second = plain(
        between_body,
        [vmem],
        [block, small],
        [returned, x_first, second_gain, high0_t, low0_t, pick1],
    )
    arrived_second = exchange(out_second)

    picked, result_second, gain_second, kept, sent, straight, cross, late1, late1_far = call(
        second_body,
        [smem] + [hbm] * 14,
        [small, small, ((8, 128), f32)] + [early_shape] * 4 + [late_shape] * 2,
        weight_scratch
        + [wide, matrix, matrix, early_room, early_room]
        + [arrival, arrival, early_room, early_room]
        + [late_room, late_room, arrival, arrival]
        + [pltpu.VMEM((8, 128), f32), sems, pltpu.SemaphoreType.DMA((13,))],
        flops=12 * 10**8,
        moved=8 * 10**6,
        out_spec=hbm,
    )(place, arrived_second, arrived_first, early0, early0_far, *own, *swapped, *portions1)
    returned = exchange(picked)

    early_parts = (kept, beside(sent), away(straight), away(cross, cross=True))
    late1_parts = (late1, beside(late1, [(0, 1)]), away(late1_far, 1), away(late1_far, 1, True))

    grad_middle, out_third = plain(
        turn_body,
        [vmem],
        [block, big],
        [returned, result_second, hidden_first, grad_last, second_gain, pick1_t, high0, low0],
    )
    arrived_third = exchange(out_third)

    picked, late0, late0_far = call(
        first_backward_body,
        [smem, vmem] + [hbm] * 16,
        [big, late_shape, late_shape],
        weight_scratch
        + [wide, matrix, arrival, arrival, plain_room, plain_room, late_room, late_room]
        + [pltpu.VMEM((64, 32, 128), bf16), sems, pltpu.SemaphoreType.DMA((7,))],
        flops=6 * 10**8,
        moved=8 * 10**6,
        out_spec=hbm,
    )(
        place,
        gain_second,
        arrived_third,
        arrived_first,
        pre_gate,
        pre_up,
        *own,
        *swapped,
        *portions0,
    )
    late0_parts = (late0, beside(late0, [(1, 0)]), away(late0_far, 0), away(late0_far, 0, True))
    returned = exchange(picked)

    hidden_second, hidden_sent = call(
        second_output_body, [smem] + [vmem] * 4, [block, block], flops=10**8, moved=10**6, grant=16
    )(place, arrived_third, hidden_first, high1_t, low1_t)
    both = ((micro_count, tokens, width), bf16)
    hidden = call(
        hidden_body, [smem] + [vmem] * 3, [both], [narrow], flops=10**5, moved=10**5, grant=16
    )(place, hidden_first, hidden_second, beside(hidden_sent))[0]

    weight_grads = call(
        weight_body,
        [smem] + [anywhere] * 12,
        [((512, 768), f32), ((512, 768), f32), ((768, 512), f32)],
        [
            pltpu.VMEM((512, 1280), bf16),
            pltpu.VMEM((512, 2048), bf16),
            pltpu.VMEM((512, 768), f32),
            pltpu.VMEM((512, 768), f32),
            pltpu.VMEM((768, 512), f32),
            pltpu.SemaphoreType.DMA((2, 4)),
            pltpu.SemaphoreType.DMA((3,)),
        ],
        flops=12 * 10**8,
        moved=8 * 10**6,
        grant=28,
        out_spec=anywhere,
    )(place, *early_parts, *late0_parts, *late1_parts)

    grad_first, grad_sent, gain_rows = call(
        last_body,
        [smem, vmem] + [hbm] * 4,
        [block, ((144, 128), f32), ((16, 128), f32)],
        [
            pltpu.VMEM((128, 128), bf16),
            pltpu.VMEM((128, 128), bf16),
            pltpu.VMEM((8, 128), f32),
            matrix,
            pltpu.SemaphoreType.DMA((4,)),
        ],
        flops=10**8,
        moved=10**6,
        grant=16,
    )(place, returned, x_first, grad_middle, first_gain, pick0_t)
    grads, gain_grad = call(
        final_body,
        [smem] + [vmem] * 7,
        [both, ((8, 128), f32)],
        [narrow],
        flops=10**5,
        moved=10**5,
        grant=16,
    )(
        place,
        grad_first,
        grad_middle,
        beside(grad_sent),
        gain_rows,
        away(gain_rows),
        away(gain_rows, cross=True),
        own_gain,
    )
    return (
        hidden[None],
        grads[None],
        gain_grad.reshape(1, width),
        weight_grads[0][None, None],
        weight_grads[1][None, None],
        weight_grads[2][None, None],
    )


def solution(mesh):
    placed = (
        P(None, ("expert", "dp"), None),
        P(None, ("expert", "dp"), None),
        P("section", None),
        P("section", "expert", "dp", None),
        P("section", "expert", "dp", None),
        P("section", "expert", None, "dp"),
        P("section", None, ("expert", "dp"), None),
        P("section", None, ("expert", "dp"), None),
    )
    return jax.shard_map(
        window,
        mesh=mesh,
        in_specs=placed,
        out_specs=(
            P("section", None, ("expert", "dp"), None),
            P("section", None, ("expert", "dp"), None),
            P("section", None),
            P("section", "expert", "dp", None),
            P("section", "expert", "dp", None),
            P("section", "expert", None, "dp"),
        ),
        check_vma=False,
    )
```
